32 devices in a mesh: obs: 4 (over y, x), par: 8 (over z, core).
Axes of the slice: x: 2, y: 2, z: 4, core: 2. Of those that a mesh axis runs over, the one named last changes fastest.
Arguments:
- jacobian: bfloat16 [2048, 32768], P('obs', 'par'), may hold values from -0.03125 to 0.03125
- probes: bfloat16 [32768, 256], P('par'), may hold values from -6 to 6
- coeffs: bfloat16 [256, 3, 128, 128], P('par'), may hold values from -0.3125 to 0.3125
- offsets: int32 [256, 2], P('par'), may hold values from -4 to 4
Outputs:
- ritz_basis: bfloat16 [32768, 256], P('par')
- basis_image: bfloat16 [32768, 256], P('par')
- ritz_matrix: float32 [256, 256], replicated
The draws below stay inside these ranges and needn't reach their ends.
All inputs are finite; a program needn't handle non-finite values.
Results may differ from the reference program's by a relative error of at most 0.015.
Values may be sent and summed in bfloat16 or wider, within the bound.
A program may use at most 128 MiB of HBM per device.

```python
import jax
import jax.numpy as jnp
from jax import lax

OBS_DEV = 512
K = 256
BLK = 128
REACH = 4
NOBS = 2048
NPAR = 32768
NBLK = 256
N_OBS = 4


def set_ends(values, rng, smallest, high):
    index_at = [jax.random.randint(jax.random.fold_in(rng, axis), (), 0, length) for axis, length in enumerate(values.shape)]
    longest = values.shape.index(max(values.shape))
    beside = index_at[:longest] + [(index_at[longest] + 1) % values.shape[longest]] + index_at[longest + 1:]
    return values.at[tuple(index_at)].set(smallest).at[tuple(beside)].set(high)


def block_levels(rng, shape, shards, smallest, high):
    gain, own = 1.0, jax.random.fold_in(rng, 6)
    for position, blocks in shards:
        steps = jnp.exp(jax.random.uniform(jax.random.fold_in(own, position), (blocks,), jnp.float32, smallest / len(shards), high / len(shards)))
        gain = gain * jnp.repeat(steps, shape[position] // blocks).reshape([-1 if axis == position else 1 for axis in range(len(shape))])
    return gain


def normal_values(key, extent, deviation, bound, split=(), held_as=jnp.bfloat16):
    entries = jax.random.normal(key, extent, jnp.float32) * deviation
    if len(split) > 0:
        entries = block_levels(key, extent, split, -0.22, 0.18) * entries
    return jnp.clip(entries, min=-bound, max=bound).astype(held_as)


def setup_inputs(seed: int = 0) -> dict:
    keys = jax.random.split(jax.random.key(seed), 5)
    jacobian = normal_values(keys[0], (NOBS, NPAR), NPAR ** -0.5, 0.03125, ((0, 4), (1, 8)))
    probes = normal_values(keys[1], (NPAR, K), 1.0, 6.0, ((0, 8),))
    coeffs = normal_values(keys[2], (NBLK, 3, BLK, BLK), (3 * BLK) ** -0.5, 0.3125, ((0, 8),))
    offsets = set_ends(jax.random.randint(keys[3], (NBLK, 2), -REACH, REACH + 1), jax.random.fold_in(keys[3], 1), -REACH, REACH).astype(jnp.int32)
    return dict(jacobian=jacobian, probes=probes, coeffs=coeffs, offsets=offsets)


def block_index(offsets):
    count = offsets.shape[0]
    full_offsets = jnp.concatenate([jnp.zeros((count, 1), jnp.int32), offsets.astype(jnp.int32)], axis=1)
    return (jnp.arange(count, dtype=jnp.int32)[:, None] + REACH + full_offsets).astype(jnp.int32)

def prior_forward(values, coeffs, offsets):
    width = values.shape[1]
    positions = block_index(offsets)
    padded = jnp.pad(values, ((REACH * BLK, REACH * BLK), (0, 0))).reshape(-1, BLK, width)
    picked = padded[positions]
    result = jnp.einsum('bjrc,bjcn->brn', coeffs.astype(jnp.float32), picked.astype(jnp.float32))
    return result.reshape(-1, width).astype(jnp.bfloat16)

def prior_adjoint(values, coeffs, offsets):
    width = values.shape[1]
    count = offsets.shape[0]
    positions = block_index(offsets)
    blocks = values.reshape(count, BLK, width)
    contrib = jnp.einsum('bjcr,bcn->bjrn', coeffs.astype(jnp.float32), blocks.astype(jnp.float32))
    accumulated = jnp.zeros((count + 2 * REACH, BLK, width), jnp.float32).at[positions].add(contrib)
    return accumulated[REACH:REACH + count].reshape(-1, width)

def reference(jacobian, probes, coeffs, offsets):
    sampled = prior_forward(probes, coeffs, offsets)
    forward = jnp.dot(jacobian.astype(jnp.float32), sampled.astype(jnp.float32), preferred_element_type=jnp.float32).astype(jnp.bfloat16)
    adjoint_total = jnp.zeros((NPAR, K), jnp.float32)
    for shard in range(N_OBS):
        jac_rows = jacobian[shard * OBS_DEV:(shard + 1) * OBS_DEV]
        fwd_rows = forward[shard * OBS_DEV:(shard + 1) * OBS_DEV]
        partial_sum = lax.dot_general(jac_rows.astype(jnp.float32), fwd_rows.astype(jnp.float32), (((0,), (0,)), ((), ())), preferred_element_type=jnp.float32)
        rounded = lax.optimization_barrier(partial_sum.astype(jnp.bfloat16))
        adjoint_total = adjoint_total + rounded.astype(jnp.float32)
    adjoint = adjoint_total.astype(jnp.bfloat16)
    range_sample = prior_adjoint(adjoint, coeffs, offsets)
    gram_matrix = jnp.dot(range_sample.T, range_sample, precision=lax.Precision.HIGHEST) / NPAR
    lower_factor = jnp.linalg.cholesky(gram_matrix)
    solved = lax.linalg.triangular_solve(lower_factor, range_sample, left_side=False, lower=True, transpose_a=True)
    ritz_basis = solved.astype(jnp.bfloat16)
    basis_image = prior_forward(ritz_basis, coeffs, offsets)
    projected = jnp.dot(jacobian.astype(jnp.float32), basis_image.astype(jnp.float32), preferred_element_type=jnp.float32)
    ritz_matrix = jnp.dot(projected.T, projected, precision=lax.Precision.HIGHEST) / NOBS
    return (ritz_basis, basis_image, ritz_matrix)
```

```python
import functools

import jax
import jax.numpy as jnp
from jax import lax
from jax.experimental import pallas as pl
from jax.experimental.pallas import tpu as pltpu
from jax.sharding import PartitionSpec as P

BLK = 128
REACH = 4
HALO = REACH * BLK
MESH = pl.DeviceIdType.MESH
F32 = jnp.float32
BF16 = jnp.bfloat16
VMEM = pl.BlockSpec(memory_space=pltpu.VMEM)
SMEM = pl.BlockSpec(memory_space=pltpu.SMEM)
LIMIT = 60 * 1024 * 1024


def greet(devices):
    barrier = pltpu.get_barrier_semaphore()
    for device in devices:
        pl.semaphore_signal(barrier, inc=1, device_id=device, device_id_type=MESH)
    pl.semaphore_wait(barrier, len(devices))


def remote(src, dst, send, recv, device):
    return pltpu.make_async_remote_copy(
        src_ref=src, dst_ref=dst, send_sem=send, recv_sem=recv, device_id=device, device_id_type=MESH
    )


def prior_block(b, base, source, coeffs, offs):
    def pick(offset):
        return source[b - base + offset]

    left = jnp.concatenate([coeffs[b, 0], coeffs[b, 1], coeffs[b, 2]], axis=1)
    right = jnp.concatenate([pick(0), pick(offs[b, 0]), pick(offs[b, 1])], axis=0)
    return jnp.dot(left, right, preferred_element_type=F32).astype(BF16)


def fetch(source, coeffs, jac, values, held, jac_held, low, high, sem):
    blocks = source.shape[0]
    side = 2 * REACH
    loads = [
        pltpu.make_async_copy(source, values, sem.at[0]),
        pltpu.make_async_copy(coeffs, held, sem.at[1]),
        pltpu.make_async_copy(source.at[pl.ds(0, side)], low.at[pl.ds(REACH, side)], sem.at[2]),
        pltpu.make_async_copy(source.at[pl.ds(blocks - side, side)], high.at[pl.ds(0, side)], sem.at[3]),
        pltpu.make_async_copy(jac, jac_held, sem.at[4]),
    ]
    for load in loads:
        load.start()
    return loads


def image_and_parts(
    n_par, o, p, offs, source, loads, values, coeffs, jac, image, low, high, part, got, hs, hr, ps, pr
):
    blocks = values.shape[0]
    side = 2 * REACH
    below = lax.rem(p + n_par - 1, n_par)
    above = lax.rem(p + 1, n_par)
    down = remote(source.at[pl.ds(0, REACH)], high.at[pl.ds(side, REACH)], hs.at[0], hr.at[0], (o, below))
    up = remote(source.at[pl.ds(blocks - REACH, REACH)], low.at[pl.ds(0, REACH)], hs.at[1], hr.at[1], (o, above))

    @pl.when(p > 0)
    def _():
        down.start()

    @pl.when(p < n_par - 1)
    def _():
        up.start()

    @pl.when(p == 0)
    def _():
        low[pl.ds(0, REACH)] = jnp.zeros((REACH,) + low.shape[1:], BF16)

    @pl.when(p == n_par - 1)
    def _():
        high[pl.ds(side, REACH)] = jnp.zeros((REACH,) + high.shape[1:], BF16)

    loads[0].wait()
    loads[1].wait()

    def inner(b, carry):
        image[pl.ds(pl.multiple_of(b * BLK, BLK), BLK), :] = prior_block(b, 0, values, coeffs, offs)
        return carry

    lax.fori_loop(REACH, blocks - REACH, inner, 0, unroll=4)

    @pl.when(p > 0)
    def _():
        down.wait_send()
        up.wait_recv()

    @pl.when(p < n_par - 1)
    def _():
        up.wait_send()
        down.wait_recv()

    loads[2].wait()
    loads[3].wait()
    for b in range(REACH):
        image[pl.ds(b * BLK, BLK), :] = prior_block(b, -REACH, low, coeffs, offs)
    for b in range(blocks - REACH, blocks):
        image[pl.ds(b * BLK, BLK), :] = prior_block(b, blocks - 2 * REACH, high, coeffs, offs)

    loads[4].wait()
    total = jnp.dot(jac[...], image[...], preferred_element_type=F32)
    return sum_over_par(n_par, o, p, total, part, got, ps, pr)


def sum_over_par(n_par, o, p, total, part, got, ps, pr):
    piece = part.shape[1]
    for q in range(n_par):
        part[q] = total[q * piece : (q + 1) * piece].astype(BF16)
    copies = []
    for d in range(1, n_par):
        q = lax.rem(p + d, n_par)
        copy = remote(part.at[q], got.at[d], ps.at[d], pr.at[d], (o, q))
        copy.start()
        copies.append(copy)
    mine = part[p].astype(F32)
    for d in range(1, n_par):
        copies[d - 1].wait()
        mine = mine + got[d].astype(F32)
    return mine


def first_kernel(
    n_obs, n_par, offs, probes, coeffs, jac_ref, out,
    low, high, values, held, jac, ls, image, part, got, fwd, adj, adj_got, hs, hr, ps, pr, gs, gr, os, orr,
):
    o, p = lax.axis_index("obs"), lax.axis_index("par")
    loads = fetch(probes, coeffs, jac_ref, values, held, jac, low, high, ls)
    greet(
        [(o, lax.rem(p + d, n_par)) for d in range(1, n_par)]
        + [(lax.rem(o + d, n_obs), p) for d in range(1, n_obs)]
    )
    mine = image_and_parts(
        n_par, o, p, offs, probes, loads, values, held, jac, image, low, high,
        part, got, hs, hr, ps, pr,
    )
    fwd[p] = mine.astype(BF16)
    copies = []
    for d in range(1, n_par):
        copy = remote(fwd.at[p], fwd.at[p], gs.at[d], gr.at[d], (o, lax.rem(p + d, n_par)))
        copy.start()
        copies.append(copy)
    for copy in copies:
        copy.wait()
    forward = fwd[...].reshape(jac.shape[0], fwd.shape[2])
    sum_over_obs(n_obs, o, p, jac, forward, adj, adj_got, os, orr, out)


def sum_over_obs(n_obs, o, p, jac, forward, adj, got, send, recv, out):
    side, across, far = partners(n_obs, o)
    half = adj.shape[1]
    tile = min(256, half)
    near = (side, p)
    over = (across, p)

    def product(slot, q, h):
        def step(t, carry):
            start = pl.multiple_of((2 * q + h) * half + t * tile, tile)
            value = lax.dot_general(
                jac[:, pl.ds(start, tile)], forward, (((0,), (0,)), ((), ())), preferred_element_type=F32
            )
            adj[slot, pl.ds(pl.multiple_of(t * tile, tile), tile), :] = value.astype(BF16)
            return carry

        lax.fori_loop(0, half // tile, step, 0, unroll=True)

    def send_slot(slot, device):
        copy = remote(adj.at[slot], got.at[slot], send.at[slot], recv.at[slot], device)
        copy.start()
        return copy

    product(0, far, 0)
    copies = [send_slot(0, near)]
    product(1, far, 1)
    copies.append(send_slot(1, over))
    product(2, side, 0)
    copies.append(send_slot(2, near))
    product(3, across, 1)
    copies.append(send_slot(3, over))
    product(4, across, 0)
    product(5, side, 1)
    product(6, o, 0)
    product(7, o, 1)
    copies[0].wait()
    adj[4] = (adj[4].astype(F32) + got[0].astype(F32)).astype(BF16)
    copies.append(send_slot(4, over))
    copies[1].wait()
    adj[5] = (adj[5].astype(F32) + got[1].astype(F32)).astype(BF16)
    copies.append(send_slot(5, near))
    copies[2].wait()
    copies[3].wait()
    copies[4].wait()
    out[pl.ds(0, half), :] = (adj[6].astype(F32) + got[2].astype(F32) + got[4].astype(F32)).astype(BF16)
    copies[5].wait()
    out[pl.ds(half, half), :] = (adj[7].astype(F32) + got[3].astype(F32) + got[5].astype(F32)).astype(BF16)


def adjoint_kernel(offs, values, coeffs, center, lower, upper, acc, held, sem):
    o = lax.axis_index("obs")
    blocks = values.shape[0] // BLK
    width = values.shape[1]
    load = pltpu.make_async_copy(coeffs.at[pl.ds(o * blocks, blocks)], held, sem.at[0])
    load.start()
    acc[...] = jnp.zeros_like(acc)
    load.wait()
    for b in range(blocks):
        v = values[pl.ds(b * BLK, BLK), :]
        for j in range(3):
            offset = 0 if j == 0 else offs[o * blocks + b, j - 1]
            where = pl.ds(pl.multiple_of((b + REACH + offset) * BLK, BLK), BLK)
            acc[where, :] += lax.dot_general(
                held[b, j], v, (((0,), (0,)), ((), ())), preferred_element_type=F32
            )
    lower[...] = acc[pl.ds(0, HALO), :].astype(BF16)
    center[...] = acc[pl.ds(HALO, blocks * BLK), :]
    upper[...] = acc[pl.ds(HALO + blocks * BLK, HALO), :].astype(BF16)


def partners(n_obs, o):
    side = o + 1 - 2 * lax.rem(o, 2)
    half = n_obs // 2
    return side, lax.rem(o + half, n_obs), lax.rem(side + half, n_obs)


def chip_peers(n_obs, n_par, o, p):
    chips = n_par // 2
    z, core = p // 2, lax.rem(p, 2)
    return [
        (lax.rem(o + i, n_obs), 2 * lax.rem(z + j, chips) + core)
        for j in range(chips)
        for i in range(n_obs)
        if i or j
    ]


def sum_everywhere(n_obs, n_par, o, p, value, pair_send, pair_got, send, got, out, sems, beside=()):
    beside = list(beside) + [lambda: None] * 3
    core = lax.rem(p, 2)
    other = (o, p + 1 - 2 * core)
    peers = chip_peers(n_obs, n_par, o, p)
    place = (p // 2) * n_obs + o
    count, piece, width = send.shape
    tall = count * piece
    pair_send[0] = value[:tall]
    pair_send[1] = value[tall:]
    copy = remote(pair_send.at[1 - core], pair_got, sems[0].at[0], sems[1].at[0], other)
    copy.start()
    copy.wait()
    mine = pair_send[core] + pair_got[...]
    for j in range(count):
        send[j] = mine[j * piece : (j + 1) * piece]
    copies = []
    for d, device in enumerate(peers, 1):
        target = (device[1] // 2) * n_obs + device[0]
        copy = remote(send.at[target], got.at[d], sems[2].at[d], sems[3].at[d], device)
        copy.start()
        copies.append(copy)
    beside[0]()
    mine = send[place]
    for d, copy in enumerate(copies, 1):
        copy.wait()
        mine = mine + got[d]
    out[core, place] = mine
    copies = []
    for d, device in enumerate(peers, 1):
        copy = remote(out.at[core, place], out.at[core, place], sems[4].at[d], sems[5].at[d], device)
        copy.start()
        copies.append(copy)
    beside[1]()
    for copy in copies:
        copy.wait()
    copy = remote(out.at[core], out.at[core], sems[6].at[0], sems[7].at[0], other)
    copy.start()
    copy.wait()
    return jnp.concatenate([out[c, j] for c in range(2) for j in range(count)], axis=0)


def sum_scratch(n_obs, n_par, width):
    count = n_obs * n_par // 2
    piece = width // 2 // count
    return [
        pltpu.VMEM((2, width // 2, width), F32),
        pltpu.VMEM((width // 2, width), F32),
        pltpu.VMEM((count, piece, width), F32),
        pltpu.VMEM((count, piece, width), F32),
        pltpu.VMEM((2, count, piece, width), F32),
        dma(1), dma(1), dma(count), dma(count), dma(count), dma(count), dma(1), dma(1),
    ]


def small_inverse_factor(matrix):
    size = matrix.shape[0]
    row = lax.broadcasted_iota(jnp.int32, (size, size), 0)
    lane = lax.broadcasted_iota(jnp.int32, (size, size), 1)
    work = jnp.concatenate([matrix, (row == lane).astype(F32)], axis=1)
    group = 8
    parts = [work[g : g + group] for g in range(0, size, group)]
    index = lax.broadcasted_iota(jnp.int32, (group, 2 * size), 0)
    scales = []
    for first in range(size // group):
        start = first * group
        columns = [
            [jnp.broadcast_to(part[:, start + t : start + t + 1], part.shape) for part in parts[first:]]
            for t in range(group)
        ]
        for t in range(group):
            pivot = columns[t][0][t : t + 1]
            scales.append(lax.rsqrt(pivot))
            reciprocal = 1.0 / pivot
            scaled = parts[first][t : t + 1] * reciprocal
            columns[t][0] = jnp.where(index > t, columns[t][0], 0.0)
            for u in range(t + 1, group):
                ratio = columns[u][0][t : t + 1] * reciprocal
                columns[u] = [c - e * ratio for c, e in zip(columns[u], columns[t])]
            for g, column in enumerate(columns[t]):
                parts[first + g] = parts[first + g] - column * scaled
    rows = [parts[j // group][j % group : j % group + 1] * scales[j] for j in range(size)]
    return jnp.concatenate(rows, axis=0)[:, size:]


def inverse_factor_steps(gram, work, out, size):
    blocks = work.shape[0]
    width = blocks * size
    row = lax.broadcasted_iota(jnp.int32, (size, width), 0)
    lane = lax.broadcasted_iota(jnp.int32, (size, width), 1)
    for k in range(blocks):
        work[k, :, pl.ds(0, width)] = gram[k * size : (k + 1) * size]
        work[k, :, pl.ds(width, width)] = (lane == row + k * size).astype(F32)

    def step(k, carry):
        rows = work[k]
        shift = lax.rem(width - k * size, width)
        diagonal = pltpu.roll(rows[:, :width], shift, 1)[:, :size]
        small = small_inverse_factor(diagonal)
        upper = jnp.dot(small, rows, precision=lax.Precision.HIGHEST, preferred_element_type=F32)
        out[k] = upper[:, width:]
        left = jnp.where(lane >= (k + 1) * size, upper[:, :width], 0.0)
        update = lax.dot_general(
            left, upper, (((0,), (0,)), ((), ())),
            precision=lax.Precision.HIGHEST, preferred_element_type=F32,
        )
        for i in range(blocks):
            work[i] -= update[i * size : (i + 1) * size]
        return carry

    return blocks, step


def gather_over_obs(n_obs, o, p, ext, send, recv):
    side, across, _ = partners(n_obs, o)
    near, over = (side, p), (across, p)
    blocks = (ext.shape[0] - 2 * REACH) // (2 * n_obs)

    def piece(slot, q, h, device):
        ref = ext.at[pl.ds(REACH + (2 * q + h) * blocks, blocks)]
        copy = remote(ref, ref, send.at[slot], recv.at[slot], device)
        copy.start()
        return copy

    copies = [piece(0, o, 0, near), piece(1, o, 1, over), piece(2, o, 1, near), piece(3, o, 0, over)]

    def forward():
        copies[0].wait()
        copies.append(piece(4, side, 0, over))
        copies[1].wait()
        copies.append(piece(5, across, 1, near))

    def finish():
        for copy in copies[2:]:
            copy.wait()

    return forward, finish


def main_kernel(
    n_obs, n_par, offs, center, lower, upper, coeffs, jac, ext, image, inverse, ritz,
    held, jac_held, ls, sample, from_low, from_high, work, part, got,
    hs, hr, rs, rr, as_, ar, ps, pr, *rest,
):
    o, p = lax.axis_index("obs"), lax.axis_index("par")
    loads = [pltpu.make_async_copy(coeffs, held, ls.at[0]), pltpu.make_async_copy(jac, jac_held, ls.at[1])]
    for load in loads:
        load.start()
    sums = len(rest) // 2
    first, second = rest[:sums], rest[sums:]
    count = n_obs * n_par
    order = p * n_obs + o
    rows, width = center.shape
    blocks = rows // BLK
    total_blocks = blocks * n_obs
    before = lax.rem(order + count - 1, count)
    after = lax.rem(order + 1, count)
    below = (lax.rem(before, n_obs), before // n_obs)
    above = (lax.rem(after, n_obs), after // n_obs)
    side, across, _ = partners(n_obs, o)
    along_par = [(o, lax.rem(p + d, n_par)) for d in range(1, n_par)]
    greet(
        [below, above, (side, p), (across, p)] + along_par + chip_peers(n_obs, n_par, o, p)
    )
    down = remote(lower, from_high, hs.at[0], hr.at[0], below)
    up = remote(upper, from_low, hs.at[1], hr.at[1], above)

    @pl.when(order > 0)
    def _():
        down.start()

    @pl.when(order < count - 1)
    def _():
        up.start()

    sample[...] = center[...]

    @pl.when(order > 0)
    def _():
        down.wait_send()
        up.wait_recv()
        sample[pl.ds(0, HALO), :] += from_low[...].astype(F32)

    @pl.when(order < count - 1)
    def _():
        up.wait_send()
        down.wait_recv()
        sample[pl.ds(rows - HALO, HALO), :] += from_high[...].astype(F32)

    ext[pl.ds(REACH + o * blocks, blocks)] = sample[...].astype(BF16).reshape(blocks, BLK, width)
    forward, finish = gather_over_obs(n_obs, o, p, ext, as_, ar)
    value = lax.dot_general(
        sample[...], sample[...], (((0,), (0,)), ((), ())),
        precision=lax.Precision.HIGHEST, preferred_element_type=F32,
    ) / (rows * count)
    matrix = sum_everywhere(n_obs, n_par, o, p, value, *first[:5], first[5:], [forward])
    steps, step = inverse_factor_steps(matrix, work, inverse, inverse.shape[1])
    lax.fori_loop(0, steps // 2, step, 0)
    finish()
    lowest, highest = REACH, REACH + total_blocks
    to_below = remote(
        ext.at[pl.ds(lowest, REACH)], ext.at[pl.ds(highest, REACH)], rs.at[0], rr.at[0],
        (o, lax.rem(p + n_par - 1, n_par)),
    )
    to_above = remote(
        ext.at[pl.ds(highest - REACH, REACH)], ext.at[pl.ds(0, REACH)], rs.at[1], rr.at[1],
        (o, lax.rem(p + 1, n_par)),
    )

    @pl.when(p > 0)
    def _():
        to_below.start()

    @pl.when(p < n_par - 1)
    def _():
        to_above.start()

    @pl.when(p == 0)
    def _():
        ext[pl.ds(0, REACH)] = jnp.zeros((REACH,) + ext.shape[1:], BF16)

    @pl.when(p == n_par - 1)
    def _():
        ext[pl.ds(highest, REACH)] = jnp.zeros((REACH,) + ext.shape[1:], BF16)

    lax.fori_loop(steps // 2, steps, step, 0)

    @pl.when(p > 0)
    def _():
        to_below.wait_send()
        to_above.wait_recv()

    @pl.when(p < n_par - 1)
    def _():
        to_above.wait_send()
        to_below.wait_recv()

    for load in loads:
        load.wait()

    def inner(b, carry):
        image[pl.ds(pl.multiple_of(b * BLK, BLK), BLK), :] = prior_block(b, -REACH, ext, held, offs)
        return carry

    lax.fori_loop(0, total_blocks, inner, 0, unroll=4)
    total = jnp.dot(jac_held[...], image[...], preferred_element_type=F32)
    mine = sum_over_par(n_par, o, p, total, part, got, ps, pr)
    factor = inverse[...].reshape(width, width)
    mine = lax.dot_general(
        mine, factor, (((1,), (1,)), ((), ())), precision=lax.Precision.HIGHEST, preferred_element_type=F32
    )
    value = lax.dot_general(
        mine, mine, (((0,), (0,)), ((), ())),
        precision=lax.Precision.HIGHEST, preferred_element_type=F32,
    ) / (jac_held.shape[0] * n_obs)
    ritz[...] = sum_everywhere(n_obs, n_par, o, p, value, *second[:5], second[5:])


def last_kernel(inverse, sample, mapped, basis, image, high, low):
    @pl.when(pl.program_id(0) == 0)
    def _():
        high[...] = inverse[...].astype(BF16)
        low[...] = (inverse[...] - high[...].astype(F32)).astype(BF16)

    def solve(value):
        last = (((1,), (1,)), ((), ()))
        return (
            lax.dot_general(value, high[...], last, preferred_element_type=F32)
            + lax.dot_general(value, low[...], last, preferred_element_type=F32)
        ).astype(BF16)

    basis[...] = solve(sample[...])
    image[...] = solve(mapped[...])


def dma(count):
    return pltpu.SemaphoreType.DMA((count,))


def params(collective):
    return pltpu.CompilerParams(
        collective_id=collective, has_side_effects=True, vmem_limit_bytes=LIMIT
    )


def body(n_obs, n_par, jacobian, probes, coeffs, offsets):
    obs, rows = jacobian.shape
    width = probes.shape[1]
    own = rows // n_obs
    count = n_obs * n_par
    halos = [pltpu.VMEM((3 * REACH, BLK, width), BF16)] * 2 + [
        pltpu.VMEM((rows // BLK, BLK, width), BF16),
        pltpu.VMEM(coeffs.shape, BF16),
        pltpu.VMEM((obs, rows), BF16),
        dma(5),
    ]
    anywhere = pl.BlockSpec(memory_space=pl.ANY)
    parts = [pltpu.VMEM((n_par, obs // n_par, width), BF16)] * 2
    adjoint = pl.pallas_call(
        functools.partial(first_kernel, n_obs, n_par),
        out_shape=jax.ShapeDtypeStruct((own, width), BF16),
        in_specs=[SMEM, anywhere, anywhere, anywhere],
        out_specs=VMEM,
        scratch_shapes=halos
        + [pltpu.VMEM((rows, width), BF16)]
        + parts
        + [pltpu.VMEM((n_par, obs // n_par, width), BF16)]
        + [pltpu.VMEM((8, own // 2, width), BF16), pltpu.VMEM((6, own // 2, width), BF16)]
        + [dma(2)] * 2
        + [dma(n_par)] * 4
        + [dma(6)] * 2,
        compiler_params=params(0),
        name="first_pass",
    )(offsets, probes.reshape(-1, BLK, width), coeffs, jacobian)
    center, lower, upper = pl.pallas_call(
        adjoint_kernel,
        out_shape=[
            jax.ShapeDtypeStruct((own, width), F32),
            jax.ShapeDtypeStruct((HALO, width), BF16),
            jax.ShapeDtypeStruct((HALO, width), BF16),
        ],
        in_specs=[SMEM, VMEM, pl.BlockSpec(memory_space=pl.ANY)],
        out_specs=[VMEM] * 3,
        scratch_shapes=[
            pltpu.VMEM((own + 2 * HALO, width), F32),
            pltpu.VMEM((own // BLK,) + coeffs.shape[1:], BF16),
            dma(1),
        ],
        compiler_params=pltpu.CompilerParams(vmem_limit_bytes=LIMIT),
        name="adjoint_prior",
    )(offsets, adjoint, coeffs)
    block = 64
    total_blocks = rows // BLK
    ext, mapped, inverse, ritz = pl.pallas_call(
        functools.partial(main_kernel, n_obs, n_par),
        out_shape=[
            jax.ShapeDtypeStruct((total_blocks + 2 * REACH, BLK, width), BF16),
            jax.ShapeDtypeStruct((rows, width), BF16),
            jax.ShapeDtypeStruct((width // block, block, width), F32),
            jax.ShapeDtypeStruct((width, width), F32),
        ],
        in_specs=[SMEM, VMEM, VMEM, VMEM, anywhere, anywhere],
        out_specs=[VMEM] * 4,
        scratch_shapes=[
            pltpu.VMEM(coeffs.shape, BF16),
            pltpu.VMEM((obs, rows), BF16),
            dma(2),
            pltpu.VMEM((own, width), F32),
        ]
        + [pltpu.VMEM((HALO, width), BF16)] * 2
        + [pltpu.VMEM((width // block, block, 2 * width), F32)]
        + parts
        + [dma(2)] * 4
        + [dma(6)] * 2
        + [dma(n_par)] * 2
        + sum_scratch(n_obs, n_par, width) * 2,
        compiler_params=params(1),
        name="main",
    )(offsets, center, lower, upper, coeffs, jacobian)
    tall = HALO
    basis, image = pl.pallas_call(
        last_kernel,
        grid=(rows // tall,),
        out_shape=[jax.ShapeDtypeStruct((rows, width), BF16)] * 2,
        in_specs=[
            pl.BlockSpec((width, width), lambda i: (0, 0)),
            pl.BlockSpec((tall, width), lambda i: (i + 1, 0)),
            pl.BlockSpec((tall, width), lambda i: (i, 0)),
        ],
        out_specs=[pl.BlockSpec((tall, width), lambda i: (i, 0))] * 2,
        scratch_shapes=[pltpu.VMEM((width, width), BF16)] * 2,
        compiler_params=pltpu.CompilerParams(vmem_limit_bytes=LIMIT),
        name="last",
    )(inverse.reshape(width, width), ext.reshape(-1, width), mapped)
    return basis, image, ritz


def solution(mesh):
    return jax.shard_map(
        functools.partial(body, mesh.shape["obs"], mesh.shape["par"]),
        mesh=mesh,
        in_specs=(P("obs", "par"), P("par", None), P("par", None, None, None), P("par", None)),
        out_specs=(P("par", None), P("par", None), P()),
        check_vma=False,
    )
```

```python
import functools

import jax
import jax.numpy as jnp
from jax import lax
from jax.experimental import pallas as pl
from jax.experimental.pallas import tpu as pltpu
from jax.sharding import PartitionSpec as P

BLK = 128
REACH = 4
HALO = REACH * BLK
MESH = pl.DeviceIdType.MESH
F32 = jnp.float32
BF16 = jnp.bfloat16
VMEM = pl.BlockSpec(memory_space=pltpu.VMEM)
SMEM = pl.BlockSpec(memory_space=pltpu.SMEM)
LIMIT = 60 * 1024 * 1024


def greet(devices):
    barrier = pltpu.get_barrier_semaphore()
    for device in devices:
        pl.semaphore_signal(barrier, inc=1, device_id=device, device_id_type=MESH)
    pl.semaphore_wait(barrier, len(devices))


def remote(src, dst, send, recv, device):
    return pltpu.make_async_remote_copy(
        src_ref=src, dst_ref=dst, send_sem=send, recv_sem=recv, device_id=device, device_id_type=MESH
    )


def prior_block(b, base, source, coeffs, offs):
    def pick(offset):
        return source[b - base + offset]

    left = jnp.concatenate([coeffs[b, 0], coeffs[b, 1], coeffs[b, 2]], axis=1)
    right = jnp.concatenate([pick(0), pick(offs[b, 0]), pick(offs[b, 1])], axis=0)
    return jnp.dot(left, right, preferred_element_type=F32).astype(BF16)


def fetch(source, coeffs, jac, values, held, jac_held, low, high, sem):
    blocks = source.shape[0]
    side = 2 * REACH
    loads = [
        pltpu.make_async_copy(source, values, sem.at[0]),
        pltpu.make_async_copy(coeffs, held, sem.at[1]),
        pltpu.make_async_copy(source.at[pl.ds(0, side)], low.at[pl.ds(REACH, side)], sem.at[2]),
        pltpu.make_async_copy(source.at[pl.ds(blocks - side, side)], high.at[pl.ds(0, side)], sem.at[3]),
        pltpu.make_async_copy(jac, jac_held, sem.at[4]),
    ]
    for load in loads:
        load.start()
    return loads


def image_and_parts(
    n_par, o, p, offs, source, loads, values, coeffs, jac, image, low, high, part, got, hs, hr, ps, pr
):
    blocks = values.shape[0]
    side = 2 * REACH
    below = lax.rem(p + n_par - 1, n_par)
    above = lax.rem(p + 1, n_par)
    down = remote(source.at[pl.ds(0, REACH)], high.at[pl.ds(side, REACH)], hs.at[0], hr.at[0], (o, below))
    up = remote(source.at[pl.ds(blocks - REACH, REACH)], low.at[pl.ds(0, REACH)], hs.at[1], hr.at[1], (o, above))

    @pl.when(p > 0)
    def _():
        down.start()

    @pl.when(p < n_par - 1)
    def _():
        up.start()

    @pl.when(p == 0)
    def _():
        low[pl.ds(0, REACH)] = jnp.zeros((REACH,) + low.shape[1:], BF16)

    @pl.when(p == n_par - 1)
    def _():
        high[pl.ds(side, REACH)] = jnp.zeros((REACH,) + high.shape[1:], BF16)

    loads[0].wait()
    loads[1].wait()

    def inner(b, carry):
        image[pl.ds(pl.multiple_of(b * BLK, BLK), BLK), :] = prior_block(b, 0, values, coeffs, offs)
        return carry

    lax.fori_loop(REACH, blocks - REACH, inner, 0, unroll=4)

    @pl.when(p > 0)
    def _():
        down.wait_send()
        up.wait_recv()

    @pl.when(p < n_par - 1)
    def _():
        up.wait_send()
        down.wait_recv()

    loads[2].wait()
    loads[3].wait()
    for b in range(REACH):
        image[pl.ds(b * BLK, BLK), :] = prior_block(b, -REACH, low, coeffs, offs)
    for b in range(blocks - REACH, blocks):
        image[pl.ds(b * BLK, BLK), :] = prior_block(b, blocks - 2 * REACH, high, coeffs, offs)

    loads[4].wait()
    total = jnp.dot(jac[...], image[...], preferred_element_type=F32)
    return sum_over_par(n_par, o, p, total, part, got, ps, pr)


def sum_over_par(n_par, o, p, total, part, got, ps, pr):
    piece = part.shape[1]
    for q in range(n_par):
        part[q] = total[q * piece : (q + 1) * piece].astype(BF16)
    copies = []
    for d in range(1, n_par):
        q = lax.rem(p + d, n_par)
        copy = remote(part.at[q], got.at[d], ps.at[d], pr.at[d], (o, q))
        copy.start()
        copies.append(copy)

    def finish():
        mine = part[p].astype(F32)
        for d in range(1, n_par):
            copies[d - 1].wait()
            mine = mine + got[d].astype(F32)
        return mine

    return finish


def first_kernel(
    n_obs, n_par, offs, probes, coeffs, jac_ref, out,
    low, high, values, held, jac, ls, image, part, got, fwd, adj, adj_got, hs, hr, ps, pr, gs, gr, os, orr,
):
    o, p = lax.axis_index("obs"), lax.axis_index("par")
    loads = fetch(probes, coeffs, jac_ref, values, held, jac, low, high, ls)
    greet(
        [(o, lax.rem(p + d, n_par)) for d in range(1, n_par)]
        + [(lax.rem(o + d, n_obs), p) for d in range(1, n_obs)]
    )
    mine = image_and_parts(
        n_par, o, p, offs, probes, loads, values, held, jac, image, low, high,
        part, got, hs, hr, ps, pr,
    )()
    fwd[p] = mine.astype(BF16)
    copies = []
    for d in range(1, n_par):
        copy = remote(fwd.at[p], fwd.at[p], gs.at[d], gr.at[d], (o, lax.rem(p + d, n_par)))
        copy.start()
        copies.append(copy)
    for copy in copies:
        copy.wait()
    forward = fwd[...].reshape(jac.shape[0], fwd.shape[2])
    sum_over_obs(n_obs, o, p, jac, forward, adj, adj_got, os, orr, out)


def sum_over_obs(n_obs, o, p, jac, forward, adj, got, send, recv, out):
    side, across, far = partners(n_obs, o)
    half = adj.shape[1]
    tile = min(256, half)
    near = (side, p)
    over = (across, p)

    def product(slot, q, h):
        def step(t, carry):
            start = pl.multiple_of((2 * q + h) * half + t * tile, tile)
            value = lax.dot_general(
                jac[:, pl.ds(start, tile)], forward, (((0,), (0,)), ((), ())), preferred_element_type=F32
            )
            adj[slot, pl.ds(pl.multiple_of(t * tile, tile), tile), :] = value.astype(BF16)
            return carry

        lax.fori_loop(0, half // tile, step, 0, unroll=True)

    def send_slot(slot, device):
        copy = remote(adj.at[slot], got.at[slot], send.at[slot], recv.at[slot], device)
        copy.start()
        return copy

    product(0, far, 0)
    copies = [send_slot(0, near)]
    product(1, far, 1)
    copies.append(send_slot(1, over))
    product(2, side, 0)
    copies.append(send_slot(2, near))
    product(3, across, 1)
    copies.append(send_slot(3, over))
    product(4, across, 0)
    product(5, side, 1)
    product(6, o, 0)
    product(7, o, 1)
    copies[0].wait()
    adj[4] = (adj[4].astype(F32) + got[0].astype(F32)).astype(BF16)
    copies.append(send_slot(4, over))
    copies[1].wait()
    adj[5] = (adj[5].astype(F32) + got[1].astype(F32)).astype(BF16)
    copies.append(send_slot(5, near))
    copies[2].wait()
    copies[3].wait()
    copies[4].wait()
    out[pl.ds(0, half), :] = (adj[6].astype(F32) + got[2].astype(F32) + got[4].astype(F32)).astype(BF16)
    copies[5].wait()
    out[pl.ds(half, half), :] = (adj[7].astype(F32) + got[3].astype(F32) + got[5].astype(F32)).astype(BF16)


def adjoint_kernel(offs, values, coeffs, center, lower, upper, acc, held, sem):
    o = lax.axis_index("obs")
    blocks = values.shape[0] // BLK
    width = values.shape[1]
    load = pltpu.make_async_copy(coeffs.at[pl.ds(o * blocks, blocks)], held, sem.at[0])
    load.start()
    acc[...] = jnp.zeros_like(acc)
    load.wait()
    for b in range(blocks):
        v = values[pl.ds(b * BLK, BLK), :]
        for j in range(3):
            offset = 0 if j == 0 else offs[o * blocks + b, j - 1]
            where = pl.ds(pl.multiple_of((b + REACH + offset) * BLK, BLK), BLK)
            acc[where, :] += lax.dot_general(
                held[b, j], v, (((0,), (0,)), ((), ())), preferred_element_type=F32
            )
    lower[...] = acc[pl.ds(0, HALO), :].astype(BF16)
    center[...] = acc[pl.ds(HALO, blocks * BLK), :]
    upper[...] = acc[pl.ds(HALO + blocks * BLK, HALO), :].astype(BF16)


def partners(n_obs, o):
    side = o + 1 - 2 * lax.rem(o, 2)
    half = n_obs // 2
    return side, lax.rem(o + half, n_obs), lax.rem(side + half, n_obs)


def chip_peers(n_obs, n_par, o, p):
    chips = n_par // 2
    z, core = p // 2, lax.rem(p, 2)
    return [
        (lax.rem(o + i, n_obs), 2 * lax.rem(z + j, chips) + core)
        for j in range(chips)
        for i in range(n_obs)
        if i or j
    ]


def all_peers(n_obs, n_par, o, p):
    return [
        (lax.rem(o + i, n_obs), lax.rem(p + j, n_par))
        for j in range(n_par)
        for i in range(n_obs)
        if i or j
    ]


def sum_everywhere(n_obs, n_par, o, p, value, send, got, out, sems, beside=()):
    beside = list(beside) + [lambda: None] * 2
    peers = all_peers(n_obs, n_par, o, p)
    place = p * n_obs + o
    count, piece, width = send.shape
    kind = send.dtype
    for j in range(count):
        send[j] = value[j * piece : (j + 1) * piece].astype(kind)
    copies = []
    for d, (i, q) in enumerate(peers, 1):
        copy = remote(send.at[q * n_obs + i], got.at[d], sems[0].at[d], sems[1].at[d], (i, q))
        copy.start()
        copies.append(copy)
    beside[0]()
    mine = send[place].astype(F32)
    for d, copy in enumerate(copies, 1):
        copy.wait()
        mine = mine + got[d].astype(F32)
    out[place] = mine.astype(kind)
    copies = []
    for d, device in enumerate(peers, 1):
        copy = remote(out.at[place], out.at[place], sems[2].at[d], sems[3].at[d], device)
        copy.start()
        copies.append(copy)
    beside[1]()
    for copy in copies:
        copy.wait()
    return jnp.concatenate([out[j].astype(F32) for j in range(count)], axis=0)


def sum_scratch(n_obs, n_par, width, kind):
    count = n_obs * n_par
    return [pltpu.VMEM((count, width // count, width), kind)] * 3 + [dma(count)] * 4


def small_inverse_factor(matrix):
    size = matrix.shape[0]
    row = lax.broadcasted_iota(jnp.int32, (size, size), 0)
    lane = lax.broadcasted_iota(jnp.int32, (size, size), 1)
    work = jnp.concatenate([matrix, (row == lane).astype(F32)], axis=1)
    group = 8
    parts = [work[g : g + group] for g in range(0, size, group)]
    index = lax.broadcasted_iota(jnp.int32, (group, 2 * size), 0)
    scales = []
    for first in range(size // group):
        start = first * group
        columns = [
            [jnp.broadcast_to(part[:, start + t : start + t + 1], part.shape) for part in parts[first:]]
            for t in range(group)
        ]
        for t in range(group):
            pivot = columns[t][0][t : t + 1]
            scales.append(lax.rsqrt(pivot))
            reciprocal = 1.0 / pivot
            scaled = parts[first][t : t + 1] * reciprocal
            columns[t][0] = jnp.where(index > t, columns[t][0], 0.0)
            for u in range(t + 1, group):
                ratio = columns[u][0][t : t + 1] * reciprocal
                columns[u] = [c - e * ratio for c, e in zip(columns[u], columns[t])]
            for g, column in enumerate(columns[t]):
                parts[first + g] = parts[first + g] - column * scaled
    rows = [parts[j // group][j % group : j % group + 1] * scales[j] for j in range(size)]
    return jnp.concatenate(rows, axis=0)[:, size:]


def inverse_factor_steps(gram, work, out, size):
    blocks = work.shape[0]
    width = blocks * size
    row = lax.broadcasted_iota(jnp.int32, (size, width), 0)
    lane = lax.broadcasted_iota(jnp.int32, (size, width), 1)
    for k in range(blocks):
        work[k, :, pl.ds(0, width)] = gram[k * size : (k + 1) * size]
        work[k, :, pl.ds(width, width)] = (lane == row + k * size).astype(F32)

    def step(k, carry):
        rows = work[k]
        shift = lax.rem(width - k * size, width)
        diagonal = pltpu.roll(rows[:, :width], shift, 1)[:, :size]
        small = small_inverse_factor(diagonal)
        upper = jnp.dot(small, rows, precision=lax.Precision.HIGHEST, preferred_element_type=F32)
        out[k] = upper[:, width:]
        left = jnp.where(lane >= (k + 1) * size, upper[:, :width], 0.0)
        update = lax.dot_general(
            left, upper, (((0,), (0,)), ((), ())),
            precision=lax.Precision.HIGHEST, preferred_element_type=F32,
        )
        for i in range(blocks):
            work[i] -= update[i * size : (i + 1) * size]
        return carry

    return blocks, step


def gather_over_obs(n_obs, o, p, ext, send, recv):
    side, across, _ = partners(n_obs, o)
    near, over = (side, p), (across, p)
    blocks = (ext.shape[0] - 2 * REACH) // (4 * n_obs)
    order = [
        [(o, 0, near), (o, 2, over)],
        [(o, 1, near), (o, 3, over)],
        [(o, 2, near), (o, 0, over)],
        [(o, 3, near), (o, 1, over)],
        [(side, 0, over), (across, 2, near)],
        [(side, 1, over), (across, 3, near)],
    ]
    copies = []

    def stage(i):
        for j, (q, h, device) in enumerate(order[i]):
            if i >= 4:
                copies[2 * (i - 4) + j].wait()
            ref = ext.at[pl.ds(REACH + (4 * q + h) * blocks, blocks)]
            slot = 2 * i + j
            copy = remote(ref, ref, send.at[slot], recv.at[slot], device)
            copy.start()
            copies.append(copy)

    def finish():
        for copy in copies[4:]:
            copy.wait()

    return stage, finish


def main_kernel(
    n_obs, n_par, offs, center, lower, upper, coeffs, jac, ext_out, image_out, inverse, ritz,
    held, jac_held, ls, ext, image, ws, sample, from_low, from_high, work, part, got,
    hs, hr, rs, rr, as_, ar, ps, pr, *rest,
):
    o, p = lax.axis_index("obs"), lax.axis_index("par")
    loads = [pltpu.make_async_copy(coeffs, held, ls.at[0]), pltpu.make_async_copy(jac, jac_held, ls.at[1])]
    for load in loads:
        load.start()
    sums = len(rest) // 2
    first, second = rest[:sums], rest[sums:]
    count = n_obs * n_par
    order = p * n_obs + o
    rows, width = center.shape
    blocks = rows // BLK
    total_blocks = blocks * n_obs
    before = lax.rem(order + count - 1, count)
    after = lax.rem(order + 1, count)
    below = (lax.rem(before, n_obs), before // n_obs)
    above = (lax.rem(after, n_obs), after // n_obs)
    greet(all_peers(n_obs, n_par, o, p))
    down = remote(lower, from_high, hs.at[0], hr.at[0], below)
    up = remote(upper, from_low, hs.at[1], hr.at[1], above)

    @pl.when(order > 0)
    def _():
        down.start()

    @pl.when(order < count - 1)
    def _():
        up.start()

    sample[...] = center[...]

    @pl.when(order > 0)
    def _():
        down.wait_send()
        up.wait_recv()
        sample[pl.ds(0, HALO), :] += from_low[...].astype(F32)

    @pl.when(order < count - 1)
    def _():
        up.wait_send()
        down.wait_recv()
        sample[pl.ds(rows - HALO, HALO), :] += from_high[...].astype(F32)

    ext[pl.ds(REACH + o * blocks, blocks)] = sample[...].astype(BF16).reshape(blocks, BLK, width)
    stage, finish = gather_over_obs(n_obs, o, p, ext, as_, ar)
    stage(0)
    value = lax.dot_general(
        sample[...], sample[...], (((0,), (0,)), ((), ())),
        precision=lax.Precision.HIGHEST, preferred_element_type=F32,
    ) / (rows * count)
    def gather_more(*which):
        return lambda: [stage(i) for i in which]

    matrix = sum_everywhere(
        n_obs, n_par, o, p, value, *first[:3], first[3:], [gather_more(1, 2), gather_more(3, 4)]
    )
    stage(5)
    steps, step = inverse_factor_steps(matrix, work, inverse, inverse.shape[1])
    lax.fori_loop(0, 1, step, 0)
    finish()
    lowest, highest = REACH, REACH + total_blocks
    to_below = remote(
        ext.at[pl.ds(lowest, REACH)], ext.at[pl.ds(highest, REACH)], rs.at[0], rr.at[0],
        (o, lax.rem(p + n_par - 1, n_par)),
    )
    to_above = remote(
        ext.at[pl.ds(highest - REACH, REACH)], ext.at[pl.ds(0, REACH)], rs.at[1], rr.at[1],
        (o, lax.rem(p + 1, n_par)),
    )

    @pl.when(p > 0)
    def _():
        to_below.start()

    @pl.when(p < n_par - 1)
    def _():
        to_above.start()

    @pl.when(p == 0)
    def _():
        ext[pl.ds(0, REACH)] = jnp.zeros((REACH,) + ext.shape[1:], BF16)

    @pl.when(p == n_par - 1)
    def _():
        ext[pl.ds(highest, REACH)] = jnp.zeros((REACH,) + ext.shape[1:], BF16)

    lax.fori_loop(1, steps - 1, step, 0)

    @pl.when(p > 0)
    def _():
        to_below.wait_send()
        to_above.wait_recv()

    @pl.when(p < n_par - 1)
    def _():
        to_above.wait_send()
        to_below.wait_recv()

    for load in loads:
        load.wait()

    writes = [pltpu.make_async_copy(ext.at[pl.ds(REACH, total_blocks)], ext_out, ws.at[0])]
    writes[0].start()
    def inner(b, carry):
        image[pl.ds(pl.multiple_of(b * BLK, BLK), BLK), :] = prior_block(b, -REACH, ext, held, offs)
        return carry

    lax.fori_loop(0, total_blocks, inner, 0, unroll=4)
    writes.append(pltpu.make_async_copy(image, image_out, ws.at[1]))
    writes[1].start()
    total = jnp.dot(jac_held[...], image[...], preferred_element_type=F32)
    finish_sum = sum_over_par(n_par, o, p, total, part, got, ps, pr)
    lax.fori_loop(steps - 1, steps, step, 0)
    mine = finish_sum()
    factor = inverse[...].reshape(width, width)
    mine = lax.dot_general(
        mine, factor, (((1,), (1,)), ((), ())), precision=lax.Precision.HIGHEST, preferred_element_type=F32
    )
    value = lax.dot_general(
        mine, mine, (((0,), (0,)), ((), ())),
        precision=lax.Precision.HIGHEST, preferred_element_type=F32,
    ) / (jac_held.shape[0] * n_obs)
    ritz[...] = sum_everywhere(n_obs, n_par, o, p, value, *second[:3], second[3:])
    for write in writes:
        write.wait()


def last_kernel(inverse, sample, mapped, basis, image, high, low):
    @pl.when(pl.program_id(0) == 0)
    def _():
        high[...] = inverse[...].astype(BF16)
        low[...] = (inverse[...] - high[...].astype(F32)).astype(BF16)

    def solve(value):
        last = (((1,), (1,)), ((), ()))
        return (
            lax.dot_general(value, high[...], last, preferred_element_type=F32)
            + lax.dot_general(value, low[...], last, preferred_element_type=F32)
        ).astype(BF16)

    basis[...] = solve(sample[...])
    image[...] = solve(mapped[...])


def dma(count):
    return pltpu.SemaphoreType.DMA((count,))


def params(collective, limit=LIMIT):
    return pltpu.CompilerParams(
        collective_id=collective, has_side_effects=True, vmem_limit_bytes=limit
    )


def body(n_obs, n_par, jacobian, probes, coeffs, offsets):
    obs, rows = jacobian.shape
    width = probes.shape[1]
    own = rows // n_obs
    count = n_obs * n_par
    halos = [pltpu.VMEM((3 * REACH, BLK, width), BF16)] * 2 + [
        pltpu.VMEM((rows // BLK, BLK, width), BF16),
        pltpu.VMEM(coeffs.shape, BF16),
        pltpu.VMEM((obs, rows), BF16),
        dma(5),
    ]
    anywhere = pl.BlockSpec(memory_space=pl.ANY)
    parts = [pltpu.VMEM((n_par, obs // n_par, width), BF16)] * 2
    adjoint = pl.pallas_call(
        functools.partial(first_kernel, n_obs, n_par),
        out_shape=jax.ShapeDtypeStruct((own, width), BF16),
        in_specs=[SMEM, anywhere, anywhere, anywhere],
        out_specs=VMEM,
        scratch_shapes=halos
        + [pltpu.VMEM((rows, width), BF16)]
        + parts
        + [pltpu.VMEM((n_par, obs // n_par, width), BF16)]
        + [pltpu.VMEM((8, own // 2, width), BF16), pltpu.VMEM((6, own // 2, width), BF16)]
        + [dma(2)] * 2
        + [dma(n_par)] * 4
        + [dma(6)] * 2,
        compiler_params=params(0),
        name="first_pass",
    )(offsets, probes.reshape(-1, BLK, width), coeffs, jacobian)
    center, lower, upper = pl.pallas_call(
        adjoint_kernel,
        out_shape=[
            jax.ShapeDtypeStruct((own, width), F32),
            jax.ShapeDtypeStruct((HALO, width), BF16),
            jax.ShapeDtypeStruct((HALO, width), BF16),
        ],
        in_specs=[SMEM, VMEM, pl.BlockSpec(memory_space=pl.ANY)],
        out_specs=[VMEM] * 3,
        scratch_shapes=[
            pltpu.VMEM((own + 2 * HALO, width), F32),
            pltpu.VMEM((own // BLK,) + coeffs.shape[1:], BF16),
            dma(1),
        ],
        compiler_params=pltpu.CompilerParams(vmem_limit_bytes=LIMIT),
        name="adjoint_prior",
    )(offsets, adjoint, coeffs)
    block = 64
    total_blocks = rows // BLK
    ext, mapped, inverse, ritz = pl.pallas_call(
        functools.partial(main_kernel, n_obs, n_par),
        out_shape=[
            jax.ShapeDtypeStruct((total_blocks, BLK, width), BF16),
            jax.ShapeDtypeStruct((rows, width), BF16),
            jax.ShapeDtypeStruct((width // block, block, width), F32),
            jax.ShapeDtypeStruct((width, width), F32),
        ],
        in_specs=[SMEM, VMEM, VMEM, VMEM, anywhere, anywhere],
        out_specs=[anywhere, anywhere, VMEM, VMEM],
        scratch_shapes=[
            pltpu.VMEM(coeffs.shape, BF16),
            pltpu.VMEM((obs, rows), BF16),
            dma(2),
            pltpu.VMEM((total_blocks + 2 * REACH, BLK, width), BF16),
            pltpu.VMEM((rows, width), BF16),
            dma(2),
            pltpu.VMEM((own, width), F32),
        ]
        + [pltpu.VMEM((HALO, width), BF16)] * 2
        + [pltpu.VMEM((width // block, block, 2 * width), F32)]
        + parts
        + [dma(2)] * 4
        + [dma(12)] * 2
        + [dma(n_par)] * 2
        + sum_scratch(n_obs, n_par, width, F32)
        + sum_scratch(n_obs, n_par, width, BF16),
        compiler_params=params(1, 28 * 1024 * 1024),
        name="main",
    )(offsets, center, lower, upper, coeffs, jacobian)
    tall = rows // 4
    basis, image = pl.pallas_call(
        last_kernel,
        grid=(rows // tall,),
        out_shape=[jax.ShapeDtypeStruct((rows, width), BF16)] * 2,
        in_specs=[
            pl.BlockSpec((width, width), lambda i: (0, 0)),
            pl.BlockSpec((tall, width), lambda i: (i, 0)),
            pl.BlockSpec((tall, width), lambda i: (i, 0)),
        ],
        out_specs=[pl.BlockSpec((tall, width), lambda i: (i, 0))] * 2,
        scratch_shapes=[pltpu.VMEM((width, width), BF16)] * 2,
        compiler_params=pltpu.CompilerParams(vmem_limit_bytes=16 * 1024 * 1024),
        name="last",
    )(inverse.reshape(width, width), ext.reshape(-1, width), mapped)
    return basis, image, ritz


def solution(mesh):
    return jax.shard_map(
        functools.partial(body, mesh.shape["obs"], mesh.shape["par"]),
        mesh=mesh,
        in_specs=(P("obs", "par"), P("par", None), P("par", None, None, None), P("par", None)),
        out_specs=(P("par", None), P("par", None), P()),
        check_vma=False,
    )
```

```python
import functools

import jax
import jax.numpy as jnp
from jax import lax
from jax.experimental import pallas as pl
from jax.experimental.pallas import tpu as pltpu
from jax.sharding import PartitionSpec as P

BLK = 128
REACH = 4
HALO = REACH * BLK
MESH = pl.DeviceIdType.MESH
F32 = jnp.float32
BF16 = jnp.bfloat16
VMEM = pl.BlockSpec(memory_space=pltpu.VMEM)
SMEM = pl.BlockSpec(memory_space=pltpu.SMEM)
LIMIT = 60 * 1024 * 1024


def greet(devices):
    barrier = pltpu.get_barrier_semaphore()
    for device in devices:
        pl.semaphore_signal(barrier, inc=1, device_id=device, device_id_type=MESH)
    pl.semaphore_wait(barrier, len(devices))


def remote(src, dst, send, recv, device):
    return pltpu.make_async_remote_copy(
        src_ref=src, dst_ref=dst, send_sem=send, recv_sem=recv, device_id=device, device_id_type=MESH
    )


def prior_block(b, base, source, coeffs, offs):
    def pick(offset):
        return source[b - base + offset]

    left = jnp.concatenate([coeffs[b, 0], coeffs[b, 1], coeffs[b, 2]], axis=1)
    right = jnp.concatenate([pick(0), pick(offs[b, 0]), pick(offs[b, 1])], axis=0)
    return jnp.dot(left, right, preferred_element_type=F32).astype(BF16)


def all_peers(n_obs, n_par, o, p):
    return [
        (lax.rem(o + i, n_obs), lax.rem(p + j, n_par))
        for j in range(n_par)
        for i in range(n_obs)
        if i or j
    ]


def chip_peers(n_obs, n_par, o, p):
    chips = n_par // 2
    z, core = p // 2, lax.rem(p, 2)
    return [
        (lax.rem(o + i, n_obs), 2 * lax.rem(z + j, chips) + core)
        for j in range(chips)
        for i in range(n_obs)
        if i or j
    ]


def partners(n_obs, o):
    side = o + 1 - 2 * lax.rem(o, 2)
    half = n_obs // 2
    return side, lax.rem(o + half, n_obs), lax.rem(side + half, n_obs)


def quarter(n_obs, o, p):
    y = o // 2
    place = 2 * y + lax.rem(o + y, 2)
    return place + lax.rem(p, 2) * (n_obs - 1 - 2 * place)


def owner(n_obs, q, p):
    place = q + lax.rem(p, 2) * (n_obs - 1 - 2 * q)
    y = place // 2
    return 2 * y + lax.rem(place + y, 2)


def wait_all(ref, sem):
    pltpu.make_async_copy(ref, ref, sem).wait()


def sum_over_par(n_par, o, p, total, part, got, send, recv):
    piece = part.shape[1]
    for q in range(n_par):
        part[q] = total[q * piece : (q + 1) * piece].astype(BF16)
    copies = []
    for d in range(1, n_par):
        q = lax.rem(p + d, n_par)
        copy = remote(part.at[q], got.at[d], send.at[d], recv.at[d], (o, q))
        copy.start()
        copies.append(copy)

    def finish():
        mine = part[p].astype(F32)
        for d in range(1, n_par):
            copies[d - 1].wait()
            mine = mine + got[d].astype(F32)
        return mine

    return finish


def sum_over_obs(n_obs, o, p, jac, forward, adj, got, send, recv, out, beside):
    side, across, far = partners(n_obs, o)
    half = adj.shape[1]
    tile = min(256, half)
    near = (side, p)
    over = (across, p)

    def product(slot, device, h):
        q = quarter(n_obs, device, p)

        def step(t, carry):
            start = pl.multiple_of((2 * q + h) * half + t * tile, tile)
            value = lax.dot_general(
                jac[:, pl.ds(start, tile)], forward, (((0,), (0,)), ((), ())), preferred_element_type=F32
            )
            adj[slot, pl.ds(pl.multiple_of(t * tile, tile), tile), :] = value.astype(BF16)
            return carry

        lax.fori_loop(0, half // tile, step, 0, unroll=True)

    def send_slot(slot, device):
        copy = remote(adj.at[slot], got.at[slot], send.at[slot], recv.at[slot], device)
        copy.start()
        return copy

    product(0, far, 0)
    copies = [send_slot(0, near)]
    product(1, far, 1)
    copies.append(send_slot(1, over))
    product(2, side, 0)
    copies.append(send_slot(2, near))
    product(3, across, 1)
    copies.append(send_slot(3, over))
    product(4, across, 0)
    product(5, side, 1)
    product(6, o, 0)
    product(7, o, 1)
    copies[0].wait()
    adj[4] = (adj[4].astype(F32) + got[0].astype(F32)).astype(BF16)
    copies.append(send_slot(4, over))
    copies[1].wait()
    adj[5] = (adj[5].astype(F32) + got[1].astype(F32)).astype(BF16)
    copies.append(send_slot(5, near))
    beside()
    copies[2].wait()
    copies[3].wait()
    copies[4].wait()
    out[pl.ds(0, half), :] = (adj[6].astype(F32) + got[2].astype(F32) + got[4].astype(F32)).astype(BF16)
    copies[5].wait()
    out[pl.ds(half, half), :] = (adj[7].astype(F32) + got[3].astype(F32) + got[5].astype(F32)).astype(BF16)


def prepare_bands(offs, coeffs, first, middle, low, high, diagonal):
    blocks = diagonal.shape[0]
    zero = jnp.zeros((BLK, BLK), BF16)
    low[...] = jnp.zeros_like(low)
    high[...] = jnp.zeros_like(high)
    for b in range(blocks):
        diagonal[b] = coeffs[first + b, 0].T
        columns = pl.ds(b * BLK, BLK)
        for j in range(2):
            block = coeffs[first + b, j + 1].T
            offset = offs[first + b, j]
            for c in range(blocks):
                if abs(c - b) > REACH:
                    middle[j, pl.ds(c * BLK, BLK), columns] = zero
            for d in range(-REACH, REACH + 1):
                value = jnp.where(offset == d, block, zero)
                c = b + d
                if c < 0:
                    low[j, pl.ds((c + REACH) * BLK, BLK), columns] = value
                elif c >= blocks:
                    columns_high = pl.ds((b - blocks + REACH) * BLK, BLK)
                    high[j, pl.ds((c - blocks) * BLK, BLK), columns_high] = value
                else:
                    middle[j, pl.ds(c * BLK, BLK), columns] = value


def two_products(bands, values):
    return jnp.dot(bands[0], values, preferred_element_type=F32) + jnp.dot(
        bands[1], values, preferred_element_type=F32
    )


def sum_everywhere(n_obs, n_par, o, p, value, pair_send, pair_got, send, got, out, sems, beside=()):
    beside = list(beside) + [lambda: None] * 2
    core = lax.rem(p, 2)
    other = (o, p + 1 - 2 * core)
    peers = chip_peers(n_obs, n_par, o, p)
    place = (p // 2) * n_obs + o
    count, piece, width = send.shape
    kind = send.dtype
    tall = count * piece
    pair_send[0] = value[:tall].astype(kind)
    pair_send[1] = value[tall:].astype(kind)
    copy = remote(pair_send.at[1 - core], pair_got, sems.at[0], sems.at[1], other)
    copy.start()
    copy.wait()
    mine = pair_send[core].astype(F32) + pair_got[...].astype(F32)
    for j in range(count):
        send[j] = mine[j * piece : (j + 1) * piece].astype(kind)
    for d, device in enumerate(peers, 1):
        target = (device[1] // 2) * n_obs + device[0]
        remote(send.at[target], got.at[d], sems.at[2], sems.at[3], device).start()
    beside[0]()
    mine = send[place].astype(F32)
    rest = got.at[pl.ds(1, count - 1)]
    wait_all(rest, sems.at[2])
    wait_all(rest, sems.at[3])
    for d in range(1, count):
        mine = mine + got[d].astype(F32)
    out[core, place] = mine.astype(kind)
    for device in peers:
        remote(out.at[core, place], out.at[core, place], sems.at[4], sems.at[5], device).start()
    beside[1]()
    wait_all(rest, sems.at[4])
    wait_all(rest, sems.at[5])
    copy = remote(out.at[core], out.at[core], sems.at[6], sems.at[7], other)
    copy.start()
    copy.wait()
    return jnp.concatenate([out[c, j].astype(F32) for c in range(2) for j in range(count)], axis=0)


def sum_scratch(n_obs, n_par, width, kind):
    count = n_obs * n_par // 2
    piece = width // 2 // count
    return [
        pltpu.VMEM((2, width // 2, width), kind),
        pltpu.VMEM((width // 2, width), kind),
        pltpu.VMEM((count, piece, width), kind),
        pltpu.VMEM((count, piece, width), kind),
        pltpu.VMEM((2, count, piece, width), kind),
        dma(8),
    ]


def small_inverse_factor(matrix):
    size = matrix.shape[0]
    row = lax.broadcasted_iota(jnp.int32, (size, size), 0)
    lane = lax.broadcasted_iota(jnp.int32, (size, size), 1)
    work = jnp.concatenate([matrix, (row == lane).astype(F32)], axis=1)
    group = 8
    parts = [work[g : g + group] for g in range(0, size, group)]
    index = lax.broadcasted_iota(jnp.int32, (group, 2 * size), 0)
    scales = []
    for first in range(size // group):
        start = first * group
        columns = [
            [jnp.broadcast_to(part[:, start + t : start + t + 1], part.shape) for part in parts[first:]]
            for t in range(group)
        ]
        for t in range(group):
            pivot = columns[t][0][t : t + 1]
            scales.append(lax.rsqrt(pivot))
            reciprocal = 1.0 / pivot
            scaled = parts[first][t : t + 1] * reciprocal
            columns[t][0] = jnp.where(index > t, columns[t][0], 0.0)
            for u in range(t + 1, group):
                ratio = columns[u][0][t : t + 1] * reciprocal
                columns[u] = [c - e * ratio for c, e in zip(columns[u], columns[t])]
            for g, column in enumerate(columns[t]):
                parts[first + g] = parts[first + g] - column * scaled
    rows = [parts[j // group][j % group : j % group + 1] * scales[j] for j in range(size)]
    return jnp.concatenate(rows, axis=0)[:, size:]


def inverse_factor_steps(gram, work, out, size):
    blocks = work.shape[0]
    width = blocks * size
    row = lax.broadcasted_iota(jnp.int32, (size, width), 0)
    lane = lax.broadcasted_iota(jnp.int32, (size, width), 1)
    for k in range(blocks):
        work[k, :, pl.ds(0, width)] = gram[k * size : (k + 1) * size]
        work[k, :, pl.ds(width, width)] = (lane == row + k * size).astype(F32)

    def step(k, carry):
        rows = work[k]
        shift = lax.rem(width - k * size, width)
        diagonal = pltpu.roll(rows[:, :width], shift, 1)[:, :size]
        small = small_inverse_factor(diagonal)
        upper = jnp.dot(small, rows, precision=lax.Precision.HIGHEST, preferred_element_type=F32)
        out[k] = upper[:, width:]
        left = jnp.where(lane >= (k + 1) * size, upper[:, :width], 0.0)
        update = lax.dot_general(
            left, upper, (((0,), (0,)), ((), ())),
            precision=lax.Precision.HIGHEST, preferred_element_type=F32,
        )
        for i in range(blocks):
            work[i] -= update[i * size : (i + 1) * size]
        return carry

    return blocks, step


def gather_over_obs(n_obs, o, p, ext, send, recv):
    side, across, _ = partners(n_obs, o)
    near, over = (side, p), (across, p)
    blocks = (ext.shape[0] - 2 * REACH) // (4 * n_obs)
    order = [
        [(o, 0, near), (o, 2, over)],
        [(o, 1, near), (o, 3, over)],
        [(o, 2, near), (o, 0, over)],
        [(o, 3, near), (o, 1, over)],
        [(side, 0, over), (across, 2, near)],
        [(side, 1, over), (across, 3, near)],
    ]
    copies = []

    def stage(i):
        for j, (source, h, device) in enumerate(order[i]):
            if i >= 4:
                copies[2 * (i - 4) + j].wait()
            start = REACH + (4 * quarter(n_obs, source, p) + h) * blocks
            ref = ext.at[pl.ds(start, blocks)]
            slot = 2 * i + j
            copy = remote(ref, ref, send.at[slot], recv.at[slot], device)
            copy.start()
            copies.append(copy)

    def finish():
        for copy in copies[4:]:
            copy.wait()

    return stage, finish


def main_kernel(
    n_obs, n_par, offs, probes, coeffs, jac_ref, ext_out, image_out, inverse, ritz,
    low, high, values, held, jac, ls, image, part, got, fwd, adj, adj_got, own, ph, par,
    bands, bands_low, bands_high, diagonal, sample, lower, upper, from_low, from_high, hs,
    ext, ags, work, part2, got2, par2, ws, *rest,
):
    o, p = lax.axis_index("obs"), lax.axis_index("par")
    q = quarter(n_obs, o, p)
    count = n_obs * n_par
    order = p * n_obs + q
    rows, width = image.shape
    total_blocks = rows // BLK
    blocks = total_blocks // n_obs
    side_blocks = 2 * REACH
    below = (o, lax.rem(p + n_par - 1, n_par))
    above = (o, lax.rem(p + 1, n_par))
    first_sum, second_sum = rest[: len(rest) // 2], rest[len(rest) // 2 :]
    loads = [
        pltpu.make_async_copy(probes, values, ls.at[0]),
        pltpu.make_async_copy(coeffs, held, ls.at[1]),
        pltpu.make_async_copy(probes.at[pl.ds(0, side_blocks)], low.at[pl.ds(REACH, side_blocks)], ls.at[2]),
        pltpu.make_async_copy(
            probes.at[pl.ds(total_blocks - side_blocks, side_blocks)], high.at[pl.ds(0, side_blocks)], ls.at[3]
        ),
        pltpu.make_async_copy(jac_ref, jac, ls.at[4]),
    ]
    for load in loads:
        load.start()
    greet(all_peers(n_obs, n_par, o, p))
    down = remote(
        probes.at[pl.ds(0, REACH)], high.at[pl.ds(side_blocks, REACH)], ph.at[0], ph.at[1], below
    )
    up = remote(
        probes.at[pl.ds(total_blocks - REACH, REACH)], low.at[pl.ds(0, REACH)], ph.at[2], ph.at[3], above
    )

    @pl.when(p > 0)
    def _():
        down.start()

    @pl.when(p < n_par - 1)
    def _():
        up.start()

    @pl.when(p == 0)
    def _():
        low[pl.ds(0, REACH)] = jnp.zeros((REACH,) + low.shape[1:], BF16)

    @pl.when(p == n_par - 1)
    def _():
        high[pl.ds(side_blocks, REACH)] = jnp.zeros((REACH,) + high.shape[1:], BF16)

    loads[0].wait()
    loads[1].wait()

    def inner(b, carry):
        image[pl.ds(pl.multiple_of(b * BLK, BLK), BLK), :] = prior_block(b, 0, values, held, offs)
        return carry

    lax.fori_loop(REACH, total_blocks - REACH, inner, 0, unroll=4)
    loads[4].wait()
    end = rows - HALO
    total = jnp.dot(jac[:, HALO:end], image[HALO:end, :], preferred_element_type=F32)
    @pl.when(p > 0)
    def _():
        down.wait_send()
        up.wait_recv()

    @pl.when(p < n_par - 1)
    def _():
        up.wait_send()
        down.wait_recv()

    loads[2].wait()
    loads[3].wait()
    for b in range(REACH):
        image[pl.ds(b * BLK, BLK), :] = prior_block(b, -REACH, low, held, offs)
    for b in range(total_blocks - REACH, total_blocks):
        image[pl.ds(b * BLK, BLK), :] = prior_block(b, total_blocks - 2 * REACH, high, held, offs)
    total = total + jnp.dot(jac[:, :HALO], image[:HALO, :], preferred_element_type=F32)
    total = total + jnp.dot(jac[:, end:], image[end:, :], preferred_element_type=F32)
    mine = sum_over_par(n_par, o, p, total, part, got, par.at[0], par.at[1])()
    fwd[p] = mine.astype(BF16)
    copies = []
    for d in range(1, n_par):
        copy = remote(fwd.at[p], fwd.at[p], par.at[2, d], par.at[3, d], (o, lax.rem(p + d, n_par)))
        copy.start()
        copies.append(copy)
    for copy in copies:
        copy.wait()
    sum_over_obs(
        n_obs, o, p, jac, fwd[...].reshape(jac.shape[0], width), adj, adj_got, hs.at[0], hs.at[1], own,
        lambda: prepare_bands(offs, held, q * blocks, bands, bands_low, bands_high, diagonal),
    )
    lower[...] = two_products(bands_low, own[:HALO, :]).astype(BF16)
    upper[...] = two_products(bands_high, own[pl.ds(blocks * BLK - HALO, HALO), :]).astype(BF16)
    before = lax.rem(order + count - 1, count)
    after = lax.rem(order + 1, count)
    down = remote(
        lower, from_high, hs.at[2, 0], hs.at[3, 0],
        (owner(n_obs, lax.rem(before, n_obs), before // n_obs), before // n_obs),
    )
    up = remote(
        upper, from_low, hs.at[2, 1], hs.at[3, 1],
        (owner(n_obs, lax.rem(after, n_obs), after // n_obs), after // n_obs),
    )

    @pl.when(order > 0)
    def _():
        down.start()

    @pl.when(order < count - 1)
    def _():
        up.start()

    sample[...] = two_products(bands, own[...])
    for b in range(blocks):
        here = pl.ds(b * BLK, BLK)
        sample[here, :] += jnp.dot(diagonal[b], own[here, :], preferred_element_type=F32)

    @pl.when(order > 0)
    def _():
        down.wait_send()
        up.wait_recv()
        sample[pl.ds(0, HALO), :] += from_low[...].astype(F32)

    @pl.when(order < count - 1)
    def _():
        up.wait_send()
        down.wait_recv()
        sample[pl.ds(blocks * BLK - HALO, HALO), :] += from_high[...].astype(F32)

    ext[pl.ds(REACH + q * blocks, blocks)] = sample[...].astype(BF16).reshape(blocks, BLK, width)
    stage, finish = gather_over_obs(n_obs, o, p, ext, ags.at[0], ags.at[1])
    stage(0)
    value = lax.dot_general(
        sample[...], sample[...], (((0,), (0,)), ((), ())),
        precision=lax.Precision.HIGHEST, preferred_element_type=F32,
    ) / (sample.shape[0] * count)

    def gather_more(*which):
        return lambda: [stage(i) for i in which]

    matrix = sum_everywhere(
        n_obs, n_par, o, p, value, *first_sum, [gather_more(1, 2), gather_more(3, 4)]
    )
    stage(5)
    steps, step = inverse_factor_steps(matrix, work, inverse, inverse.shape[1])
    lax.fori_loop(0, 1, step, 0)
    finish()
    writes = [pltpu.make_async_copy(ext.at[pl.ds(REACH, total_blocks)], ext_out, ws.at[0])]
    writes[0].start()
    lowest, highest = REACH, REACH + total_blocks
    to_below = remote(
        ext.at[pl.ds(lowest, REACH)], ext.at[pl.ds(highest, REACH)], hs.at[2, 2], hs.at[3, 2], below
    )
    to_above = remote(
        ext.at[pl.ds(highest - REACH, REACH)], ext.at[pl.ds(0, REACH)], hs.at[2, 3], hs.at[3, 3], above
    )

    @pl.when(p > 0)
    def _():
        to_below.start()

    @pl.when(p < n_par - 1)
    def _():
        to_above.start()

    @pl.when(p == 0)
    def _():
        ext[pl.ds(0, REACH)] = jnp.zeros((REACH,) + ext.shape[1:], BF16)

    @pl.when(p == n_par - 1)
    def _():
        ext[pl.ds(highest, REACH)] = jnp.zeros((REACH,) + ext.shape[1:], BF16)

    lax.fori_loop(1, steps - 1, step, 0)

    @pl.when(p > 0)
    def _():
        to_below.wait_send()
        to_above.wait_recv()

    @pl.when(p < n_par - 1)
    def _():
        to_above.wait_send()
        to_below.wait_recv()

    def outer(b, carry):
        image[pl.ds(pl.multiple_of(b * BLK, BLK), BLK), :] = prior_block(b, -REACH, ext, held, offs)
        return carry

    lax.fori_loop(0, total_blocks, outer, 0, unroll=4)
    writes.append(pltpu.make_async_copy(image, image_out, ws.at[1]))
    writes[1].start()
    total = jnp.dot(jac[...], image[...], preferred_element_type=F32)
    finish_sum = sum_over_par(n_par, o, p, total, part2, got2, par2.at[0], par2.at[1])
    lax.fori_loop(steps - 1, steps, step, 0)
    mine = finish_sum()
    factor = inverse[...].reshape(width, width)
    mine = lax.dot_general(
        mine, factor, (((1,), (1,)), ((), ())), precision=lax.Precision.HIGHEST, preferred_element_type=F32
    )
    value = lax.dot_general(
        mine, mine, (((0,), (0,)), ((), ())),
        precision=lax.Precision.HIGHEST, preferred_element_type=F32,
    ) / (jac.shape[0] * n_obs)
    ritz[...] = sum_everywhere(n_obs, n_par, o, p, value, *second_sum)
    for write in writes:
        write.wait()


def last_kernel(inverse, sample, mapped, basis, image, high, low):
    @pl.when(pl.program_id(0) == 0)
    def _():
        high[...] = inverse[...].astype(BF16)
        low[...] = (inverse[...] - high[...].astype(F32)).astype(BF16)

    def solve(value):
        last = (((1,), (1,)), ((), ()))
        return (
            lax.dot_general(value, high[...], last, preferred_element_type=F32)
            + lax.dot_general(value, low[...], last, preferred_element_type=F32)
        ).astype(BF16)

    basis[...] = solve(sample[...])
    image[...] = solve(mapped[...])


def dma(*count):
    return pltpu.SemaphoreType.DMA(count)


def body(n_obs, n_par, jacobian, probes, coeffs, offsets):
    obs, rows = jacobian.shape
    width = probes.shape[1]
    own = rows // n_obs
    half = own // 2
    total_blocks = rows // BLK
    block = 64
    hbm = pl.BlockSpec(memory_space=pltpu.HBM)
    anywhere = pl.BlockSpec(memory_space=pl.ANY)
    parts = [pltpu.VMEM((n_par, obs // n_par, width), BF16)] * 2
    ext, mapped, inverse, ritz = pl.pallas_call(
        functools.partial(main_kernel, n_obs, n_par),
        out_shape=[
            jax.ShapeDtypeStruct((total_blocks, BLK, width), BF16),
            jax.ShapeDtypeStruct((rows, width), BF16),
            jax.ShapeDtypeStruct((width // block, block, width), F32),
            jax.ShapeDtypeStruct((width, width), F32),
        ],
        in_specs=[SMEM, hbm, hbm, hbm],
        out_specs=[anywhere, anywhere, VMEM, VMEM],
        scratch_shapes=[pltpu.VMEM((3 * REACH, BLK, width), BF16)] * 2
        + [
            pltpu.VMEM((total_blocks, BLK, width), BF16),
            pltpu.VMEM(coeffs.shape, BF16),
            pltpu.VMEM((obs, rows), BF16),
            dma(5),
            pltpu.VMEM((rows, width), BF16),
        ]
        + parts
        + [
            pltpu.VMEM((n_par, obs // n_par, width), BF16),
            pltpu.VMEM((8, half, width), BF16),
            pltpu.VMEM((6, half, width), BF16),
            pltpu.VMEM((own, width), BF16),
            dma(4),
            dma(4, n_par),
            pltpu.VMEM((2, own, own), BF16),
            pltpu.VMEM((2, HALO, HALO), BF16),
            pltpu.VMEM((2, HALO, HALO), BF16),
            pltpu.VMEM((own // BLK, BLK, BLK), BF16),
            pltpu.VMEM((own, width), F32),
        ]
        + [pltpu.VMEM((HALO, width), BF16)] * 4
        + [
            dma(4, 6),
            pltpu.VMEM((total_blocks + 2 * REACH, BLK, width), BF16),
            dma(2, 12),
            pltpu.VMEM((width // block, block, 2 * width), F32),
        ]
        + parts
        + [dma(2, n_par), dma(2)]
        + sum_scratch(n_obs, n_par, width, F32)
        + sum_scratch(n_obs, n_par, width, BF16),
        compiler_params=pltpu.CompilerParams(
            collective_id=0, has_side_effects=True, vmem_limit_bytes=46 * 1024 * 1024
        ),
        name="main",
    )(offsets, probes.reshape(-1, BLK, width), coeffs, jacobian)
    tall = rows // 4
    basis, image = pl.pallas_call(
        last_kernel,
        grid=(rows // tall,),
        out_shape=[jax.ShapeDtypeStruct((rows, width), BF16)] * 2,
        in_specs=[
            pl.BlockSpec((width, width), lambda i: (0, 0)),
            pl.BlockSpec((tall, width), lambda i: (i, 0)),
            pl.BlockSpec((tall, width), lambda i: (i, 0)),
        ],
        out_specs=[pl.BlockSpec((tall, width), lambda i: (i, 0))] * 2,
        scratch_shapes=[pltpu.VMEM((width, width), BF16)] * 2,
        compiler_params=pltpu.CompilerParams(vmem_limit_bytes=16 * 1024 * 1024),
        name="last",
    )(inverse.reshape(width, width), ext.reshape(-1, width), mapped)
    return basis, image, ritz


def solution(mesh):
    return jax.shard_map(
        functools.partial(body, mesh.shape["obs"], mesh.shape["par"]),
        mesh=mesh,
        in_specs=(P("obs", "par"), P("par", None), P("par", None, None, None), P("par", None)),
        out_specs=(P("par", None), P("par", None), P()),
        check_vma=False,
    )
```

```python
import functools

import jax
import jax.numpy as jnp
from jax import lax
from jax.experimental import pallas as pl
from jax.experimental.pallas import tpu as pltpu
from jax.sharding import PartitionSpec as P

BLK = 128
REACH = 4
HALO = REACH * BLK
MESH = pl.DeviceIdType.MESH
F32 = jnp.float32
BF16 = jnp.bfloat16
VMEM = pl.BlockSpec(memory_space=pltpu.VMEM)
SMEM = pl.BlockSpec(memory_space=pltpu.SMEM)
LIMIT = 48 * 1024 * 1024


def greet(devices):
    barrier = pltpu.get_barrier_semaphore()
    for device in devices:
        pl.semaphore_signal(barrier, inc=1, device_id=device, device_id_type=MESH)
    pl.semaphore_wait(barrier, len(devices))


def remote(src, dst, send, recv, device):
    return pltpu.make_async_remote_copy(
        src_ref=src, dst_ref=dst, send_sem=send, recv_sem=recv, device_id=device, device_id_type=MESH
    )


def prior_block(b, base, source, coeffs, offs):
    def pick(offset):
        block = b - base + offset
        if len(source.shape) == 3:
            return source[block]
        return jnp.concatenate([source[0, block], source[1, block]], axis=1)

    left = jnp.concatenate([coeffs[b, 0], coeffs[b, 1], coeffs[b, 2]], axis=1)
    right = jnp.concatenate([pick(0), pick(offs[0, b]), pick(offs[1, b])], axis=0)
    return jnp.dot(left, right, preferred_element_type=F32).astype(BF16)


def split(value):
    upper = value.astype(BF16)
    return upper, (value - upper.astype(F32)).astype(BF16)


def dot_f32(left, right, dims):
    return sum(
        lax.dot_general(left[i], right[j], (dims, ((), ())), preferred_element_type=F32)
        for i, j in ((0, 0), (0, 1), (1, 0))
    )


def all_peers(n_obs, n_par, o, p):
    return [
        (lax.rem(o + i, n_obs), lax.rem(p + j, n_par))
        for j in range(n_par)
        for i in range(n_obs)
        if i or j
    ]


def chip_peers(n_obs, n_par, o, p):
    chips = n_par // 2
    z, core = p // 2, lax.rem(p, 2)
    return [
        (lax.rem(o + i, n_obs), 2 * lax.rem(z + j, chips) + core)
        for j in range(chips)
        for i in range(n_obs)
        if i or j
    ]


def partners(n_obs, o):
    side = o + 1 - 2 * lax.rem(o, 2)
    half = n_obs // 2
    return side, lax.rem(o + half, n_obs), lax.rem(side + half, n_obs)


def quarter(n_obs, o, p):
    y = o // 2
    place = 2 * y + lax.rem(o + y, 2)
    return place + lax.rem(p, 2) * (n_obs - 1 - 2 * place)


def owner(n_obs, q, p):
    place = q + lax.rem(p, 2) * (n_obs - 1 - 2 * q)
    y = place // 2
    return 2 * y + lax.rem(place + y, 2)


def wait_all(ref, sem):
    pltpu.make_async_copy(ref, ref, sem).wait()


def sum_over_par(n_par, o, p, total, part, got, send, recv):
    piece = part.shape[1]
    for q in range(n_par):
        part[q] = total[q * piece : (q + 1) * piece].astype(BF16)
    copies = []
    for d in range(1, n_par):
        q = lax.rem(p + d, n_par)
        copy = remote(part.at[q], got.at[d], send.at[d], recv.at[d], (o, q))
        copy.start()
        copies.append(copy)

    def finish():
        mine = part[p].astype(F32)
        for d in range(1, n_par):
            copies[d - 1].wait()
            mine = mine + got[d].astype(F32)
        return mine

    return finish


def sum_over_obs(n_obs, o, p, jac, forward, adj, got, send, recv, out):
    side, across, far = partners(n_obs, o)
    half = adj.shape[1]
    near = (side, p)
    over = (across, p)
    copies = []

    def product(slot, device, h):
        start = pl.multiple_of((2 * quarter(n_obs, device, p) + h) * half, half)
        value = lax.dot_general(
            jac[:, pl.ds(start, half)], forward(), (((0,), (0,)), ((), ())), preferred_element_type=F32
        )
        adj[slot] = value.astype(BF16)

    def send_slot(slot, device):
        copy = remote(adj.at[slot], got.at[slot], send.at[slot], recv.at[slot], device)
        copy.start()
        copies.append(copy)

    def first():
        product(0, far, 0)
        send_slot(0, near)
        product(1, far, 1)
        send_slot(1, over)

    def second():
        product(2, side, 0)
        send_slot(2, near)
        product(3, across, 1)
        send_slot(3, over)

    def rest():
        product(4, across, 0)
        product(5, side, 1)
        product(6, o, 0)
        product(7, o, 1)

    def third():
        for slot, device in ((0, over), (1, near)):
            copies[slot].wait()
            adj[4 + slot] = (adj[4 + slot].astype(F32) + got[slot].astype(F32)).astype(BF16)
            send_slot(4 + slot, device)

    def finish():
        for h in range(2):
            copies[2 + h].wait()
            copies[4 + h].wait()
            total = adj[6 + h].astype(F32) + got[2 + h].astype(F32) + got[4 + h].astype(F32)
            out[pl.ds(h * half, half), :] = total.astype(BF16)

    return first, second, rest, third, finish


def prepare_bands(offs, coeffs, first, middle, low, high, diagonal):
    blocks = diagonal.shape[0]
    zero = jnp.zeros((BLK, BLK), BF16)
    low[...] = jnp.zeros_like(low)
    high[...] = jnp.zeros_like(high)
    for b in range(blocks):
        diagonal[b] = coeffs[first + b, 0].T
        columns = pl.ds(b * BLK, BLK)
        for j in range(2):
            block = coeffs[first + b, j + 1].T
            offset = offs[j, first + b]
            for c in range(blocks):
                if abs(c - b) > REACH:
                    middle[j, pl.ds(c * BLK, BLK), columns] = zero
            for d in range(-REACH, REACH + 1):
                value = jnp.where(offset == d, block, zero)
                c = b + d
                if c < 0:
                    low[j, pl.ds((c + REACH) * BLK, BLK), columns] = value
                elif c >= blocks:
                    columns_high = pl.ds((b - blocks + REACH) * BLK, BLK)
                    high[j, pl.ds((c - blocks) * BLK, BLK), columns_high] = value
                else:
                    middle[j, pl.ds(c * BLK, BLK), columns] = value


def two_products(bands, values):
    return jnp.dot(bands[0], values, preferred_element_type=F32) + jnp.dot(
        bands[1], values, preferred_element_type=F32
    )


def sum_everywhere(n_obs, n_par, o, p, value, pair_send, pair_got, send, got, out, sems, beside=()):
    beside = list(beside) + [lambda: None] * 2
    core = lax.rem(p, 2)
    other = (o, p + 1 - 2 * core)
    peers = chip_peers(n_obs, n_par, o, p)
    place = (p // 2) * n_obs + o
    count, piece, width = send.shape
    kind = send.dtype
    tall = count * piece
    pair_send[0] = value[:tall].astype(kind)
    pair_send[1] = value[tall:].astype(kind)
    copy = remote(pair_send.at[1 - core], pair_got, sems.at[0], sems.at[1], other)
    copy.start()
    copy.wait()
    mine = pair_send[core].astype(F32) + pair_got[...].astype(F32)
    for j in range(count):
        send[j] = mine[j * piece : (j + 1) * piece].astype(kind)
    for d, device in enumerate(peers, 1):
        target = (device[1] // 2) * n_obs + device[0]
        remote(send.at[target], got.at[d], sems.at[2], sems.at[3], device).start()
    beside[0]()
    mine = send[place].astype(F32)
    rest = got.at[pl.ds(1, count - 1)]
    wait_all(rest, sems.at[2])
    wait_all(rest, sems.at[3])
    for d in range(1, count):
        mine = mine + got[d].astype(F32)
    out[core, place] = mine.astype(kind)
    for device in peers:
        remote(out.at[core, place], out.at[core, place], sems.at[4], sems.at[5], device).start()
    beside[1]()
    wait_all(rest, sems.at[4])
    wait_all(rest, sems.at[5])
    copy = remote(out.at[core], out.at[core], sems.at[6], sems.at[7], other)
    copy.start()
    copy.wait()
    return jnp.concatenate([out[c, j].astype(F32) for c in range(2) for j in range(count)], axis=0)


def sum_directly(n_obs, n_par, o, p, value, send, got, out, sems, beside=()):
    peers = all_peers(n_obs, n_par, o, p)
    place = p * n_obs + o
    count, piece, width = send.shape
    kind = send.dtype
    for j in range(count):
        send[j] = value[j * piece : (j + 1) * piece].astype(kind)
    for d, (i, q) in enumerate(peers, 1):
        remote(send.at[q * n_obs + i], got.at[d], sems.at[0], sems.at[1], (i, q)).start()
    beside[0]()
    mine = send[place].astype(F32)
    rest = got.at[pl.ds(1, count - 1)]
    wait_all(rest, sems.at[0])
    wait_all(rest, sems.at[1])
    for d in range(1, count):
        mine = mine + got[d].astype(F32)
    out[place] = mine.astype(kind)
    for device in peers:
        remote(out.at[place], out.at[place], sems.at[2], sems.at[3], device).start()
    beside[1]()
    wait_all(rest, sems.at[2])
    wait_all(rest, sems.at[3])
    return jnp.concatenate([out[j].astype(F32) for j in range(count)], axis=0)


def few_devices(n_obs, n_par, width):
    return width // (n_obs * n_par) >= 8


def sum_scratch(n_obs, n_par, width, kind):
    count = n_obs * n_par // 2
    piece = width // 2 // count
    if kind == BF16 and few_devices(n_obs, n_par, width):
        return [pltpu.VMEM((2 * count, piece, width), kind)] * 3 + [dma(4)]
    return [
        pltpu.VMEM((2, width // 2, width), kind),
        pltpu.VMEM((width // 2, width), kind),
        pltpu.VMEM((count, piece, width), kind),
        pltpu.VMEM((count, piece, width), kind),
        pltpu.VMEM((2, count, piece, width), kind),
        dma(8),
    ]


def small_inverse_factor(matrix):
    size = matrix.shape[0]
    row = lax.broadcasted_iota(jnp.int32, (size, size), 0)
    lane = lax.broadcasted_iota(jnp.int32, (size, size), 1)
    work = jnp.concatenate([matrix, (row == lane).astype(F32)], axis=1)
    group = 8
    parts = [work[g : g + group] for g in range(0, size, group)]
    index = lax.broadcasted_iota(jnp.int32, (group, 2 * size), 0)
    scales = []
    for first in range(size // group):
        start = first * group
        columns = [
            [jnp.broadcast_to(part[:, start + t : start + t + 1], part.shape) for part in parts[first:]]
            for t in range(group)
        ]
        for t in range(group):
            pivot = columns[t][0][t : t + 1]
            scales.append(lax.rsqrt(pivot))
            reciprocal = 1.0 / pivot
            scaled = parts[first][t : t + 1] * reciprocal
            columns[t][0] = jnp.where(index > t, columns[t][0], 0.0)
            for u in range(t + 1, group):
                ratio = columns[u][0][t : t + 1] * reciprocal
                columns[u] = [c - e * ratio for c, e in zip(columns[u], columns[t])]
            for g, column in enumerate(columns[t]):
                parts[first + g] = parts[first + g] - column * scaled
    rows = [parts[j // group][j % group : j % group + 1] * scales[j] for j in range(size)]
    return jnp.concatenate(rows, axis=0)[:, size:]


def inverse_factor_steps(gram, work, out, size):
    blocks = work.shape[0]
    width = blocks * size
    row = lax.broadcasted_iota(jnp.int32, (size, width), 0)
    lane = lax.broadcasted_iota(jnp.int32, (size, width), 1)
    for k in range(blocks):
        work[k, :, pl.ds(0, width)] = gram[k * size : (k + 1) * size]
        work[k, :, pl.ds(width, width)] = (lane == row + k * size).astype(F32)

    def step(k, carry):
        rows = work[k]
        shift = lax.rem(width - k * size, width)
        diagonal = pltpu.roll(rows[:, :width], shift, 1)[:, :size]
        small = small_inverse_factor(diagonal)
        upper = jnp.dot(small, rows, precision=lax.Precision.HIGHEST, preferred_element_type=F32)
        out[k] = upper[:, width:]
        left = jnp.where(lane >= (k + 1) * size, upper[:, :width], 0.0)
        update = lax.dot_general(
            left, upper, (((0,), (0,)), ((), ())),
            precision=lax.Precision.HIGHEST, preferred_element_type=F32,
        )
        for i in range(blocks):
            work[i] -= update[i * size : (i + 1) * size]
        return carry

    return blocks, step


def gather_over_obs(n_obs, o, p, ext, send, recv):
    side, across, _ = partners(n_obs, o)
    near, over = (side, p), (across, p)
    blocks = ext.shape[0] // (2 * n_obs)
    order = [
        [(o, 0, near), (o, 1, over)],
        [(o, 1, near), (o, 0, over)],
        [(side, 0, over), (across, 1, near)],
    ]
    copies = []

    def stage(i):
        for j, (source, h, device) in enumerate(order[i]):
            if i == 2:
                copies[j].wait()
            start = (2 * quarter(n_obs, source, p) + h) * blocks
            ref = ext.at[pl.ds(start, blocks)]
            slot = 2 * i + j
            copy = remote(ref, ref, send.at[slot], recv.at[slot], device)
            copy.start()
            copies.append(copy)

    def finish():
        for copy in copies[2:]:
            copy.wait()

    return stage, finish


def swap_sides(at_start, at_end, low_copy, high_copy):
    def start():
        @pl.when(at_start)
        def _():
            low_copy.start()

        @pl.when(at_end)
        def _():
            high_copy.start()

    def finish(low_arrived=None, high_arrived=None):
        @pl.when(at_start)
        def _():
            low_copy.wait_send()
            high_copy.wait_recv()
            if low_arrived is not None:
                low_arrived()

        @pl.when(at_end)
        def _():
            high_copy.wait_send()
            low_copy.wait_recv()
            if high_arrived is not None:
                high_arrived()

    return start, finish


def main_kernel(
    n_obs, n_par, offs, probes, coeffs, jac_ref, basis_out, image_out, ritz,
    low, high, values, held, jac, ls, image, part, got, fwd, adj, adj_got, own, ph, par, rs,
    bands, bands_low, bands_high, diagonal, sample, lower, upper, from_low, from_high, hs,
    low2, high2, fine, ext, ags, work, inverse, part2, got2, par2, basis, mapped, ws, *rest,
):
    o, p = lax.axis_index("obs"), lax.axis_index("par")
    q = quarter(n_obs, o, p)
    count = n_obs * n_par
    order = p * n_obs + q
    rows, width = image.shape
    half = width // 2
    total_blocks = rows // BLK
    blocks = total_blocks // n_obs
    side_blocks = 2 * REACH
    below = (o, lax.rem(p + n_par - 1, n_par))
    above = (o, lax.rem(p + 1, n_par))
    first_sum, second_sum = rest[:6], rest[6:]
    loads = [
        pltpu.make_async_copy(probes, values, ls.at[0]),
        pltpu.make_async_copy(coeffs, held, ls.at[1]),
        pltpu.make_async_copy(jac_ref, jac, ls.at[2]),
    ]
    sides = [
        pltpu.make_async_copy(values.at[pl.ds(0, side_blocks)], low.at[pl.ds(REACH, side_blocks)], ls.at[3]),
        pltpu.make_async_copy(
            values.at[pl.ds(total_blocks - side_blocks, side_blocks)], high.at[pl.ds(0, side_blocks)], ls.at[4]
        ),
    ]
    for load in loads:
        load.start()
    greet(all_peers(n_obs, n_par, o, p))
    loads[0].wait()
    start, finish_sides = swap_sides(
        p > 0,
        p < n_par - 1,
        remote(values.at[pl.ds(0, REACH)], high.at[pl.ds(side_blocks, REACH)], ph.at[0], ph.at[1], below),
        remote(
            values.at[pl.ds(total_blocks - REACH, REACH)], low.at[pl.ds(0, REACH)], ph.at[2], ph.at[3], above
        ),
    )
    start()
    for side in sides:
        side.start()

    @pl.when(p == 0)
    def _():
        low[pl.ds(0, REACH)] = jnp.zeros((REACH,) + low.shape[1:], BF16)
        low2[:, pl.ds(0, REACH)] = jnp.zeros((2, REACH) + ext.shape[2:], BF16)

    @pl.when(p == n_par - 1)
    def _():
        high[pl.ds(side_blocks, REACH)] = jnp.zeros((REACH,) + high.shape[1:], BF16)
        high2[:, pl.ds(side_blocks, REACH)] = jnp.zeros((2, REACH) + ext.shape[2:], BF16)

    loads[1].wait()

    def inner(b, carry):
        image[pl.ds(pl.multiple_of(b * BLK, BLK), BLK), :] = prior_block(b, 0, values, held, offs)
        return carry

    lax.fori_loop(REACH, total_blocks - REACH, inner, 0, unroll=4)
    loads[2].wait()
    end = rows - HALO
    halves = [slice(0, half), slice(half, width)]
    totals = [
        jnp.dot(jac[:, HALO:end], image[HALO:end, columns], preferred_element_type=F32) for columns in halves
    ]
    finish_sides()
    for side in sides:
        side.wait()
    for b in range(REACH):
        image[pl.ds(b * BLK, BLK), :] = prior_block(b, -REACH, low, held, offs)
    for b in range(total_blocks - REACH, total_blocks):
        image[pl.ds(b * BLK, BLK), :] = prior_block(b, total_blocks - 2 * REACH, high, held, offs)
    sums = []
    for k, columns in enumerate(halves):
        total = totals[k]
        total = total + jnp.dot(jac[:, :HALO], image[:HALO, columns], preferred_element_type=F32)
        total = total + jnp.dot(jac[:, end:], image[end:, columns], preferred_element_type=F32)
        sums.append(sum_over_par(n_par, o, p, total, part.at[k], got.at[k], par.at[k, 0], par.at[k, 1]))
    gathers = []
    for k in range(2):
        fwd[k, p] = sums[k]().astype(BF16)
        mine = fwd.at[k, p]
        copies = []
        for d in range(1, n_par):
            copy = remote(mine, mine, par.at[k, 2, d], par.at[k, 3, d], (o, lax.rem(p + d, n_par)))
            copy.start()
            copies.append(copy)
        gathers.append(copies)

    def reduce_half(k):
        def forward():
            return fwd[k].reshape(jac.shape[0], half)

        return sum_over_obs(
            n_obs, o, p, jac, forward, adj.at[k], adj_got.at[k], rs.at[k, 0], rs.at[k, 1], own.at[k]
        )

    reduce0, reduce1 = reduce_half(0), reduce_half(1)
    for copy in gathers[0]:
        copy.wait()
    reduce0[0]()
    reduce0[1]()
    for copy in gathers[1]:
        copy.wait()
    reduce1[0]()
    reduce0[2]()
    reduce0[3]()
    reduce1[1]()
    reduce1[2]()
    prepare_bands(offs, held, q * blocks, bands, bands_low, bands_high, diagonal)
    reduce1[3]()
    before = lax.rem(order + count - 1, count)
    after = lax.rem(order + 1, count)
    down_device = (owner(n_obs, lax.rem(before, n_obs), before // n_obs), before // n_obs)
    up_device = (owner(n_obs, lax.rem(after, n_obs), after // n_obs), after // n_obs)
    swaps = []

    def prior(k):
        lower[k] = two_products(bands_low, own[k, :HALO, :]).astype(BF16)
        upper[k] = two_products(bands_high, own[k, pl.ds(blocks * BLK - HALO, HALO), :]).astype(BF16)
        start, finish_sides = swap_sides(
            order > 0,
            order < count - 1,
            remote(lower.at[k], from_high.at[k], hs.at[k, 0], hs.at[k, 1], down_device),
            remote(upper.at[k], from_low.at[k], hs.at[k, 2], hs.at[k, 3], up_device),
        )
        start()
        swaps.append(finish_sides)
        sample[:, halves[k]] = two_products(bands, own[k])
        for b in range(blocks):
            here = pl.ds(b * BLK, BLK)
            sample[here, halves[k]] += jnp.dot(diagonal[b], own[k, here, :], preferred_element_type=F32)

    def prior_end(k):
        def low_arrived():
            sample[pl.ds(0, HALO), halves[k]] += from_low[k].astype(F32)

        def high_arrived():
            sample[pl.ds(blocks * BLK - HALO, HALO), halves[k]] += from_high[k].astype(F32)

        swaps[k](low_arrived, high_arrived)
        parts = split(sample[:, halves[k]])
        ext[k, pl.ds(q * blocks, blocks)] = parts[0].reshape(blocks, BLK, half)
        fine[k] = parts[1]

    reduce0[4]()
    prior(0)
    reduce1[4]()
    prior(1)
    prior_end(0)
    stage0, finish0 = gather_over_obs(n_obs, o, p, ext.at[0], ags.at[0, 0], ags.at[0, 1])
    stage1, finish1 = gather_over_obs(n_obs, o, p, ext.at[1], ags.at[1, 0], ags.at[1, 1])
    stage0(0)
    stage0(1)
    coarse = [ext.at[k, pl.ds(q * blocks, blocks)] for k in range(2)]

    def cross(i, j):
        left = coarse[i][...].reshape(fine.shape[1:]), fine[i]
        right = coarse[j][...].reshape(fine.shape[1:]), fine[j]
        both = jnp.concatenate(right, axis=1)
        over_rows = (((0,), (0,)), ((), ()))
        value = lax.dot_general(left[0], both, over_rows, preferred_element_type=F32)
        if i == j:
            other = value[:, half:].T
        else:
            other = lax.dot_general(left[1], right[0], over_rows, preferred_element_type=F32)
        return value[:, :half] + value[:, half:] + other

    first_block = cross(0, 0)
    prior_end(1)
    off_block = cross(1, 0)
    value = jnp.concatenate(
        [
            jnp.concatenate([first_block, off_block.T], axis=1),
            jnp.concatenate([off_block, cross(1, 1)], axis=1),
        ],
        axis=0,
    ) / (sample.shape[0] * count)

    def more0():
        stage0(2)
        stage1(0)

    def more1():
        stage1(1)
        stage1(2)

    matrix = sum_everywhere(n_obs, n_par, o, p, value, *first_sum, [more0, more1])
    steps, step = inverse_factor_steps(matrix, work, inverse, inverse.shape[1])
    lax.fori_loop(0, 1, step, 0)
    finish0()
    finish1()
    last = total_blocks - REACH
    start, finish_sides = swap_sides(
        p > 0,
        p < n_par - 1,
        remote(
            ext.at[:, pl.ds(0, REACH)], high2.at[:, pl.ds(side_blocks, REACH)], hs.at[2, 0], hs.at[2, 1], below
        ),
        remote(ext.at[:, pl.ds(last, REACH)], low2.at[:, pl.ds(0, REACH)], hs.at[2, 2], hs.at[2, 3], above),
    )
    start()
    sides = [
        pltpu.make_async_copy(
            ext.at[:, pl.ds(0, side_blocks)], low2.at[:, pl.ds(REACH, side_blocks)], ls.at[3]
        ),
        pltpu.make_async_copy(
            ext.at[:, pl.ds(total_blocks - side_blocks, side_blocks)], high2.at[:, pl.ds(0, side_blocks)],
            ls.at[4],
        ),
    ]
    for side in sides:
        side.start()

    def outer(b, carry):
        image[pl.ds(pl.multiple_of(b * BLK, BLK), BLK), :] = prior_block(b, 0, ext, held, offs)
        return carry

    lax.fori_loop(REACH, last, outer, 0, unroll=4)
    total = jnp.dot(jac[:, HALO:end], image[HALO:end, :], preferred_element_type=F32)
    finish_sides()
    for side in sides:
        side.wait()
    for b in range(REACH):
        image[pl.ds(b * BLK, BLK), :] = prior_block(b, -REACH, low2, held, offs)
    for b in range(last, total_blocks):
        image[pl.ds(b * BLK, BLK), :] = prior_block(b, total_blocks - 2 * REACH, high2, held, offs)
    total = total + jnp.dot(jac[:, :HALO], image[:HALO, :], preferred_element_type=F32)
    total = total + jnp.dot(jac[:, end:], image[end:, :], preferred_element_type=F32)
    finish_sum = sum_over_par(n_par, o, p, total, part2, got2, par2.at[0], par2.at[1])
    lax.fori_loop(1, steps, step, 0)
    mine = finish_sum()
    factor = split(inverse[...].reshape(width, width))
    mine = split(dot_f32(split(mine), factor, ((1,), (1,))))
    value = dot_f32(mine, mine, ((0,), (0,))) / (jac.shape[0] * n_obs)

    def solve(value):
        last = (((1,), (1,)), ((), ()))
        return (
            lax.dot_general(value, factor[0], last, preferred_element_type=F32)
            + lax.dot_general(value, factor[1], last, preferred_element_type=F32)
        ).astype(BF16)

    tall = min(512, rows)

    def solve_basis():
        def tile(t, carry):
            here = pl.ds(t * (tall // BLK), tall // BLK)
            value = jnp.concatenate([ext[k, here].reshape(tall, half) for k in range(2)], axis=1)
            basis[pl.ds(pl.multiple_of(t * tall, tall), tall), :] = solve(value)
            return carry

        lax.fori_loop(0, rows // tall, tile, 0)
        pltpu.make_async_copy(basis, basis_out, ws.at[0]).start()

    def solve_image():
        def tile(t, carry):
            here = pl.ds(pl.multiple_of(t * tall, tall), tall)
            mapped[here, :] = solve(image[here, :])
            return carry

        lax.fori_loop(0, rows // tall, tile, 0)
        pltpu.make_async_copy(mapped, image_out, ws.at[1]).start()

    add = sum_directly if few_devices(n_obs, n_par, width) else sum_everywhere
    ritz[...] = add(n_obs, n_par, o, p, value, *second_sum, [solve_basis, solve_image])
    pltpu.make_async_copy(basis, basis_out, ws.at[0]).wait()
    pltpu.make_async_copy(mapped, image_out, ws.at[1]).wait()


def write_kernel(*refs):
    count = len(refs) // 2
    copies = [pltpu.make_async_copy(refs[i], refs[count + i], refs[-1].at[i]) for i in range(count)]
    for copy in copies:
        copy.start()
    for copy in copies:
        copy.wait()


def dma(*count):
    return pltpu.SemaphoreType.DMA(count)


def body(n_obs, n_par, jacobian, probes, coeffs, offsets):
    obs, rows = jacobian.shape
    width = probes.shape[1]
    half = width // 2
    own = rows // n_obs
    total_blocks = rows // BLK
    block = 64
    hbm = pl.BlockSpec(memory_space=pltpu.HBM)
    anywhere = pl.BlockSpec(memory_space=pl.ANY)
    piece = obs // n_par
    shapes = [
        jax.ShapeDtypeStruct((rows, width), BF16),
        jax.ShapeDtypeStruct((rows, width), BF16),
        jax.ShapeDtypeStruct((width, width), F32),
    ]
    results = pl.pallas_call(
        functools.partial(main_kernel, n_obs, n_par),
        out_shape=shapes,
        in_specs=[SMEM, hbm, hbm, hbm],
        out_specs=[anywhere, anywhere, VMEM],
        scratch_shapes=[pltpu.VMEM((3 * REACH, BLK, width), BF16)] * 2
        + [
            pltpu.VMEM((total_blocks, BLK, width), BF16),
            pltpu.VMEM(coeffs.shape, BF16),
            pltpu.VMEM((obs, rows), BF16),
            dma(5),
            pltpu.VMEM((rows, width), BF16),
        ]
        + [pltpu.VMEM((2, n_par, piece, half), BF16)] * 3
        + [
            pltpu.VMEM((2, 8, own // 2, half), BF16),
            pltpu.VMEM((2, 6, own // 2, half), BF16),
            pltpu.VMEM((2, own, half), BF16),
            dma(4),
            dma(2, 4, n_par),
            dma(2, 2, 6),
            pltpu.VMEM((2, own, own), BF16),
            pltpu.VMEM((2, HALO, HALO), BF16),
            pltpu.VMEM((2, HALO, HALO), BF16),
            pltpu.VMEM((own // BLK, BLK, BLK), BF16),
            pltpu.VMEM((own, width), F32),
        ]
        + [pltpu.VMEM((2, HALO, half), BF16)] * 4
        + [
            dma(3, 4),
            pltpu.VMEM((2, 3 * REACH, BLK, half), BF16),
            pltpu.VMEM((2, 3 * REACH, BLK, half), BF16),
            pltpu.VMEM((2, own, half), BF16),
            pltpu.VMEM((2, total_blocks, BLK, half), BF16),
            dma(2, 2, 6),
            pltpu.VMEM((width // block, block, 2 * width), F32),
            pltpu.VMEM((width // block, block, width), F32),
        ]
        + [pltpu.VMEM((n_par, piece, width), BF16)] * 2
        + [dma(2, n_par)]
        + [pltpu.VMEM((rows, width), BF16)] * 2
        + [dma(2)]
        + sum_scratch(n_obs, n_par, width, F32)
        + sum_scratch(n_obs, n_par, width, BF16),
        compiler_params=pltpu.CompilerParams(
            collective_id=0, has_side_effects=True, vmem_limit_bytes=LIMIT
        ),
        name="main",
    )(offsets.T, probes.reshape(-1, BLK, width), coeffs, jacobian)
    return pl.pallas_call(
        write_kernel,
        out_shape=shapes,
        in_specs=[anywhere] * 3,
        out_specs=[hbm] * 3,
        scratch_shapes=[dma(3)],
        compiler_params=pltpu.CompilerParams(vmem_limit_bytes=1024 * 1024),
        name="write",
    )(*results)


def solution(mesh):
    return jax.shard_map(
        functools.partial(body, mesh.shape["obs"], mesh.shape["par"]),
        mesh=mesh,
        in_specs=(P("obs", "par"), P("par", None), P("par", None, None, None), P("par", None)),
        out_specs=(P("par", None), P("par", None), P()),
        check_vma=False,
    )
```

```python
import functools

import jax
import jax.numpy as jnp
from jax import lax
from jax.experimental import pallas as pl
from jax.experimental.pallas import tpu as pltpu
from jax.sharding import PartitionSpec as P

BLK = 128
REACH = 4
HALO = REACH * BLK
MESH = pl.DeviceIdType.MESH
F32 = jnp.float32
BF16 = jnp.bfloat16
VMEM = pl.BlockSpec(memory_space=pltpu.VMEM)
SMEM = pl.BlockSpec(memory_space=pltpu.SMEM)
LIMIT = 48 * 1024 * 1024


def greet(devices):
    barrier = pltpu.get_barrier_semaphore()
    for device in devices:
        pl.semaphore_signal(barrier, inc=1, device_id=device, device_id_type=MESH)
    pl.semaphore_wait(barrier, len(devices))


def remote(src, dst, send, recv, device):
    return pltpu.make_async_remote_copy(
        src_ref=src, dst_ref=dst, send_sem=send, recv_sem=recv, device_id=device, device_id_type=MESH
    )


def prior_block(b, base, source, coeffs, offs):
    def pick(offset):
        block = b - base + offset
        if len(source.shape) == 3:
            return source[block]
        return jnp.concatenate([source[0, block], source[1, block]], axis=1)

    left = jnp.concatenate([coeffs[b, 0], coeffs[b, 1], coeffs[b, 2]], axis=1)
    right = jnp.concatenate([pick(0), pick(offs[0, b]), pick(offs[1, b])], axis=0)
    return jnp.dot(left, right, preferred_element_type=F32).astype(BF16)


def split(value):
    upper = value.astype(BF16)
    return upper, (value - upper.astype(F32)).astype(BF16)


def dot_f32(left, right, dims):
    return sum(
        lax.dot_general(left[i], right[j], (dims, ((), ())), preferred_element_type=F32)
        for i, j in ((0, 0), (0, 1), (1, 0))
    )


def all_peers(n_obs, n_par, o, p):
    return [
        (lax.rem(o + i, n_obs), lax.rem(p + j, n_par))
        for j in range(n_par)
        for i in range(n_obs)
        if i or j
    ]


def chip_peers(n_obs, n_par, o, p):
    chips = n_par // 2
    z, core = p // 2, lax.rem(p, 2)
    return [
        (lax.rem(o + i, n_obs), 2 * lax.rem(z + j, chips) + core)
        for j in range(chips)
        for i in range(n_obs)
        if i or j
    ]


def partners(n_obs, o):
    side = o + 1 - 2 * lax.rem(o, 2)
    half = n_obs // 2
    return side, lax.rem(o + half, n_obs), lax.rem(side + half, n_obs)


def quarter(n_obs, o, p):
    y = o // 2
    place = 2 * y + lax.rem(o + y, 2)
    return place + lax.rem(p, 2) * (n_obs - 1 - 2 * place)


def owner(n_obs, q, p):
    place = q + lax.rem(p, 2) * (n_obs - 1 - 2 * q)
    y = place // 2
    return 2 * y + lax.rem(place + y, 2)


def wait_all(ref, sem):
    pltpu.make_async_copy(ref, ref, sem).wait()


def sum_over_par(n_par, o, p, total, part, got, send, recv):
    piece = part.shape[1]
    for q in range(n_par):
        part[q] = total[q * piece : (q + 1) * piece].astype(BF16)
    copies = []
    for d in range(1, n_par):
        q = lax.rem(p + d, n_par)
        copy = remote(part.at[q], got.at[d], send.at[d], recv.at[d], (o, q))
        copy.start()
        copies.append(copy)

    def finish():
        mine = part[p].astype(F32)
        for d in range(1, n_par):
            copies[d - 1].wait()
            mine = mine + got[d].astype(F32)
        return mine

    return finish


def sum_over_obs(n_obs, o, p, jac, forward, adj, got, send, recv, out):
    side, across, far = partners(n_obs, o)
    half = adj.shape[1]
    near = (side, p)
    over = (across, p)
    copies = []

    def product(slot, device, h):
        start = pl.multiple_of((2 * quarter(n_obs, device, p) + h) * half, half)
        value = lax.dot_general(
            jac[:, pl.ds(start, half)], forward(), (((0,), (0,)), ((), ())), preferred_element_type=F32
        )
        adj[slot] = value.astype(BF16)

    def send_slot(slot, device):
        copy = remote(adj.at[slot], got.at[slot], send.at[slot], recv.at[slot], device)
        copy.start()
        copies.append(copy)

    def first():
        product(0, far, 0)
        send_slot(0, near)
        product(1, far, 1)
        send_slot(1, over)

    def second():
        product(2, side, 0)
        send_slot(2, near)
        product(3, across, 1)
        send_slot(3, over)

    def rest():
        product(4, across, 0)
        product(5, side, 1)
        product(6, o, 0)
        product(7, o, 1)

    def third():
        for slot, device in ((0, over), (1, near)):
            copies[slot].wait()
            adj[4 + slot] = (adj[4 + slot].astype(F32) + got[slot].astype(F32)).astype(BF16)
            send_slot(4 + slot, device)

    def finish():
        for h in range(2):
            copies[2 + h].wait()
            copies[4 + h].wait()
            total = adj[6 + h].astype(F32) + got[2 + h].astype(F32) + got[4 + h].astype(F32)
            out[pl.ds(h * half, half), :] = total.astype(BF16)

    return first, second, rest, third, finish


def prepare_bands(offs, coeffs, first, middle, low, high, diagonal):
    blocks = diagonal.shape[0]
    zero = jnp.zeros((BLK, BLK), BF16)
    low[...] = jnp.zeros_like(low)
    high[...] = jnp.zeros_like(high)
    for b in range(blocks):
        diagonal[b] = coeffs[first + b, 0].T
        columns = pl.ds(b * BLK, BLK)
        for j in range(2):
            block = coeffs[first + b, j + 1].T
            offset = offs[j, first + b]
            for c in range(blocks):
                if abs(c - b) > REACH:
                    middle[j, pl.ds(c * BLK, BLK), columns] = zero
            for d in range(-REACH, REACH + 1):
                value = jnp.where(offset == d, block, zero)
                c = b + d
                if c < 0:
                    low[j, pl.ds((c + REACH) * BLK, BLK), columns] = value
                elif c >= blocks:
                    columns_high = pl.ds((b - blocks + REACH) * BLK, BLK)
                    high[j, pl.ds((c - blocks) * BLK, BLK), columns_high] = value
                else:
                    middle[j, pl.ds(c * BLK, BLK), columns] = value


def two_products(bands, values):
    return jnp.dot(bands[0], values, preferred_element_type=F32) + jnp.dot(
        bands[1], values, preferred_element_type=F32
    )


def sum_everywhere(n_obs, n_par, o, p, value, pair_send, pair_got, send, got, out, sems, beside=()):
    beside = list(beside) + [lambda: None] * 2
    core = lax.rem(p, 2)
    other = (o, p + 1 - 2 * core)
    peers = chip_peers(n_obs, n_par, o, p)
    place = (p // 2) * n_obs + o
    count, piece, width = send.shape
    kind = send.dtype
    tall = count * piece
    pair_send[0] = value[:tall].astype(kind)
    pair_send[1] = value[tall:].astype(kind)
    copy = remote(pair_send.at[1 - core], pair_got, sems.at[0], sems.at[1], other)
    copy.start()
    copy.wait()
    mine = pair_send[core].astype(F32) + pair_got[...].astype(F32)
    for j in range(count):
        send[j] = mine[j * piece : (j + 1) * piece].astype(kind)
    for d, device in enumerate(peers, 1):
        target = (device[1] // 2) * n_obs + device[0]
        remote(send.at[target], got.at[d], sems.at[2], sems.at[3], device).start()
    beside[0]()
    mine = send[place].astype(F32)
    rest = got.at[pl.ds(1, count - 1)]
    wait_all(rest, sems.at[2])
    wait_all(rest, sems.at[3])
    for d in range(1, count):
        mine = mine + got[d].astype(F32)
    out[core, place] = mine.astype(kind)
    for device in peers:
        remote(out.at[core, place], out.at[core, place], sems.at[4], sems.at[5], device).start()
    beside[1]()
    wait_all(rest, sems.at[4])
    wait_all(rest, sems.at[5])
    copy = remote(out.at[core], out.at[core], sems.at[6], sems.at[7], other)
    copy.start()
    copy.wait()
    return jnp.concatenate([out[c, j].astype(F32) for c in range(2) for j in range(count)], axis=0)


def sum_directly(n_obs, n_par, o, p, value, send, got, out, sems, beside=()):
    peers = all_peers(n_obs, n_par, o, p)
    place = p * n_obs + o
    count, piece, width = send.shape
    kind = send.dtype
    for j in range(count):
        send[j] = value[j * piece : (j + 1) * piece].astype(kind)
    for d, (i, q) in enumerate(peers, 1):
        remote(send.at[q * n_obs + i], got.at[d], sems.at[0], sems.at[1], (i, q)).start()
    beside[0]()
    mine = send[place].astype(F32)
    rest = got.at[pl.ds(1, count - 1)]
    wait_all(rest, sems.at[0])
    wait_all(rest, sems.at[1])
    for d in range(1, count):
        mine = mine + got[d].astype(F32)
    out[place] = mine.astype(kind)
    for device in peers:
        remote(out.at[place], out.at[place], sems.at[2], sems.at[3], device).start()
    beside[1]()
    wait_all(rest, sems.at[2])
    wait_all(rest, sems.at[3])
    return jnp.concatenate([out[j].astype(F32) for j in range(count)], axis=0)


def few_devices(n_obs, n_par, width):
    return width // (n_obs * n_par) >= 8


def sum_scratch(n_obs, n_par, width, kind):
    count = n_obs * n_par // 2
    piece = width // 2 // count
    if kind == BF16 and few_devices(n_obs, n_par, width):
        return [pltpu.VMEM((2 * count, piece, width), kind)] * 3 + [dma(4)]
    return [
        pltpu.VMEM((2, width // 2, width), kind),
        pltpu.VMEM((width // 2, width), kind),
        pltpu.VMEM((count, piece, width), kind),
        pltpu.VMEM((count, piece, width), kind),
        pltpu.VMEM((2, count, piece, width), kind),
        dma(8),
    ]


def small_inverse_factor(matrix):
    size = matrix.shape[0]
    row = lax.broadcasted_iota(jnp.int32, (size, size), 0)
    lane = lax.broadcasted_iota(jnp.int32, (size, size), 1)
    work = jnp.concatenate([matrix, (row == lane).astype(F32)], axis=1)
    group = 8
    parts = [work[g : g + group] for g in range(0, size, group)]
    index = lax.broadcasted_iota(jnp.int32, (group, 2 * size), 0)
    scales = []
    for first in range(size // group):
        start = first * group
        columns = [
            [jnp.broadcast_to(part[:, start + t : start + t + 1], part.shape) for part in parts[first:]]
            for t in range(group)
        ]
        for t in range(group):
            pivot = columns[t][0][t : t + 1]
            scales.append(lax.rsqrt(pivot))
            reciprocal = 1.0 / pivot
            scaled = parts[first][t : t + 1] * reciprocal
            columns[t][0] = jnp.where(index > t, columns[t][0], 0.0)
            for u in range(t + 1, group):
                ratio = columns[u][0][t : t + 1] * reciprocal
                columns[u] = [c - e * ratio for c, e in zip(columns[u], columns[t])]
            for g, column in enumerate(columns[t]):
                parts[first + g] = parts[first + g] - column * scaled
    rows = [parts[j // group][j % group : j % group + 1] * scales[j] for j in range(size)]
    return jnp.concatenate(rows, axis=0)[:, size:]


def inverse_factor_steps(gram, work, out, size):
    blocks = work.shape[0]
    width = blocks * size
    row = lax.broadcasted_iota(jnp.int32, (size, width), 0)
    lane = lax.broadcasted_iota(jnp.int32, (size, width), 1)
    for k in range(blocks):
        work[k, :, pl.ds(0, width)] = gram[k * size : (k + 1) * size]
        work[k, :, pl.ds(width, width)] = (lane == row + k * size).astype(F32)

    def step(k, carry):
        rows = work[k]
        shift = lax.rem(width - k * size, width)
        diagonal = pltpu.roll(rows[:, :width], shift, 1)[:, :size]
        small = small_inverse_factor(diagonal)
        upper = dot_f32(split(small), split(rows), ((1,), (0,)))
        out[k] = upper[:, width:]
        left = jnp.where(lane >= (k + 1) * size, upper[:, :width], 0.0)
        update = dot_f32(split(left), split(upper), ((0,), (0,)))
        for i in range(blocks):
            work[i] -= update[i * size : (i + 1) * size]
        return carry

    return blocks, step


def gather_over_obs(n_obs, o, p, ext, send, recv):
    side, across, _ = partners(n_obs, o)
    near, over = (side, p), (across, p)
    blocks = ext.shape[0] // (2 * n_obs)
    order = [
        [(o, 0, near), (o, 1, over)],
        [(o, 1, near), (o, 0, over)],
        [(side, 0, over), (across, 1, near)],
    ]
    copies = []

    def stage(i):
        for j, (source, h, device) in enumerate(order[i]):
            if i == 2:
                copies[j].wait()
            start = (2 * quarter(n_obs, source, p) + h) * blocks
            ref = ext.at[pl.ds(start, blocks)]
            slot = 2 * i + j
            copy = remote(ref, ref, send.at[slot], recv.at[slot], device)
            copy.start()
            copies.append(copy)

    def finish():
        for copy in copies[2:]:
            copy.wait()

    return stage, finish


def swap_sides(at_start, at_end, low_copy, high_copy):
    def start():
        @pl.when(at_start)
        def _():
            low_copy.start()

        @pl.when(at_end)
        def _():
            high_copy.start()

    def finish(low_arrived=None, high_arrived=None):
        @pl.when(at_start)
        def _():
            low_copy.wait_send()
            high_copy.wait_recv()
            if low_arrived is not None:
                low_arrived()

        @pl.when(at_end)
        def _():
            high_copy.wait_send()
            low_copy.wait_recv()
            if high_arrived is not None:
                high_arrived()

    return start, finish


def main_kernel(
    n_obs, n_par, offs, probes, coeffs, jac_ref, basis_out, image_out, ritz,
    low0, low1, high0, high1, values, held, jac, ls, image, part, got, fwd, adj, adj_got, own, ph, par, rs,
    bands, bands_low, bands_high, diagonal, sample, lower, upper, from_low, from_high, hs,
    low2, high2, fine, ext, ags, work, inverse, part2, got2, par2, basis, mapped, ws, *rest,
):
    o, p = lax.axis_index("obs"), lax.axis_index("par")
    q = quarter(n_obs, o, p)
    count = n_obs * n_par
    order = p * n_obs + q
    rows, width = image.shape
    half = width // 2
    total_blocks = rows // BLK
    blocks = total_blocks // n_obs
    side_blocks = 2 * REACH
    below = (o, lax.rem(p + n_par - 1, n_par))
    above = (o, lax.rem(p + 1, n_par))
    first_sum, second_sum = rest[:6], rest[6:]
    loads = [
        pltpu.make_async_copy(probes, values, ls.at[0]),
        pltpu.make_async_copy(coeffs, held, ls.at[1]),
        pltpu.make_async_copy(jac_ref, jac, ls.at[2]),
    ]
    low, high = [low0, low1], [high0, high1]
    halves = [slice(0, half), slice(half, width)]

    def probe_blocks(start, size, k):
        return values.at[pl.ds(start, size), :, pl.ds(k * half, half)]

    sides = []
    for k in range(2):
        sides.append(
            pltpu.make_async_copy(
                probe_blocks(0, side_blocks, k), low[k].at[pl.ds(REACH, side_blocks)], ls.at[3 + k]
            )
        )
        sides.append(
            pltpu.make_async_copy(
                probe_blocks(total_blocks - side_blocks, side_blocks, k),
                high[k].at[pl.ds(0, side_blocks)],
                ls.at[5 + k],
            )
        )
    for load in loads:
        load.start()
    greet(all_peers(n_obs, n_par, o, p))
    loads[0].wait()
    end = rows - HALO
    edges = []
    for k in range(2):
        start, finish_sides = swap_sides(
            p > 0,
            p < n_par - 1,
            remote(
                probe_blocks(0, REACH, k), high[k].at[pl.ds(side_blocks, REACH)], ph.at[k, 0], ph.at[k, 1], below
            ),
            remote(
                probe_blocks(total_blocks - REACH, REACH, k), low[k].at[pl.ds(0, REACH)],
                ph.at[k, 2], ph.at[k, 3], above,
            ),
        )
        start()
        edges.append(finish_sides)
    for side in sides:
        side.start()

    @pl.when(p == 0)
    def _():
        for ref in low:
            ref[pl.ds(0, REACH)] = jnp.zeros((REACH,) + ref.shape[1:], BF16)
        low2[:, pl.ds(0, REACH)] = jnp.zeros((2, REACH) + ext.shape[2:], BF16)

    @pl.when(p == n_par - 1)
    def _():
        for ref in high:
            ref[pl.ds(side_blocks, REACH)] = jnp.zeros((REACH,) + ref.shape[1:], BF16)
        high2[:, pl.ds(side_blocks, REACH)] = jnp.zeros((2, REACH) + ext.shape[2:], BF16)

    loads[1].wait()

    def inner(b, carry):
        image[pl.ds(pl.multiple_of(b * BLK, BLK), BLK), :] = prior_block(b, 0, values, held, offs)
        return carry

    lax.fori_loop(REACH, total_blocks - REACH, inner, 0, unroll=4)
    loads[2].wait()
    totals = [
        jnp.dot(jac[:, HALO:end], image[HALO:end, columns], preferred_element_type=F32) for columns in halves
    ]
    for side in sides:
        side.wait()
    sums = []
    for k, columns in enumerate(halves):
        edges[k]()
        for b in range(REACH):
            image[pl.ds(b * BLK, BLK), columns] = prior_block(b, -REACH, low[k], held, offs)
        for b in range(total_blocks - REACH, total_blocks):
            image[pl.ds(b * BLK, BLK), columns] = prior_block(
                b, total_blocks - 2 * REACH, high[k], held, offs
            )
        total = totals[k]
        total = total + jnp.dot(jac[:, :HALO], image[:HALO, columns], preferred_element_type=F32)
        total = total + jnp.dot(jac[:, end:], image[end:, columns], preferred_element_type=F32)
        sums.append(sum_over_par(n_par, o, p, total, part.at[k], got.at[k], par.at[k, 0], par.at[k, 1]))
    gathers = []
    for k in range(2):
        fwd[k, p] = sums[k]().astype(BF16)
        mine = fwd.at[k, p]
        copies = []
        for d in range(1, n_par):
            copy = remote(mine, mine, par.at[k, 2, d], par.at[k, 3, d], (o, lax.rem(p + d, n_par)))
            copy.start()
            copies.append(copy)
        gathers.append(copies)

    def reduce_half(k):
        def forward():
            return fwd[k].reshape(jac.shape[0], half)

        return sum_over_obs(
            n_obs, o, p, jac, forward, adj.at[k], adj_got.at[k], rs.at[k, 0], rs.at[k, 1], own.at[k]
        )

    reduce0, reduce1 = reduce_half(0), reduce_half(1)
    for copy in gathers[0]:
        copy.wait()
    reduce0[0]()
    reduce0[1]()
    for copy in gathers[1]:
        copy.wait()
    reduce1[0]()
    reduce0[2]()
    reduce0[3]()
    reduce1[1]()
    reduce1[2]()
    prepare_bands(offs, held, q * blocks, bands, bands_low, bands_high, diagonal)
    reduce1[3]()
    before = lax.rem(order + count - 1, count)
    after = lax.rem(order + 1, count)
    down_device = (owner(n_obs, lax.rem(before, n_obs), before // n_obs), before // n_obs)
    up_device = (owner(n_obs, lax.rem(after, n_obs), after // n_obs), after // n_obs)
    swaps = []

    def prior(k):
        lower[k] = two_products(bands_low, own[k, :HALO, :]).astype(BF16)
        upper[k] = two_products(bands_high, own[k, pl.ds(blocks * BLK - HALO, HALO), :]).astype(BF16)
        start, finish_sides = swap_sides(
            order > 0,
            order < count - 1,
            remote(lower.at[k], from_high.at[k], hs.at[k, 0], hs.at[k, 1], down_device),
            remote(upper.at[k], from_low.at[k], hs.at[k, 2], hs.at[k, 3], up_device),
        )
        start()
        swaps.append(finish_sides)
        sample[:, halves[k]] = two_products(bands, own[k])
        for b in range(blocks):
            here = pl.ds(b * BLK, BLK)
            sample[here, halves[k]] += jnp.dot(diagonal[b], own[k, here, :], preferred_element_type=F32)

    def prior_end(k):
        def low_arrived():
            sample[pl.ds(0, HALO), halves[k]] += from_low[k].astype(F32)

        def high_arrived():
            sample[pl.ds(blocks * BLK - HALO, HALO), halves[k]] += from_high[k].astype(F32)

        swaps[k](low_arrived, high_arrived)
        parts = split(sample[:, halves[k]])
        ext[k, pl.ds(q * blocks, blocks)] = parts[0].reshape(blocks, BLK, half)
        fine[k] = parts[1]

    reduce0[4]()
    prior(0)
    reduce1[4]()
    prior(1)
    prior_end(0)
    stage0, finish0 = gather_over_obs(n_obs, o, p, ext.at[0], ags.at[0, 0], ags.at[0, 1])
    stage1, finish1 = gather_over_obs(n_obs, o, p, ext.at[1], ags.at[1, 0], ags.at[1, 1])
    stage0(0)
    stage0(1)
    coarse = [ext.at[k, pl.ds(q * blocks, blocks)] for k in range(2)]

    def cross(i, j):
        left = coarse[i][...].reshape(fine.shape[1:]), fine[i]
        right = coarse[j][...].reshape(fine.shape[1:]), fine[j]
        both = jnp.concatenate(right, axis=1)
        over_rows = (((0,), (0,)), ((), ()))
        value = lax.dot_general(left[0], both, over_rows, preferred_element_type=F32)
        if i == j:
            other = value[:, half:].T
        else:
            other = lax.dot_general(left[1], right[0], over_rows, preferred_element_type=F32)
        return value[:, :half] + value[:, half:] + other

    first_block = cross(0, 0)
    prior_end(1)
    off_block = cross(1, 0)
    value = jnp.concatenate(
        [
            jnp.concatenate([first_block, off_block.T], axis=1),
            jnp.concatenate([off_block, cross(1, 1)], axis=1),
        ],
        axis=0,
    ) / (sample.shape[0] * count)

    def more0():
        stage0(2)
        stage1(0)

    def more1():
        stage1(1)
        stage1(2)

    matrix = sum_everywhere(n_obs, n_par, o, p, value, *first_sum, [more0, more1])
    last = total_blocks - REACH

    def sample_edges(k):
        return swap_sides(
            p > 0,
            p < n_par - 1,
            remote(
                ext.at[k, pl.ds(0, REACH)], high2.at[k, pl.ds(side_blocks, REACH)],
                hs.at[2 + k, 0], hs.at[2 + k, 1], below,
            ),
            remote(
                ext.at[k, pl.ds(last, REACH)], low2.at[k, pl.ds(0, REACH)], hs.at[2 + k, 2], hs.at[2 + k, 3], above
            ),
        )

    finish0()
    start, finish_sides0 = sample_edges(0)
    start()
    steps, step = inverse_factor_steps(matrix, work, inverse, inverse.shape[1])
    lax.fori_loop(0, 1, step, 0)
    finish1()
    start, finish_sides1 = sample_edges(1)
    start()
    sides = [
        pltpu.make_async_copy(
            ext.at[:, pl.ds(0, side_blocks)], low2.at[:, pl.ds(REACH, side_blocks)], ls.at[3]
        ),
        pltpu.make_async_copy(
            ext.at[:, pl.ds(total_blocks - side_blocks, side_blocks)], high2.at[:, pl.ds(0, side_blocks)],
            ls.at[4],
        ),
    ]
    for side in sides:
        side.start()

    def outer(b, carry):
        image[pl.ds(pl.multiple_of(b * BLK, BLK), BLK), :] = prior_block(b, 0, ext, held, offs)
        return carry

    lax.fori_loop(REACH, last, outer, 0, unroll=4)
    total = jnp.dot(jac[:, HALO:end], image[HALO:end, :], preferred_element_type=F32)
    finish_sides0()
    finish_sides1()
    for side in sides:
        side.wait()
    for b in range(REACH):
        image[pl.ds(b * BLK, BLK), :] = prior_block(b, -REACH, low2, held, offs)
    for b in range(last, total_blocks):
        image[pl.ds(b * BLK, BLK), :] = prior_block(b, total_blocks - 2 * REACH, high2, held, offs)
    total = total + jnp.dot(jac[:, :HALO], image[:HALO, :], preferred_element_type=F32)
    total = total + jnp.dot(jac[:, end:], image[end:, :], preferred_element_type=F32)
    finish_sum = sum_over_par(n_par, o, p, total, part2, got2, par2.at[0], par2.at[1])
    lax.fori_loop(1, steps, step, 0)
    mine = finish_sum()
    factor = split(inverse[...].reshape(width, width))
    mine = split(dot_f32(split(mine), factor, ((1,), (1,))))
    value = dot_f32(mine, mine, ((0,), (0,))) / (jac.shape[0] * n_obs)

    def solve(value):
        last = (((1,), (1,)), ((), ()))
        return (
            lax.dot_general(value, factor[0], last, preferred_element_type=F32)
            + lax.dot_general(value, factor[1], last, preferred_element_type=F32)
        ).astype(BF16)

    tall = min(512, rows)

    def solve_basis():
        def tile(t, carry):
            here = pl.ds(t * (tall // BLK), tall // BLK)
            value = jnp.concatenate([ext[k, here].reshape(tall, half) for k in range(2)], axis=1)
            basis[pl.ds(pl.multiple_of(t * tall, tall), tall), :] = solve(value)
            return carry

        lax.fori_loop(0, rows // tall, tile, 0)
        pltpu.make_async_copy(basis, basis_out, ws.at[0]).start()

    def solve_image():
        def tile(t, carry):
            here = pl.ds(pl.multiple_of(t * tall, tall), tall)
            mapped[here, :] = solve(image[here, :])
            return carry

        lax.fori_loop(0, rows // tall, tile, 0)
        pltpu.make_async_copy(mapped, image_out, ws.at[1]).start()

    add = sum_directly if few_devices(n_obs, n_par, width) else sum_everywhere
    ritz[...] = add(n_obs, n_par, o, p, value, *second_sum, [solve_basis, solve_image])
    pltpu.make_async_copy(basis, basis_out, ws.at[0]).wait()
    pltpu.make_async_copy(mapped, image_out, ws.at[1]).wait()


def write_kernel(*refs):
    count = len(refs) // 2
    copies = [pltpu.make_async_copy(refs[i], refs[count + i], refs[-1].at[i]) for i in range(count)]
    for copy in copies:
        copy.start()
    for copy in copies:
        copy.wait()


def dma(*count):
    return pltpu.SemaphoreType.DMA(count)


def body(n_obs, n_par, jacobian, probes, coeffs, offsets):
    obs, rows = jacobian.shape
    width = probes.shape[1]
    half = width // 2
    own = rows // n_obs
    total_blocks = rows // BLK
    block = 64
    hbm = pl.BlockSpec(memory_space=pltpu.HBM)
    anywhere = pl.BlockSpec(memory_space=pl.ANY)
    piece = obs // n_par
    shapes = [
        jax.ShapeDtypeStruct((rows, width), BF16),
        jax.ShapeDtypeStruct((rows, width), BF16),
        jax.ShapeDtypeStruct((width, width), F32),
    ]
    results = pl.pallas_call(
        functools.partial(main_kernel, n_obs, n_par),
        out_shape=shapes,
        in_specs=[SMEM, hbm, hbm, hbm],
        out_specs=[anywhere, anywhere, VMEM],
        scratch_shapes=[pltpu.VMEM((3 * REACH, BLK, half), BF16)] * 4
        + [
            pltpu.VMEM((total_blocks, BLK, width), BF16),
            pltpu.VMEM(coeffs.shape, BF16),
            pltpu.VMEM((obs, rows), BF16),
            dma(7),
            pltpu.VMEM((rows, width), BF16),
        ]
        + [pltpu.VMEM((2, n_par, piece, half), BF16)] * 3
        + [
            pltpu.VMEM((2, 8, own // 2, half), BF16),
            pltpu.VMEM((2, 6, own // 2, half), BF16),
            pltpu.VMEM((2, own, half), BF16),
            dma(2, 4),
            dma(2, 4, n_par),
            dma(2, 2, 6),
            pltpu.VMEM((2, own, own), BF16),
            pltpu.VMEM((2, HALO, HALO), BF16),
            pltpu.VMEM((2, HALO, HALO), BF16),
            pltpu.VMEM((own // BLK, BLK, BLK), BF16),
            pltpu.VMEM((own, width), F32),
        ]
        + [pltpu.VMEM((2, HALO, half), BF16)] * 4
        + [
            dma(4, 4),
            pltpu.VMEM((2, 3 * REACH, BLK, half), BF16),
            pltpu.VMEM((2, 3 * REACH, BLK, half), BF16),
            pltpu.VMEM((2, own, half), BF16),
            pltpu.VMEM((2, total_blocks, BLK, half), BF16),
            dma(2, 2, 6),
            pltpu.VMEM((width // block, block, 2 * width), F32),
            pltpu.VMEM((width // block, block, width), F32),
        ]
        + [pltpu.VMEM((n_par, piece, width), BF16)] * 2
        + [dma(2, n_par)]
        + [pltpu.VMEM((rows, width), BF16)] * 2
        + [dma(2)]
        + sum_scratch(n_obs, n_par, width, F32)
        + sum_scratch(n_obs, n_par, width, BF16),
        compiler_params=pltpu.CompilerParams(
            collective_id=0, has_side_effects=True, vmem_limit_bytes=LIMIT
        ),
        name="main",
    )(offsets.T, probes.reshape(-1, BLK, width), coeffs, jacobian)
    return pl.pallas_call(
        write_kernel,
        out_shape=shapes,
        in_specs=[anywhere] * 3,
        out_specs=[hbm] * 3,
        scratch_shapes=[dma(3)],
        compiler_params=pltpu.CompilerParams(vmem_limit_bytes=1024 * 1024),
        name="write",
    )(*results)


def solution(mesh):
    return jax.shard_map(
        functools.partial(body, mesh.shape["obs"], mesh.shape["par"]),
        mesh=mesh,
        in_specs=(P("obs", "par"), P("par", None), P("par", None, None, None), P("par", None)),
        out_specs=(P("par", None), P("par", None), P()),
        check_vma=False,
    )
```

```python
import functools

import jax
import jax.numpy as jnp
from jax import lax
from jax.experimental import pallas as pl
from jax.experimental.pallas import tpu as pltpu
from jax.sharding import PartitionSpec as P

BLK = 128
REACH = 4
HALO = REACH * BLK
MESH = pl.DeviceIdType.MESH
F32 = jnp.float32
BF16 = jnp.bfloat16
VMEM = pl.BlockSpec(memory_space=pltpu.VMEM)
SMEM = pl.BlockSpec(memory_space=pltpu.SMEM)
LIMIT = 48 * 1024 * 1024


def greet(devices):
    barrier = pltpu.get_barrier_semaphore()
    for device in devices:
        pl.semaphore_signal(barrier, inc=1, device_id=device, device_id_type=MESH)
    pl.semaphore_wait(barrier, len(devices))


def remote(src, dst, send, recv, device):
    return pltpu.make_async_remote_copy(
        src_ref=src, dst_ref=dst, send_sem=send, recv_sem=recv, device_id=device, device_id_type=MESH
    )


def prior_block(b, base, source, coeffs, offs):
    def pick(offset):
        block = b - base + offset
        if len(source.shape) == 3:
            return source[block]
        return jnp.concatenate([source[0, block], source[1, block]], axis=1)

    left = jnp.concatenate([coeffs[b, 0], coeffs[b, 1], coeffs[b, 2]], axis=1)
    right = jnp.concatenate([pick(0), pick(offs[0, b]), pick(offs[1, b])], axis=0)
    return jnp.dot(left, right, preferred_element_type=F32).astype(BF16)


def split(value):
    upper = value.astype(BF16)
    return upper, (value - upper.astype(F32)).astype(BF16)


def dot_f32(left, right, dims):
    return sum(
        lax.dot_general(left[i], right[j], (dims, ((), ())), preferred_element_type=F32)
        for i, j in ((0, 0), (0, 1), (1, 0))
    )


def all_peers(n_obs, n_par, o, p):
    return [
        (lax.rem(o + i, n_obs), lax.rem(p + j, n_par))
        for j in range(n_par)
        for i in range(n_obs)
        if i or j
    ]


def chip_peers(n_obs, n_par, o, p):
    chips = n_par // 2
    z, core = p // 2, lax.rem(p, 2)
    return [
        (lax.rem(o + i, n_obs), 2 * lax.rem(z + j, chips) + core)
        for j in range(chips)
        for i in range(n_obs)
        if i or j
    ]


def partners(n_obs, o):
    side = o + 1 - 2 * lax.rem(o, 2)
    half = n_obs // 2
    return side, lax.rem(o + half, n_obs), lax.rem(side + half, n_obs)


def quarter(n_obs, o, p):
    y = o // 2
    place = 2 * y + lax.rem(o + y, 2)
    return place + lax.rem(p, 2) * (n_obs - 1 - 2 * place)


def owner(n_obs, q, p):
    place = q + lax.rem(p, 2) * (n_obs - 1 - 2 * q)
    y = place // 2
    return 2 * y + lax.rem(place + y, 2)


def wait_all(ref, sem):
    pltpu.make_async_copy(ref, ref, sem).wait()


def sum_over_par(n_par, o, p, total, part, got, send, recv):
    piece = part.shape[1]
    for q in range(n_par):
        part[q] = total[q * piece : (q + 1) * piece].astype(BF16)
    copies = []
    for d in range(1, n_par):
        q = lax.rem(p + d, n_par)
        copy = remote(part.at[q], got.at[d], send.at[d], recv.at[d], (o, q))
        copy.start()
        copies.append(copy)

    def finish():
        mine = part[p].astype(F32)
        for d in range(1, n_par):
            copies[d - 1].wait()
            mine = mine + got[d].astype(F32)
        return mine

    return finish


def sum_over_obs(n_obs, o, p, jac, forward, adj, got, send, recv, out):
    side, across, far = partners(n_obs, o)
    half = adj.shape[1]
    near = (side, p)
    over = (across, p)
    copies = []

    def product(slot, device, h):
        start = pl.multiple_of((2 * quarter(n_obs, device, p) + h) * half, half)
        value = lax.dot_general(
            jac[:, pl.ds(start, half)], forward(), (((0,), (0,)), ((), ())), preferred_element_type=F32
        )
        adj[slot] = value.astype(BF16)

    def send_slot(slot, device):
        copy = remote(adj.at[slot], got.at[slot], send.at[slot], recv.at[slot], device)
        copy.start()
        copies.append(copy)

    def first():
        product(0, far, 0)
        send_slot(0, near)
        product(1, far, 1)
        send_slot(1, over)

    def second():
        product(2, side, 0)
        send_slot(2, near)
        product(3, across, 1)
        send_slot(3, over)

    def rest():
        product(4, across, 0)
        product(5, side, 1)
        product(6, o, 0)
        product(7, o, 1)

    def third():
        for slot, device in ((0, over), (1, near)):
            copies[slot].wait()
            adj[4 + slot] = (adj[4 + slot].astype(F32) + got[slot].astype(F32)).astype(BF16)
            send_slot(4 + slot, device)

    def finish():
        for h in range(2):
            copies[2 + h].wait()
            copies[4 + h].wait()
            total = adj[6 + h].astype(F32) + got[2 + h].astype(F32) + got[4 + h].astype(F32)
            out[pl.ds(h * half, half), :] = total.astype(BF16)

    return first, second, rest, third, finish


def prepare_bands(offs, coeffs, first, middle, low, high, diagonal):
    blocks = diagonal.shape[0]
    zero = jnp.zeros((BLK, BLK), BF16)
    low[...] = jnp.zeros_like(low)
    high[...] = jnp.zeros_like(high)
    for b in range(blocks):
        diagonal[b] = coeffs[first + b, 0].T
        columns = pl.ds(b * BLK, BLK)
        for j in range(2):
            block = coeffs[first + b, j + 1].T
            offset = offs[j, first + b]
            for c in range(blocks):
                if abs(c - b) > REACH:
                    middle[j, pl.ds(c * BLK, BLK), columns] = zero
            for d in range(-REACH, REACH + 1):
                value = jnp.where(offset == d, block, zero)
                c = b + d
                if c < 0:
                    low[j, pl.ds((c + REACH) * BLK, BLK), columns] = value
                elif c >= blocks:
                    columns_high = pl.ds((b - blocks + REACH) * BLK, BLK)
                    high[j, pl.ds((c - blocks) * BLK, BLK), columns_high] = value
                else:
                    middle[j, pl.ds(c * BLK, BLK), columns] = value


def two_products(bands, values):
    return jnp.dot(bands[0], values, preferred_element_type=F32) + jnp.dot(
        bands[1], values, preferred_element_type=F32
    )


def sum_everywhere(n_obs, n_par, o, p, value, pair_send, pair_got, send, got, out, sems, beside=()):
    beside = list(beside) + [lambda: None] * 2
    core = lax.rem(p, 2)
    other = (o, p + 1 - 2 * core)
    peers = chip_peers(n_obs, n_par, o, p)
    place = (p // 2) * n_obs + o
    count, piece, width = send.shape
    kind = send.dtype
    tall = count * piece
    pair_send[0] = value[:tall].astype(kind)
    pair_send[1] = value[tall:].astype(kind)
    copy = remote(pair_send.at[1 - core], pair_got, sems.at[0], sems.at[1], other)
    copy.start()
    copy.wait()
    mine = pair_send[core].astype(F32) + pair_got[...].astype(F32)
    for j in range(count):
        send[j] = mine[j * piece : (j + 1) * piece].astype(kind)
    for d, device in enumerate(peers, 1):
        target = (device[1] // 2) * n_obs + device[0]
        remote(send.at[target], got.at[d], sems.at[2], sems.at[3], device).start()
    beside[0]()
    mine = send[place].astype(F32)
    rest = got.at[pl.ds(1, count - 1)]
    wait_all(rest, sems.at[2])
    wait_all(rest, sems.at[3])
    for d in range(1, count):
        mine = mine + got[d].astype(F32)
    out[core, place] = mine.astype(kind)
    for device in peers:
        remote(out.at[core, place], out.at[core, place], sems.at[4], sems.at[5], device).start()
    beside[1]()
    wait_all(rest, sems.at[4])
    wait_all(rest, sems.at[5])
    copy = remote(out.at[core], out.at[core], sems.at[6], sems.at[7], other)
    copy.start()
    copy.wait()
    return jnp.concatenate([out[c, j].astype(F32) for c in range(2) for j in range(count)], axis=0)


def sum_directly(n_obs, n_par, o, p, value, send, got, out, sems, beside=()):
    peers = all_peers(n_obs, n_par, o, p)
    place = p * n_obs + o
    count, tall, half = send.shape
    piece = tall // 2
    kind = send.dtype
    for j in range(count):
        rows = value[j * piece : (j + 1) * piece]
        send[j] = jnp.concatenate([rows[:, :half], rows[:, half:]], axis=0).astype(kind)
    for d, (i, q) in enumerate(peers, 1):
        remote(send.at[q * n_obs + i], got.at[d], sems.at[0], sems.at[1], (i, q)).start()
    beside[0]()
    mine = send[place].astype(F32)
    rest = got.at[pl.ds(1, count - 1)]
    wait_all(rest, sems.at[0])
    wait_all(rest, sems.at[1])
    for d in range(1, count):
        mine = mine + got[d].astype(F32)
    out[place] = mine.astype(kind)
    for device in peers:
        remote(out.at[place], out.at[place], sems.at[2], sems.at[3], device).start()
    beside[1]()
    wait_all(rest, sems.at[2])
    wait_all(rest, sems.at[3])
    sums = [out[j].astype(F32) for j in range(count)]
    return jnp.concatenate([jnp.concatenate([rows[:piece], rows[piece:]], axis=1) for rows in sums], axis=0)


def few_devices(n_obs, n_par, width):
    return width // (n_obs * n_par) >= 8


def sum_scratch(n_obs, n_par, width, kind):
    count = n_obs * n_par // 2
    piece = width // 2 // count
    if kind == BF16 and few_devices(n_obs, n_par, width):
        return [pltpu.VMEM((2 * count, 2 * piece, width // 2), kind)] * 3 + [dma(4)]
    return [
        pltpu.VMEM((2, width // 2, width), kind),
        pltpu.VMEM((width // 2, width), kind),
        pltpu.VMEM((count, piece, width), kind),
        pltpu.VMEM((count, piece, width), kind),
        pltpu.VMEM((2, count, piece, width), kind),
        dma(8),
    ]


def small_inverse_factor(matrix):
    size = matrix.shape[0]
    row = lax.broadcasted_iota(jnp.int32, (size, size), 0)
    lane = lax.broadcasted_iota(jnp.int32, (size, size), 1)
    work = jnp.concatenate([matrix, (row == lane).astype(F32)], axis=1)
    group = 8
    parts = [work[g : g + group] for g in range(0, size, group)]
    index = lax.broadcasted_iota(jnp.int32, (group, 2 * size), 0)
    scales = []
    for first in range(size // group):
        start = first * group
        columns = [
            [jnp.broadcast_to(part[:, start + t : start + t + 1], part.shape) for part in parts[first:]]
            for t in range(group)
        ]
        for t in range(group):
            pivot = columns[t][0][t : t + 1]
            scales.append(lax.rsqrt(pivot))
            reciprocal = 1.0 / pivot
            scaled = parts[first][t : t + 1] * reciprocal
            columns[t][0] = jnp.where(index > t, columns[t][0], 0.0)
            for u in range(t + 1, group):
                ratio = columns[u][0][t : t + 1] * reciprocal
                columns[u] = [c - e * ratio for c, e in zip(columns[u], columns[t])]
            for g, column in enumerate(columns[t]):
                parts[first + g] = parts[first + g] - column * scaled
    rows = [parts[j // group][j % group : j % group + 1] * scales[j] for j in range(size)]
    return jnp.concatenate(rows, axis=0)[:, size:]


def inverse_factor_steps(gram, work, out, size):
    blocks = work.shape[0]
    width = blocks * size
    row = lax.broadcasted_iota(jnp.int32, (size, width), 0)
    lane = lax.broadcasted_iota(jnp.int32, (size, width), 1)
    for k in range(blocks):
        work[k, :, pl.ds(0, width)] = gram[k * size : (k + 1) * size]
        work[k, :, pl.ds(width, width)] = (lane == row + k * size).astype(F32)

    def step(k, carry):
        rows = work[k]
        shift = lax.rem(width - k * size, width)
        diagonal = pltpu.roll(rows[:, :width], shift, 1)[:, :size]
        small = small_inverse_factor(diagonal)
        upper = dot_f32(split(small), split(rows), ((1,), (0,)))
        out[k] = upper[:, width:]
        left = jnp.where(lane >= (k + 1) * size, upper[:, :width], 0.0)
        update = dot_f32(split(left), split(upper), ((0,), (0,)))
        for i in range(blocks):
            work[i] -= update[i * size : (i + 1) * size]
        return carry

    return blocks, step


def gather_over_obs(n_obs, o, p, ext, send, recv):
    side, across, _ = partners(n_obs, o)
    near, over = (side, p), (across, p)
    blocks = ext.shape[0] // (2 * n_obs)
    order = [
        [(o, 0, near), (o, 1, over)],
        [(o, 1, near), (o, 0, over)],
        [(side, 0, over), (across, 1, near)],
    ]
    copies = []

    def stage(i):
        for j, (source, h, device) in enumerate(order[i]):
            if i == 2:
                copies[j].wait()
            start = (2 * quarter(n_obs, source, p) + h) * blocks
            ref = ext.at[pl.ds(start, blocks)]
            slot = 2 * i + j
            copy = remote(ref, ref, send.at[slot], recv.at[slot], device)
            copy.start()
            copies.append(copy)

    def finish():
        for copy in copies[2:]:
            copy.wait()

    return stage, finish


def swap_sides(at_start, at_end, low_copy, high_copy):
    def start():
        @pl.when(at_start)
        def _():
            low_copy.start()

        @pl.when(at_end)
        def _():
            high_copy.start()

    def finish(low_arrived=None, high_arrived=None):
        @pl.when(at_start)
        def _():
            low_copy.wait_send()
            high_copy.wait_recv()
            if low_arrived is not None:
                low_arrived()

        @pl.when(at_end)
        def _():
            high_copy.wait_send()
            low_copy.wait_recv()
            if high_arrived is not None:
                high_arrived()

    return start, finish


def main_kernel(
    n_obs, n_par, offs, probes, coeffs, jac_ref, basis_out, image_out, ritz,
    low0, low1, high0, high1, values, held, jac, ls, image, part, got, fwd, adj, adj_got, own, ph, par, rs,
    bands, bands_low, bands_high, diagonal, sample, lower, upper, from_low, from_high, hs,
    low2, high2, fine, ext, ags, work, inverse, part2, got2, par2, basis, mapped, ws, *rest,
):
    o, p = lax.axis_index("obs"), lax.axis_index("par")
    q = quarter(n_obs, o, p)
    count = n_obs * n_par
    order = p * n_obs + q
    rows, width = image.shape
    half = width // 2
    total_blocks = rows // BLK
    blocks = total_blocks // n_obs
    side_blocks = 2 * REACH
    below = (o, lax.rem(p + n_par - 1, n_par))
    above = (o, lax.rem(p + 1, n_par))
    first_sum, second_sum = rest[:6], rest[6:]
    loads = [
        pltpu.make_async_copy(probes, values, ls.at[0]),
        pltpu.make_async_copy(coeffs, held, ls.at[1]),
        pltpu.make_async_copy(jac_ref, jac, ls.at[2]),
    ]
    low, high = [low0, low1], [high0, high1]
    halves = [slice(0, half), slice(half, width)]

    def probe_blocks(start, size, k):
        return values.at[pl.ds(start, size), :, pl.ds(k * half, half)]

    sides = []
    for k in range(2):
        sides.append(
            pltpu.make_async_copy(
                probe_blocks(0, side_blocks, k), low[k].at[pl.ds(REACH, side_blocks)], ls.at[3 + k]
            )
        )
        sides.append(
            pltpu.make_async_copy(
                probe_blocks(total_blocks - side_blocks, side_blocks, k),
                high[k].at[pl.ds(0, side_blocks)],
                ls.at[5 + k],
            )
        )
    for load in loads:
        load.start()
    greet(all_peers(n_obs, n_par, o, p))
    loads[0].wait()
    end = rows - HALO
    edges = []
    for k in range(2):
        start, finish_sides = swap_sides(
            p > 0,
            p < n_par - 1,
            remote(
                probe_blocks(0, REACH, k), high[k].at[pl.ds(side_blocks, REACH)], ph.at[k, 0], ph.at[k, 1], below
            ),
            remote(
                probe_blocks(total_blocks - REACH, REACH, k), low[k].at[pl.ds(0, REACH)],
                ph.at[k, 2], ph.at[k, 3], above,
            ),
        )
        start()
        edges.append(finish_sides)
    for side in sides:
        side.start()

    @pl.when(p == 0)
    def _():
        for ref in low:
            ref[pl.ds(0, REACH)] = jnp.zeros((REACH,) + ref.shape[1:], BF16)
        low2[:, pl.ds(0, REACH)] = jnp.zeros((2, REACH) + ext.shape[2:], BF16)

    @pl.when(p == n_par - 1)
    def _():
        for ref in high:
            ref[pl.ds(side_blocks, REACH)] = jnp.zeros((REACH,) + ref.shape[1:], BF16)
        high2[:, pl.ds(side_blocks, REACH)] = jnp.zeros((2, REACH) + ext.shape[2:], BF16)

    loads[1].wait()

    def inner(b, carry):
        image[pl.ds(pl.multiple_of(b * BLK, BLK), BLK), :] = prior_block(b, 0, values, held, offs)
        return carry

    lax.fori_loop(REACH, total_blocks - REACH, inner, 0, unroll=4)
    loads[2].wait()
    totals = [
        jnp.dot(jac[:, HALO:end], image[HALO:end, columns], preferred_element_type=F32) for columns in halves
    ]
    for side in sides:
        side.wait()
    sums = []
    for k, columns in enumerate(halves):
        edges[k]()
        for b in range(REACH):
            image[pl.ds(b * BLK, BLK), columns] = prior_block(b, -REACH, low[k], held, offs)
        for b in range(total_blocks - REACH, total_blocks):
            image[pl.ds(b * BLK, BLK), columns] = prior_block(
                b, total_blocks - 2 * REACH, high[k], held, offs
            )
        total = totals[k]
        total = total + jnp.dot(jac[:, :HALO], image[:HALO, columns], preferred_element_type=F32)
        total = total + jnp.dot(jac[:, end:], image[end:, columns], preferred_element_type=F32)
        sums.append(sum_over_par(n_par, o, p, total, part.at[k], got.at[k], par.at[k, 0], par.at[k, 1]))
    gathers = []
    for k in range(2):
        fwd[k, p] = sums[k]().astype(BF16)
        mine = fwd.at[k, p]
        copies = []
        for d in range(1, n_par):
            copy = remote(mine, mine, par.at[k, 2, d], par.at[k, 3, d], (o, lax.rem(p + d, n_par)))
            copy.start()
            copies.append(copy)
        gathers.append(copies)

    def reduce_half(k):
        def forward():
            return fwd[k].reshape(jac.shape[0], half)

        return sum_over_obs(
            n_obs, o, p, jac, forward, adj.at[k], adj_got.at[k], rs.at[k, 0], rs.at[k, 1], own.at[k]
        )

    reduce0, reduce1 = reduce_half(0), reduce_half(1)
    for copy in gathers[0]:
        copy.wait()
    reduce0[0]()
    reduce0[1]()
    for copy in gathers[1]:
        copy.wait()
    reduce1[0]()
    reduce0[2]()
    reduce0[3]()
    reduce1[1]()
    reduce1[2]()
    prepare_bands(offs, held, q * blocks, bands, bands_low, bands_high, diagonal)
    reduce1[3]()
    before = lax.rem(order + count - 1, count)
    after = lax.rem(order + 1, count)
    down_device = (owner(n_obs, lax.rem(before, n_obs), before // n_obs), before // n_obs)
    up_device = (owner(n_obs, lax.rem(after, n_obs), after // n_obs), after // n_obs)
    swaps = []

    def prior(k):
        lower[k] = two_products(bands_low, own[k, :HALO, :]).astype(BF16)
        upper[k] = two_products(bands_high, own[k, pl.ds(blocks * BLK - HALO, HALO), :]).astype(BF16)
        start, finish_sides = swap_sides(
            order > 0,
            order < count - 1,
            remote(lower.at[k], from_high.at[k], hs.at[k, 0], hs.at[k, 1], down_device),
            remote(upper.at[k], from_low.at[k], hs.at[k, 2], hs.at[k, 3], up_device),
        )
        start()
        swaps.append(finish_sides)
        sample[:, halves[k]] = two_products(bands, own[k])
        for b in range(blocks):
            here = pl.ds(b * BLK, BLK)
            sample[here, halves[k]] += jnp.dot(diagonal[b], own[k, here, :], preferred_element_type=F32)

    def prior_end(k):
        def low_arrived():
            sample[pl.ds(0, HALO), halves[k]] += from_low[k].astype(F32)

        def high_arrived():
            sample[pl.ds(blocks * BLK - HALO, HALO), halves[k]] += from_high[k].astype(F32)

        swaps[k](low_arrived, high_arrived)
        parts = split(sample[:, halves[k]])
        ext[k, pl.ds(q * blocks, blocks)] = parts[0].reshape(blocks, BLK, half)
        fine[k] = parts[1]

    reduce0[4]()
    prior(0)
    reduce1[4]()
    prior(1)
    prior_end(0)
    stage0, finish0 = gather_over_obs(n_obs, o, p, ext.at[0], ags.at[0, 0], ags.at[0, 1])
    stage1, finish1 = gather_over_obs(n_obs, o, p, ext.at[1], ags.at[1, 0], ags.at[1, 1])
    stage0(0)
    stage0(1)
    coarse = [ext.at[k, pl.ds(q * blocks, blocks)] for k in range(2)]

    def cross(i, j):
        left = coarse[i][...].reshape(fine.shape[1:]), fine[i]
        right = coarse[j][...].reshape(fine.shape[1:]), fine[j]
        both = jnp.concatenate(right, axis=1)
        over_rows = (((0,), (0,)), ((), ()))
        value = lax.dot_general(left[0], both, over_rows, preferred_element_type=F32)
        if i == j:
            other = value[:, half:].T
        else:
            other = lax.dot_general(left[1], right[0], over_rows, preferred_element_type=F32)
        return value[:, :half] + value[:, half:] + other

    first_block = cross(0, 0)
    prior_end(1)
    off_block = cross(1, 0)
    value = jnp.concatenate(
        [
            jnp.concatenate([first_block, off_block.T], axis=1),
            jnp.concatenate([off_block, cross(1, 1)], axis=1),
        ],
        axis=0,
    ) / (sample.shape[0] * count)

    def more0():
        stage0(2)
        stage1(0)

    def more1():
        stage1(1)
        stage1(2)

    matrix = sum_everywhere(n_obs, n_par, o, p, value, *first_sum, [more0, more1])
    last = total_blocks - REACH

    def sample_edges(k):
        return swap_sides(
            p > 0,
            p < n_par - 1,
            remote(
                ext.at[k, pl.ds(0, REACH)], high2.at[k, pl.ds(side_blocks, REACH)],
                hs.at[2 + k, 0], hs.at[2 + k, 1], below,
            ),
            remote(
                ext.at[k, pl.ds(last, REACH)], low2.at[k, pl.ds(0, REACH)], hs.at[2 + k, 2], hs.at[2 + k, 3], above
            ),
        )

    finish0()
    start, finish_sides0 = sample_edges(0)
    start()
    steps, step = inverse_factor_steps(matrix, work, inverse, inverse.shape[1])
    lax.fori_loop(0, 1, step, 0)
    finish1()
    start, finish_sides1 = sample_edges(1)
    start()
    sides = [
        pltpu.make_async_copy(
            ext.at[:, pl.ds(0, side_blocks)], low2.at[:, pl.ds(REACH, side_blocks)], ls.at[3]
        ),
        pltpu.make_async_copy(
            ext.at[:, pl.ds(total_blocks - side_blocks, side_blocks)], high2.at[:, pl.ds(0, side_blocks)],
            ls.at[4],
        ),
    ]
    for side in sides:
        side.start()

    def outer(b, carry):
        image[pl.ds(pl.multiple_of(b * BLK, BLK), BLK), :] = prior_block(b, 0, ext, held, offs)
        return carry

    lax.fori_loop(REACH, last, outer, 0, unroll=4)
    total = jnp.dot(jac[:, HALO:end], image[HALO:end, :], preferred_element_type=F32)
    finish_sides0()
    finish_sides1()
    for side in sides:
        side.wait()
    for b in range(REACH):
        image[pl.ds(b * BLK, BLK), :] = prior_block(b, -REACH, low2, held, offs)
    for b in range(last, total_blocks):
        image[pl.ds(b * BLK, BLK), :] = prior_block(b, total_blocks - 2 * REACH, high2, held, offs)
    total = total + jnp.dot(jac[:, :HALO], image[:HALO, :], preferred_element_type=F32)
    total = total + jnp.dot(jac[:, end:], image[end:, :], preferred_element_type=F32)
    finish_sum = sum_over_par(n_par, o, p, total, part2, got2, par2.at[0], par2.at[1])
    lax.fori_loop(1, steps, step, 0)
    mine = finish_sum()
    factor = split(inverse[...].reshape(width, width))
    mine = split(dot_f32(split(mine), factor, ((1,), (1,))))
    value = dot_f32(mine, mine, ((0,), (0,))) / (jac.shape[0] * n_obs)

    def solve(value):
        last = (((1,), (1,)), ((), ()))
        return (
            lax.dot_general(value, factor[0], last, preferred_element_type=F32)
            + lax.dot_general(value, factor[1], last, preferred_element_type=F32)
        ).astype(BF16)

    tall = min(512, rows)

    def solve_basis():
        def tile(t, carry):
            here = pl.ds(t * (tall // BLK), tall // BLK)
            value = jnp.concatenate([ext[k, here].reshape(tall, half) for k in range(2)], axis=1)
            basis[pl.ds(pl.multiple_of(t * tall, tall), tall), :] = solve(value)
            return carry

        lax.fori_loop(0, rows // tall, tile, 0)
        pltpu.make_async_copy(basis, basis_out, ws.at[0]).start()

    def solve_image():
        def tile(t, carry):
            here = pl.ds(pl.multiple_of(t * tall, tall), tall)
            mapped[here, :] = solve(image[here, :])
            return carry

        lax.fori_loop(0, rows // tall, tile, 0)
        pltpu.make_async_copy(mapped, image_out, ws.at[1]).start()

    add = sum_directly if few_devices(n_obs, n_par, width) else sum_everywhere
    ritz[...] = add(n_obs, n_par, o, p, value, *second_sum, [solve_basis, solve_image])
    pltpu.make_async_copy(basis, basis_out, ws.at[0]).wait()
    pltpu.make_async_copy(mapped, image_out, ws.at[1]).wait()


def write_kernel(*refs):
    count = len(refs) // 2
    copies = [pltpu.make_async_copy(refs[i], refs[count + i], refs[-1].at[i]) for i in range(count)]
    for copy in copies:
        copy.start()
    for copy in copies:
        copy.wait()


def dma(*count):
    return pltpu.SemaphoreType.DMA(count)


def body(n_obs, n_par, jacobian, probes, coeffs, offsets):
    obs, rows = jacobian.shape
    width = probes.shape[1]
    half = width // 2
    own = rows // n_obs
    total_blocks = rows // BLK
    block = 64
    hbm = pl.BlockSpec(memory_space=pltpu.HBM)
    anywhere = pl.BlockSpec(memory_space=pl.ANY)
    piece = obs // n_par
    shapes = [
        jax.ShapeDtypeStruct((rows, width), BF16),
        jax.ShapeDtypeStruct((rows, width), BF16),
        jax.ShapeDtypeStruct((width, width), F32),
    ]
    results = pl.pallas_call(
        functools.partial(main_kernel, n_obs, n_par),
        out_shape=shapes,
        in_specs=[SMEM, hbm, hbm, hbm],
        out_specs=[anywhere, anywhere, VMEM],
        scratch_shapes=[pltpu.VMEM((3 * REACH, BLK, half), BF16)] * 4
        + [
            pltpu.VMEM((total_blocks, BLK, width), BF16),
            pltpu.VMEM(coeffs.shape, BF16),
            pltpu.VMEM((obs, rows), BF16),
            dma(7),
            pltpu.VMEM((rows, width), BF16),
        ]
        + [pltpu.VMEM((2, n_par, piece, half), BF16)] * 3
        + [
            pltpu.VMEM((2, 8, own // 2, half), BF16),
            pltpu.VMEM((2, 6, own // 2, half), BF16),
            pltpu.VMEM((2, own, half), BF16),
            dma(2, 4),
            dma(2, 4, n_par),
            dma(2, 2, 6),
            pltpu.VMEM((2, own, own), BF16),
            pltpu.VMEM((2, HALO, HALO), BF16),
            pltpu.VMEM((2, HALO, HALO), BF16),
            pltpu.VMEM((own // BLK, BLK, BLK), BF16),
            pltpu.VMEM((own, width), F32),
        ]
        + [pltpu.VMEM((2, HALO, half), BF16)] * 4
        + [
            dma(4, 4),
            pltpu.VMEM((2, 3 * REACH, BLK, half), BF16),
            pltpu.VMEM((2, 3 * REACH, BLK, half), BF16),
            pltpu.VMEM((2, own, half), BF16),
            pltpu.VMEM((2, total_blocks, BLK, half), BF16),
            dma(2, 2, 6),
            pltpu.VMEM((width // block, block, 2 * width), F32),
            pltpu.VMEM((width // block, block, width), F32),
        ]
        + [pltpu.VMEM((n_par, piece, width), BF16)] * 2
        + [dma(2, n_par)]
        + [pltpu.VMEM((rows, width), BF16)] * 2
        + [dma(2)]
        + sum_scratch(n_obs, n_par, width, F32)
        + sum_scratch(n_obs, n_par, width, BF16),
        compiler_params=pltpu.CompilerParams(
            collective_id=0, has_side_effects=True, vmem_limit_bytes=LIMIT
        ),
        name="main",
    )(offsets.T, probes.reshape(-1, BLK, width), coeffs, jacobian)
    return pl.pallas_call(
        write_kernel,
        out_shape=shapes,
        in_specs=[anywhere] * 3,
        out_specs=[hbm] * 3,
        scratch_shapes=[dma(3)],
        compiler_params=pltpu.CompilerParams(vmem_limit_bytes=1024 * 1024),
        name="write",
    )(*results)


def solution(mesh):
    return jax.shard_map(
        functools.partial(body, mesh.shape["obs"], mesh.shape["par"]),
        mesh=mesh,
        in_specs=(P("obs", "par"), P("par", None), P("par", None, None, None), P("par", None)),
        out_specs=(P("par", None), P("par", None), P()),
        check_vma=False,
    )
```

```python
import functools

import jax
import jax.numpy as jnp
from jax import lax
from jax.experimental import pallas as pl
from jax.experimental.pallas import tpu as pltpu
from jax.sharding import PartitionSpec as P

BLK = 128
REACH = 4
HALO = REACH * BLK
MESH = pl.DeviceIdType.MESH
F32 = jnp.float32
BF16 = jnp.bfloat16
VMEM = pl.BlockSpec(memory_space=pltpu.VMEM)
SMEM = pl.BlockSpec(memory_space=pltpu.SMEM)
LIMIT = 48 * 1024 * 1024


def greet(devices):
    barrier = pltpu.get_barrier_semaphore()
    for device in devices:
        pl.semaphore_signal(barrier, inc=1, device_id=device, device_id_type=MESH)
    pl.semaphore_wait(barrier, len(devices))


def remote(src, dst, send, recv, device):
    return pltpu.make_async_remote_copy(
        src_ref=src, dst_ref=dst, send_sem=send, recv_sem=recv, device_id=device, device_id_type=MESH
    )


def prior_block(b, base, source, coeffs, offs):
    def pick(offset):
        block = b - base + offset
        if len(source.shape) == 3:
            return source[block]
        return jnp.concatenate([source[0, block], source[1, block]], axis=1)

    left = jnp.concatenate([coeffs[b, 0], coeffs[b, 1], coeffs[b, 2]], axis=1)
    right = jnp.concatenate([pick(0), pick(offs[0, b]), pick(offs[1, b])], axis=0)
    return jnp.dot(left, right, preferred_element_type=F32).astype(BF16)


def split(value):
    upper = value.astype(BF16)
    return upper, (value - upper.astype(F32)).astype(BF16)


def dot_f32(left, right, dims):
    return sum(
        lax.dot_general(left[i], right[j], (dims, ((), ())), preferred_element_type=F32)
        for i, j in ((0, 0), (0, 1), (1, 0))
    )


def all_peers(n_obs, n_par, o, p):
    return [
        (lax.rem(o + i, n_obs), lax.rem(p + j, n_par))
        for j in range(n_par)
        for i in range(n_obs)
        if i or j
    ]


def chip_peers(n_obs, n_par, o, p):
    chips = n_par // 2
    z, core = p // 2, lax.rem(p, 2)
    return [
        (lax.rem(o + i, n_obs), 2 * lax.rem(z + j, chips) + core)
        for j in range(chips)
        for i in range(n_obs)
        if i or j
    ]


def partners(n_obs, o):
    side = o + 1 - 2 * lax.rem(o, 2)
    half = n_obs // 2
    return side, lax.rem(o + half, n_obs), lax.rem(side + half, n_obs)


def quarter(n_obs, o, p):
    y = o // 2
    place = 2 * y + lax.rem(o + y, 2)
    return place + lax.rem(p, 2) * (n_obs - 1 - 2 * place)


def owner(n_obs, q, p):
    place = q + lax.rem(p, 2) * (n_obs - 1 - 2 * q)
    y = place // 2
    return 2 * y + lax.rem(place + y, 2)


def wait_all(ref, sem):
    pltpu.make_async_copy(ref, ref, sem).wait()


def sum_over_par(n_par, o, p, total, part, got, send, recv):
    piece = part.shape[1]
    for q in range(n_par):
        part[q] = total[q * piece : (q + 1) * piece].astype(BF16)
    copies = []
    for d in range(1, n_par):
        q = lax.rem(p + d, n_par)
        copy = remote(part.at[q], got.at[d], send.at[d], recv.at[d], (o, q))
        copy.start()
        copies.append(copy)

    def finish():
        mine = part[p].astype(F32)
        for d in range(1, n_par):
            copies[d - 1].wait()
            mine = mine + got[d].astype(F32)
        return mine

    return finish


def sum_over_obs(n_obs, o, p, jac, forward, adj, got, send, recv, out):
    side, across, far = partners(n_obs, o)
    half = adj.shape[1]
    near = (side, p)
    over = (across, p)
    copies = []

    def product(slot, device, h):
        start = pl.multiple_of((2 * quarter(n_obs, device, p) + h) * half, half)
        value = lax.dot_general(
            jac[:, pl.ds(start, half)], forward(), (((0,), (0,)), ((), ())), preferred_element_type=F32
        )
        adj[slot] = value.astype(BF16)

    def send_slot(slot, device):
        copy = remote(adj.at[slot], got.at[slot], send.at[slot], recv.at[slot], device)
        copy.start()
        copies.append(copy)

    def first():
        product(0, far, 0)
        send_slot(0, near)
        product(1, far, 1)
        send_slot(1, over)

    def second():
        product(2, side, 0)
        send_slot(2, near)
        product(3, across, 1)
        send_slot(3, over)

    def rest():
        product(4, across, 0)
        product(5, side, 1)
        product(6, o, 0)
        product(7, o, 1)

    def third():
        for slot, device in ((0, over), (1, near)):
            copies[slot].wait()
            adj[4 + slot] = (adj[4 + slot].astype(F32) + got[slot].astype(F32)).astype(BF16)
            send_slot(4 + slot, device)

    def finish():
        for h in range(2):
            copies[2 + h].wait()
            copies[4 + h].wait()
            total = adj[6 + h].astype(F32) + got[2 + h].astype(F32) + got[4 + h].astype(F32)
            out[pl.ds(h * half, half), :] = total.astype(BF16)

    return first, second, rest, third, finish


def prepare_bands(offs, coeffs, first, middle, low, high, diagonal):
    blocks = diagonal.shape[0]
    zero = jnp.zeros((BLK, BLK), BF16)
    low[...] = jnp.zeros_like(low)
    high[...] = jnp.zeros_like(high)
    for b in range(blocks):
        diagonal[b] = coeffs[first + b, 0].T
        columns = pl.ds(b * BLK, BLK)
        for j in range(2):
            block = coeffs[first + b, j + 1].T
            offset = offs[j, first + b]
            for c in range(blocks):
                if abs(c - b) > REACH:
                    middle[j, pl.ds(c * BLK, BLK), columns] = zero
            for d in range(-REACH, REACH + 1):
                value = jnp.where(offset == d, block, zero)
                c = b + d
                if c < 0:
                    low[j, pl.ds((c + REACH) * BLK, BLK), columns] = value
                elif c >= blocks:
                    columns_high = pl.ds((b - blocks + REACH) * BLK, BLK)
                    high[j, pl.ds((c - blocks) * BLK, BLK), columns_high] = value
                else:
                    middle[j, pl.ds(c * BLK, BLK), columns] = value


def two_products(bands, values):
    return jnp.dot(bands[0], values, preferred_element_type=F32) + jnp.dot(
        bands[1], values, preferred_element_type=F32
    )


def sum_everywhere(n_obs, n_par, o, p, value, pair_send, pair_got, send, got, out, sems, beside=()):
    beside = list(beside) + [lambda: None] * 2
    core = lax.rem(p, 2)
    other = (o, p + 1 - 2 * core)
    peers = chip_peers(n_obs, n_par, o, p)
    place = (p // 2) * n_obs + o
    count, piece, width = send.shape
    kind = send.dtype
    tall = count * piece
    pair_send[0] = value[:tall].astype(kind)
    pair_send[1] = value[tall:].astype(kind)
    copy = remote(pair_send.at[1 - core], pair_got, sems.at[0], sems.at[1], other)
    copy.start()
    copy.wait()
    mine = pair_send[core].astype(F32) + pair_got[...].astype(F32)
    for j in range(count):
        send[j] = mine[j * piece : (j + 1) * piece].astype(kind)
    for d, device in enumerate(peers, 1):
        target = (device[1] // 2) * n_obs + device[0]
        remote(send.at[target], got.at[d], sems.at[2], sems.at[3], device).start()
    beside[0]()
    mine = send[place].astype(F32)
    rest = got.at[pl.ds(1, count - 1)]
    wait_all(rest, sems.at[2])
    wait_all(rest, sems.at[3])
    for d in range(1, count):
        mine = mine + got[d].astype(F32)
    out[core, place] = mine.astype(kind)
    for device in peers:
        remote(out.at[core, place], out.at[core, place], sems.at[4], sems.at[5], device).start()
    beside[1]()
    wait_all(rest, sems.at[4])
    wait_all(rest, sems.at[5])
    copy = remote(out.at[core], out.at[core], sems.at[6], sems.at[7], other)
    copy.start()
    copy.wait()
    return jnp.concatenate([out[c, j].astype(F32) for c in range(2) for j in range(count)], axis=0)


def sum_directly(n_obs, n_par, o, p, value, send, got, out, sems, beside=()):
    peers = all_peers(n_obs, n_par, o, p)
    place = p * n_obs + o
    count, tall, half = send.shape
    piece = tall // 2
    kind = send.dtype
    for j in range(count):
        rows = value[j * piece : (j + 1) * piece]
        send[j] = jnp.concatenate([rows[:, :half], rows[:, half:]], axis=0).astype(kind)
    for d, (i, q) in enumerate(peers, 1):
        remote(send.at[q * n_obs + i], got.at[d], sems.at[0], sems.at[1], (i, q)).start()
    beside[0]()
    mine = send[place].astype(F32)
    rest = got.at[pl.ds(1, count - 1)]
    wait_all(rest, sems.at[0])
    wait_all(rest, sems.at[1])
    for d in range(1, count):
        mine = mine + got[d].astype(F32)
    out[place] = mine.astype(kind)
    for device in peers:
        remote(out.at[place], out.at[place], sems.at[2], sems.at[3], device).start()
    beside[1]()
    wait_all(rest, sems.at[2])
    wait_all(rest, sems.at[3])
    sums = [out[j].astype(F32) for j in range(count)]
    return jnp.concatenate([jnp.concatenate([rows[:piece], rows[piece:]], axis=1) for rows in sums], axis=0)


def few_devices(n_obs, n_par, width):
    return width // (n_obs * n_par) >= 8


def sum_scratch(n_obs, n_par, width, kind):
    count = n_obs * n_par // 2
    piece = width // 2 // count
    if kind == BF16 and few_devices(n_obs, n_par, width):
        return [pltpu.VMEM((2 * count, 2 * piece, width // 2), kind)] * 3 + [dma(4)]
    return [
        pltpu.VMEM((2, width // 2, width), kind),
        pltpu.VMEM((width // 2, width), kind),
        pltpu.VMEM((count, piece, width), kind),
        pltpu.VMEM((count, piece, width), kind),
        pltpu.VMEM((2, count, piece, width), kind),
        dma(8),
    ]


def small_inverse_factor(matrix):
    size = matrix.shape[0]
    row = lax.broadcasted_iota(jnp.int32, (size, size), 0)
    lane = lax.broadcasted_iota(jnp.int32, (size, size), 1)
    work = jnp.concatenate([matrix, (row == lane).astype(F32)], axis=1)
    group = 8
    parts = [work[g : g + group] for g in range(0, size, group)]
    index = lax.broadcasted_iota(jnp.int32, (group, 2 * size), 0)
    scales = []
    for first in range(size // group):
        start = first * group
        columns = [
            [jnp.broadcast_to(part[:, start + t : start + t + 1], part.shape) for part in parts[first:]]
            for t in range(group)
        ]
        for t in range(group):
            pivot = columns[t][0][t : t + 1]
            scales.append(lax.rsqrt(pivot))
            reciprocal = 1.0 / pivot
            scaled = parts[first][t : t + 1] * reciprocal
            columns[t][0] = jnp.where(index > t, columns[t][0], 0.0)
            for u in range(t + 1, group):
                ratio = columns[u][0][t : t + 1] * reciprocal
                columns[u] = [c - e * ratio for c, e in zip(columns[u], columns[t])]
            for g, column in enumerate(columns[t]):
                parts[first + g] = parts[first + g] - column * scaled
    rows = [parts[j // group][j % group : j % group + 1] * scales[j] for j in range(size)]
    return jnp.concatenate(rows, axis=0)[:, size:]


def inverse_factor_steps(gram, work, out, size):
    blocks = work.shape[0]
    width = blocks * size
    row = lax.broadcasted_iota(jnp.int32, (size, width), 0)
    lane = lax.broadcasted_iota(jnp.int32, (size, width), 1)
    for k in range(blocks):
        work[k, :, pl.ds(0, width)] = gram[k * size : (k + 1) * size]
        work[k, :, pl.ds(width, width)] = (lane == row + k * size).astype(F32)

    def step(k, carry):
        rows = work[k]
        shift = lax.rem(width - k * size, width)
        diagonal = pltpu.roll(rows[:, :width], shift, 1)[:, :size]
        small = small_inverse_factor(diagonal)
        upper = dot_f32(split(small), split(rows), ((1,), (0,)))
        out[k] = upper[:, width:]
        left = jnp.where(lane >= (k + 1) * size, upper[:, :width], 0.0)
        update = dot_f32(split(left), split(upper), ((0,), (0,)))
        for i in range(blocks):
            work[i] -= update[i * size : (i + 1) * size]
        return carry

    return blocks, step


def gather_over_obs(n_obs, o, p, ext, send, recv):
    side, across, _ = partners(n_obs, o)
    near, over = (side, p), (across, p)
    blocks = ext.shape[0] // (2 * n_obs)
    order = [
        [(o, 0, near), (o, 1, over)],
        [(o, 1, near), (o, 0, over)],
        [(side, 0, over), (across, 1, near)],
    ]
    copies = []

    def stage(i):
        for j, (source, h, device) in enumerate(order[i]):
            if i == 2:
                copies[j].wait()
            start = (2 * quarter(n_obs, source, p) + h) * blocks
            ref = ext.at[pl.ds(start, blocks)]
            slot = 2 * i + j
            copy = remote(ref, ref, send.at[slot], recv.at[slot], device)
            copy.start()
            copies.append(copy)

    def finish():
        for copy in copies[2:]:
            copy.wait()

    return stage, finish


def swap_sides(at_start, at_end, low_copy, high_copy):
    def start():
        @pl.when(at_start)
        def _():
            low_copy.start()

        @pl.when(at_end)
        def _():
            high_copy.start()

    def finish(low_arrived=None, high_arrived=None):
        @pl.when(at_start)
        def _():
            low_copy.wait_send()
            high_copy.wait_recv()
            if low_arrived is not None:
                low_arrived()

        @pl.when(at_end)
        def _():
            high_copy.wait_send()
            low_copy.wait_recv()
            if high_arrived is not None:
                high_arrived()

    return start, finish


def main_kernel(
    n_obs, n_par, offs, probes, coeffs, jac_ref, basis_out, image_out, ritz,
    low0, low1, high0, high1, values, held, jac, ls, image, part, got, fwd, adj, adj_got, own, ph, par, rs,
    bands, bands_low, bands_high, diagonal, sample, lower, upper, from_low, from_high, hs,
    low2, high2, fine, ext, ags, work, inverse, part2, got2, par2, basis, mapped, ws, *rest,
):
    o, p = lax.axis_index("obs"), lax.axis_index("par")
    q = quarter(n_obs, o, p)
    count = n_obs * n_par
    order = p * n_obs + q
    rows, width = image.shape
    half = width // 2
    total_blocks = rows // BLK
    blocks = total_blocks // n_obs
    side_blocks = 2 * REACH
    below = (o, lax.rem(p + n_par - 1, n_par))
    above = (o, lax.rem(p + 1, n_par))
    first_sum, second_sum = rest[:6], rest[6:]
    loads = [
        pltpu.make_async_copy(probes, values, ls.at[0]),
        pltpu.make_async_copy(coeffs, held, ls.at[1]),
        pltpu.make_async_copy(jac_ref, jac, ls.at[2]),
    ]
    low, high = [low0, low1], [high0, high1]
    halves = [slice(0, half), slice(half, width)]

    def probe_blocks(start, size, k):
        return values.at[pl.ds(start, size), :, pl.ds(k * half, half)]

    sides = []
    for k in range(2):
        sides.append(
            pltpu.make_async_copy(
                probe_blocks(0, side_blocks, k), low[k].at[pl.ds(REACH, side_blocks)], ls.at[3 + k]
            )
        )
        sides.append(
            pltpu.make_async_copy(
                probe_blocks(total_blocks - side_blocks, side_blocks, k),
                high[k].at[pl.ds(0, side_blocks)],
                ls.at[5 + k],
            )
        )
    for load in loads:
        load.start()
    greet(all_peers(n_obs, n_par, o, p))
    loads[0].wait()
    end = rows - HALO
    edges = []
    for k in range(2):
        start, finish_sides = swap_sides(
            p > 0,
            p < n_par - 1,
            remote(
                probe_blocks(0, REACH, k), high[k].at[pl.ds(side_blocks, REACH)], ph.at[k, 0], ph.at[k, 1], below
            ),
            remote(
                probe_blocks(total_blocks - REACH, REACH, k), low[k].at[pl.ds(0, REACH)],
                ph.at[k, 2], ph.at[k, 3], above,
            ),
        )
        start()
        edges.append(finish_sides)
    for side in sides:
        side.start()

    @pl.when(p == 0)
    def _():
        for ref in low:
            ref[pl.ds(0, REACH)] = jnp.zeros((REACH,) + ref.shape[1:], BF16)
        low2[:, pl.ds(0, REACH)] = jnp.zeros((2, REACH) + ext.shape[2:], BF16)

    @pl.when(p == n_par - 1)
    def _():
        for ref in high:
            ref[pl.ds(side_blocks, REACH)] = jnp.zeros((REACH,) + ref.shape[1:], BF16)
        high2[:, pl.ds(side_blocks, REACH)] = jnp.zeros((2, REACH) + ext.shape[2:], BF16)

    loads[1].wait()

    def inner(b, carry):
        image[pl.ds(pl.multiple_of(b * BLK, BLK), BLK), :] = prior_block(b, 0, values, held, offs)
        return carry

    lax.fori_loop(REACH, total_blocks - REACH, inner, 0, unroll=4)
    loads[2].wait()
    totals = [
        jnp.dot(jac[:, HALO:end], image[HALO:end, columns], preferred_element_type=F32) for columns in halves
    ]
    for side in sides:
        side.wait()
    sums = []
    for k, columns in enumerate(halves):
        edges[k]()
        for b in range(REACH):
            image[pl.ds(b * BLK, BLK), columns] = prior_block(b, -REACH, low[k], held, offs)
        for b in range(total_blocks - REACH, total_blocks):
            image[pl.ds(b * BLK, BLK), columns] = prior_block(
                b, total_blocks - 2 * REACH, high[k], held, offs
            )
        total = totals[k]
        total = total + jnp.dot(jac[:, :HALO], image[:HALO, columns], preferred_element_type=F32)
        total = total + jnp.dot(jac[:, end:], image[end:, columns], preferred_element_type=F32)
        sums.append(sum_over_par(n_par, o, p, total, part.at[k], got.at[k], par.at[k, 0], par.at[k, 1]))
    gathers = []
    for k in range(2):
        fwd[k, p] = sums[k]().astype(BF16)
        mine = fwd.at[k, p]
        copies = []
        for d in range(1, n_par):
            copy = remote(mine, mine, par.at[k, 2, d], par.at[k, 3, d], (o, lax.rem(p + d, n_par)))
            copy.start()
            copies.append(copy)
        gathers.append(copies)

    def reduce_half(k):
        def forward():
            return fwd[k].reshape(jac.shape[0], half)

        return sum_over_obs(
            n_obs, o, p, jac, forward, adj.at[k], adj_got.at[k], rs.at[k, 0], rs.at[k, 1], own.at[k]
        )

    reduce0, reduce1 = reduce_half(0), reduce_half(1)
    for copy in gathers[0]:
        copy.wait()
    reduce0[0]()
    reduce0[1]()
    for copy in gathers[1]:
        copy.wait()
    reduce1[0]()
    reduce0[2]()
    reduce0[3]()
    reduce1[1]()
    reduce1[2]()
    prepare_bands(offs, held, q * blocks, bands, bands_low, bands_high, diagonal)
    reduce1[3]()
    before = lax.rem(order + count - 1, count)
    after = lax.rem(order + 1, count)
    down_device = (owner(n_obs, lax.rem(before, n_obs), before // n_obs), before // n_obs)
    up_device = (owner(n_obs, lax.rem(after, n_obs), after // n_obs), after // n_obs)
    swaps = []

    def prior(k):
        lower[k] = two_products(bands_low, own[k, :HALO, :]).astype(BF16)
        upper[k] = two_products(bands_high, own[k, pl.ds(blocks * BLK - HALO, HALO), :]).astype(BF16)
        start, finish_sides = swap_sides(
            order > 0,
            order < count - 1,
            remote(lower.at[k], from_high.at[k], hs.at[k, 0], hs.at[k, 1], down_device),
            remote(upper.at[k], from_low.at[k], hs.at[k, 2], hs.at[k, 3], up_device),
        )
        start()
        swaps.append(finish_sides)

    def prior_center(k):
        sample[:, halves[k]] = two_products(bands, own[k])
        for b in range(blocks):
            here = pl.ds(b * BLK, BLK)
            sample[here, halves[k]] += jnp.dot(diagonal[b], own[k, here, :], preferred_element_type=F32)

    def prior_end(k):
        def low_arrived():
            sample[pl.ds(0, HALO), halves[k]] += from_low[k].astype(F32)

        def high_arrived():
            sample[pl.ds(blocks * BLK - HALO, HALO), halves[k]] += from_high[k].astype(F32)

        swaps[k](low_arrived, high_arrived)
        parts = split(sample[:, halves[k]])
        ext[k, pl.ds(q * blocks, blocks)] = parts[0].reshape(blocks, BLK, half)
        fine[k] = parts[1]

    reduce0[4]()
    prior(0)
    prior_center(0)
    reduce1[4]()
    prior(1)
    prior_end(0)
    stage0, finish0 = gather_over_obs(n_obs, o, p, ext.at[0], ags.at[0, 0], ags.at[0, 1])
    stage1, finish1 = gather_over_obs(n_obs, o, p, ext.at[1], ags.at[1, 0], ags.at[1, 1])
    stage0(0)
    prior_center(1)
    stage0(1)
    coarse = [ext.at[k, pl.ds(q * blocks, blocks)] for k in range(2)]

    def cross(i, j):
        left = coarse[i][...].reshape(fine.shape[1:]), fine[i]
        right = coarse[j][...].reshape(fine.shape[1:]), fine[j]
        both = jnp.concatenate(right, axis=1)
        over_rows = (((0,), (0,)), ((), ()))
        value = lax.dot_general(left[0], both, over_rows, preferred_element_type=F32)
        if i == j:
            other = value[:, half:].T
        else:
            other = lax.dot_general(left[1], right[0], over_rows, preferred_element_type=F32)
        return value[:, :half] + value[:, half:] + other

    first_block = cross(0, 0)
    prior_end(1)
    off_block = cross(1, 0)
    value = jnp.concatenate(
        [
            jnp.concatenate([first_block, off_block.T], axis=1),
            jnp.concatenate([off_block, cross(1, 1)], axis=1),
        ],
        axis=0,
    ) / (sample.shape[0] * count)

    def more0():
        stage0(2)
        stage1(0)

    def more1():
        stage1(1)
        stage1(2)

    matrix = sum_everywhere(n_obs, n_par, o, p, value, *first_sum, [more0, more1])
    last = total_blocks - REACH

    def sample_edges(k):
        return swap_sides(
            p > 0,
            p < n_par - 1,
            remote(
                ext.at[k, pl.ds(0, REACH)], high2.at[k, pl.ds(side_blocks, REACH)],
                hs.at[2 + k, 0], hs.at[2 + k, 1], below,
            ),
            remote(
                ext.at[k, pl.ds(last, REACH)], low2.at[k, pl.ds(0, REACH)], hs.at[2 + k, 2], hs.at[2 + k, 3], above
            ),
        )

    finish0()
    start, finish_sides0 = sample_edges(0)
    start()
    steps, step = inverse_factor_steps(matrix, work, inverse, inverse.shape[1])
    lax.fori_loop(0, 1, step, 0)
    finish1()
    start, finish_sides1 = sample_edges(1)
    start()
    sides = [
        pltpu.make_async_copy(
            ext.at[:, pl.ds(0, side_blocks)], low2.at[:, pl.ds(REACH, side_blocks)], ls.at[3]
        ),
        pltpu.make_async_copy(
            ext.at[:, pl.ds(total_blocks - side_blocks, side_blocks)], high2.at[:, pl.ds(0, side_blocks)],
            ls.at[4],
        ),
    ]
    for side in sides:
        side.start()

    def outer(b, carry):
        image[pl.ds(pl.multiple_of(b * BLK, BLK), BLK), :] = prior_block(b, 0, ext, held, offs)
        return carry

    lax.fori_loop(REACH, last, outer, 0, unroll=4)
    total = jnp.dot(jac[:, HALO:end], image[HALO:end, :], preferred_element_type=F32)
    finish_sides0()
    finish_sides1()
    for side in sides:
        side.wait()
    for b in range(REACH):
        image[pl.ds(b * BLK, BLK), :] = prior_block(b, -REACH, low2, held, offs)
    for b in range(last, total_blocks):
        image[pl.ds(b * BLK, BLK), :] = prior_block(b, total_blocks - 2 * REACH, high2, held, offs)
    total = total + jnp.dot(jac[:, :HALO], image[:HALO, :], preferred_element_type=F32)
    total = total + jnp.dot(jac[:, end:], image[end:, :], preferred_element_type=F32)
    finish_sum = sum_over_par(n_par, o, p, total, part2, got2, par2.at[0], par2.at[1])
    lax.fori_loop(1, steps, step, 0)
    mine = finish_sum()
    factor = split(inverse[...].reshape(width, width))
    mine = split(dot_f32(split(mine), factor, ((1,), (1,))))
    value = dot_f32(mine, mine, ((0,), (0,))) / (jac.shape[0] * n_obs)

    def solve(value):
        last = (((1,), (1,)), ((), ()))
        return (
            lax.dot_general(value, factor[0], last, preferred_element_type=F32)
            + lax.dot_general(value, factor[1], last, preferred_element_type=F32)
        ).astype(BF16)

    tall = min(512, rows)

    def solve_basis():
        def tile(t, carry):
            here = pl.ds(t * (tall // BLK), tall // BLK)
            value = jnp.concatenate([ext[k, here].reshape(tall, half) for k in range(2)], axis=1)
            basis[pl.ds(pl.multiple_of(t * tall, tall), tall), :] = solve(value)
            return carry

        lax.fori_loop(0, rows // tall, tile, 0)
        pltpu.make_async_copy(basis, basis_out, ws.at[0]).start()

    def solve_image():
        def tile(t, carry):
            here = pl.ds(pl.multiple_of(t * tall, tall), tall)
            mapped[here, :] = solve(image[here, :])
            return carry

        lax.fori_loop(0, rows // tall, tile, 0)
        pltpu.make_async_copy(mapped, image_out, ws.at[1]).start()

    add = sum_directly if few_devices(n_obs, n_par, width) else sum_everywhere
    ritz[...] = add(n_obs, n_par, o, p, value, *second_sum, [solve_basis, solve_image])
    pltpu.make_async_copy(basis, basis_out, ws.at[0]).wait()
    pltpu.make_async_copy(mapped, image_out, ws.at[1]).wait()


def write_kernel(*refs):
    count = len(refs) // 2
    copies = [pltpu.make_async_copy(refs[i], refs[count + i], refs[-1].at[i]) for i in range(count)]
    for copy in copies:
        copy.start()
    for copy in copies:
        copy.wait()


def dma(*count):
    return pltpu.SemaphoreType.DMA(count)


def body(n_obs, n_par, jacobian, probes, coeffs, offsets):
    obs, rows = jacobian.shape
    width = probes.shape[1]
    half = width // 2
    own = rows // n_obs
    total_blocks = rows // BLK
    block = 64
    hbm = pl.BlockSpec(memory_space=pltpu.HBM)
    anywhere = pl.BlockSpec(memory_space=pl.ANY)
    piece = obs // n_par
    shapes = [
        jax.ShapeDtypeStruct((rows, width), BF16),
        jax.ShapeDtypeStruct((rows, width), BF16),
        jax.ShapeDtypeStruct((width, width), F32),
    ]
    results = pl.pallas_call(
        functools.partial(main_kernel, n_obs, n_par),
        out_shape=shapes,
        in_specs=[SMEM, hbm, hbm, hbm],
        out_specs=[anywhere, anywhere, VMEM],
        scratch_shapes=[pltpu.VMEM((3 * REACH, BLK, half), BF16)] * 4
        + [
            pltpu.VMEM((total_blocks, BLK, width), BF16),
            pltpu.VMEM(coeffs.shape, BF16),
            pltpu.VMEM((obs, rows), BF16),
            dma(7),
            pltpu.VMEM((rows, width), BF16),
        ]
        + [pltpu.VMEM((2, n_par, piece, half), BF16)] * 3
        + [
            pltpu.VMEM((2, 8, own // 2, half), BF16),
            pltpu.VMEM((2, 6, own // 2, half), BF16),
            pltpu.VMEM((2, own, half), BF16),
            dma(2, 4),
            dma(2, 4, n_par),
            dma(2, 2, 6),
            pltpu.VMEM((2, own, own), BF16),
            pltpu.VMEM((2, HALO, HALO), BF16),
            pltpu.VMEM((2, HALO, HALO), BF16),
            pltpu.VMEM((own // BLK, BLK, BLK), BF16),
            pltpu.VMEM((own, width), F32),
        ]
        + [pltpu.VMEM((2, HALO, half), BF16)] * 4
        + [
            dma(4, 4),
            pltpu.VMEM((2, 3 * REACH, BLK, half), BF16),
            pltpu.VMEM((2, 3 * REACH, BLK, half), BF16),
            pltpu.VMEM((2, own, half), BF16),
            pltpu.VMEM((2, total_blocks, BLK, half), BF16),
            dma(2, 2, 6),
            pltpu.VMEM((width // block, block, 2 * width), F32),
            pltpu.VMEM((width // block, block, width), F32),
        ]
        + [pltpu.VMEM((n_par, piece, width), BF16)] * 2
        + [dma(2, n_par)]
        + [pltpu.VMEM((rows, width), BF16)] * 2
        + [dma(2)]
        + sum_scratch(n_obs, n_par, width, F32)
        + sum_scratch(n_obs, n_par, width, BF16),
        compiler_params=pltpu.CompilerParams(
            collective_id=0, has_side_effects=True, vmem_limit_bytes=LIMIT
        ),
        name="main",
    )(offsets.T, probes.reshape(-1, BLK, width), coeffs, jacobian)
    return pl.pallas_call(
        write_kernel,
        out_shape=shapes,
        in_specs=[anywhere] * 3,
        out_specs=[hbm] * 3,
        scratch_shapes=[dma(3)],
        compiler_params=pltpu.CompilerParams(vmem_limit_bytes=1024 * 1024),
        name="write",
    )(*results)


def solution(mesh):
    return jax.shard_map(
        functools.partial(body, mesh.shape["obs"], mesh.shape["par"]),
        mesh=mesh,
        in_specs=(P("obs", "par"), P("par", None), P("par", None, None, None), P("par", None)),
        out_specs=(P("par", None), P("par", None), P()),
        check_vma=False,
    )
```
